512 devices in a mesh: sub: 32 (over y, x, core), node: 16 (over z).
Axes of the slice: x: 4, y: 4, z: 16, core: 2. Of those that a mesh axis runs over, the one named last changes fastest.
Arguments:
- node_tensor: bfloat16 [32, 16, 128, 128, 128], P('sub', 'node'), may hold values from -0.046875 to 0.046875
- outer_env: bfloat16 [32, 16, 2, 1, 128, 128], P('sub', 'node'), may hold values from -6 to 6
- upper_env: bfloat16 [32, 16, 1, 128, 128], P('sub', 'node'), may hold values from -6 to 6
- role_map: int32 [32, 16], P('sub'), may hold values from 0 to 15, each once within a row
- child_slots: int32 [32, 16], P('sub'), may hold values from -1 to 3, as said below
Outputs:
- mean_field: bfloat16 [32, 16, 1, 128, 128], P('sub', 'node')
The draws below stay inside these ranges and needn't reach their ends.
Inputs may be any that keep to these rules, and one draw needn't show every extreme that they name: `role_map`: each group's row is a permutation of the roles 0 to 15. `child_slots`: each group's row names every lower node 0 to 3 exactly once; all other entries are -1.
All inputs are finite; a program needn't handle non-finite values.
Results may differ from the reference program's by a relative error of at most 0.012.
Values may be sent and summed in bfloat16 or wider, within the bound.
A program may use at most 64 MiB of HBM per device.

```python
import jax
import jax.numpy as jnp
from jax import lax

B = 128
TERMS = 1
GROUPS = 32
SLOTS = 16
MIDS = 8
LEAVES = 4


def draw_child_slots(key, part):
    group_keys = jax.random.split(key, GROUPS)
    orders = jax.vmap(lambda k: jax.random.permutation(k, 2 * MIDS))(group_keys)
    return jnp.where(orders < LEAVES, orders, -1).astype(jnp.int32)


def block_levels(rng, dims, pieces, least, largest):
    gain, own = 1.0, jax.random.fold_in(rng, 6)
    for axis_at, shards_of in pieces:
        heights = jnp.exp(jax.random.uniform(jax.random.fold_in(own, axis_at), (shards_of,), jnp.float32, least / len(pieces), largest / len(pieces)))
        gain = gain * jnp.repeat(heights, dims[axis_at] // shards_of).reshape([-1 if axis == axis_at else 1 for axis in range(len(dims))])
    return gain


def bell_draw(own_key, dims, width, bound, pieces=(), kind=jnp.bfloat16):
    result = jax.random.normal(own_key, dims, jnp.float32) * width
    if len(pieces) > 0:
        result = block_levels(own_key, dims, pieces, -0.22, 0.18) * result
    return jnp.clip(result, min=-bound, max=bound).astype(kind)


def setup_inputs(seed: int = 0) -> dict:
    streams_of = jax.random.split(jax.random.key(seed), 6)
    node_tensor = bell_draw(streams_of[0], (GROUPS, SLOTS, B, B, B), (B * B) ** -0.5, 0.046875, ((0, 32), (1, 16)))
    outer_env = bell_draw(streams_of[1], (GROUPS, SLOTS, 2, TERMS, B, B), 1.0, 6.0, ((0, 32), (1, 16)))
    upper_env = bell_draw(streams_of[2], (GROUPS, SLOTS, TERMS, B, B), 1.0, 6.0, ((0, 32), (1, 16)))
    role_map = jax.vmap(lambda own: jax.random.permutation(own, SLOTS))(jax.random.split(streams_of[3], GROUPS)).reshape((GROUPS, SLOTS)).astype(jnp.int32)
    child_slots = draw_child_slots(jax.random.fold_in(streams_of[5], 71), 0)
    return {"node_tensor": node_tensor, "outer_env": outer_env, "upper_env": upper_env, "role_map": role_map, "child_slots": child_slots}


def node_up(tensor_here, left_env, right_env):
    wide = tensor_here.astype(jnp.float32)
    first = jnp.einsum("xa,abp->xbp", left_env.astype(jnp.float32), wide).astype(jnp.bfloat16)
    second = jnp.einsum("yb,xbp->xyp", right_env.astype(jnp.float32), first.astype(jnp.float32)).astype(jnp.bfloat16)
    return jnp.einsum("xyq,xyp->qp", wide, second.astype(jnp.float32)).astype(jnp.bfloat16)


def node_down(tensor_here, left_env, right_env, upper_here):
    wide = tensor_here.astype(jnp.float32)
    weighted = jnp.einsum("qp,abp->abq", upper_here.astype(jnp.float32), wide).astype(jnp.bfloat16)
    right_part = jnp.einsum("xyq,yb->xbq", wide, right_env.astype(jnp.float32)).astype(jnp.bfloat16)
    left_part = jnp.einsum("xyq,xa->ayq", wide, left_env.astype(jnp.float32)).astype(jnp.bfloat16)
    first_child = jnp.einsum("xbq,abq->xa", right_part.astype(jnp.float32), weighted.astype(jnp.float32)).astype(jnp.bfloat16)
    second_child = jnp.einsum("ayq,abq->yb", left_part.astype(jnp.float32), weighted.astype(jnp.float32)).astype(jnp.bfloat16)
    return first_child, second_child


def reference(node_tensor, outer_env, upper_env, role_map, child_slots):
    group_count, group_size = role_map.shape
    top_count = group_size // 4
    mid_count = 2 * top_count
    leaf_count = group_size - top_count - mid_count
    term_count = outer_env.shape[3]
    bond_size = node_tensor.shape[2]
    spots = jnp.arange(group_size, dtype=jnp.int32)
    role_spot = jnp.sum(jnp.where(role_map[:, None, :] == spots[None, :, None], spots[None, None, :], 0), axis=2).astype(jnp.int32)

    def leaf_group(group):
        def per_leaf(index):
            position = role_spot[group, top_count + mid_count + index]
            tensor_here = node_tensor[group, position]
            child_envs = outer_env[group, position]
            return jnp.stack([node_up(tensor_here, child_envs[0, t], child_envs[1, t]) for t in range(term_count)])
        return lax.map(per_leaf, jnp.arange(leaf_count, dtype=jnp.int32))

    leaf_envs = lax.map(leaf_group, jnp.arange(group_count, dtype=jnp.int32))

    def mid_group(group):
        def per_mid(index):
            position = role_spot[group, top_count + index]
            tensor_here = node_tensor[group, position]
            child_envs = []
            for branch in range(2):
                slot_link = child_slots[group, 2 * index + branch]
                leaf_pick = leaf_envs[group, jnp.maximum(slot_link, 0)]
                child_envs.append(jnp.where(slot_link >= 0, leaf_pick, outer_env[group, position, branch]))
            return jnp.stack([node_up(tensor_here, child_envs[0][t], child_envs[1][t]) for t in range(term_count)])
        return lax.map(per_mid, jnp.arange(mid_count, dtype=jnp.int32))

    mid_envs = lax.map(mid_group, jnp.arange(group_count, dtype=jnp.int32))
    next_mids = jnp.roll(mid_envs, -1, axis=0)

    def top_group(group):
        def per_top(index):
            position = role_spot[group, index]
            tensor_here = node_tensor[group, position]
            upper_here = upper_env[group, position]
            left_env = mid_envs[group, index]
            right_env = next_mids[group, top_count + index]
            results = [node_down(tensor_here, left_env[t], right_env[t], upper_here[t]) for t in range(term_count)]
            return jnp.stack([r[0] for r in results]), jnp.stack([r[1] for r in results])
        return lax.map(per_top, jnp.arange(top_count, dtype=jnp.int32))

    first_fields, second_fields = lax.map(top_group, jnp.arange(group_count, dtype=jnp.int32))
    mid_fields = jnp.concatenate([first_fields, jnp.roll(second_fields, 1, axis=0)], axis=1)
    zero_envs = jnp.zeros((group_count, top_count, term_count, bond_size, bond_size), jnp.bfloat16)
    by_role = jnp.concatenate([zero_envs, mid_fields, leaf_envs], axis=1)
    return jnp.take_along_axis(by_role, role_map[:, :, None, None, None], axis=1)
```

```python
import functools

import jax
import jax.numpy as jnp
from jax import lax
from jax.experimental import pallas as pl
from jax.experimental.pallas import tpu as pltpu
from jax.sharding import PartitionSpec as P

TERMS = 1
MESH = pl.DeviceIdType.MESH


def from_behind(block, axis, distance):
    devices = range(lax.axis_size(axis))
    route = [((i - distance) % len(devices), i) for i in devices]
    return lax.ppermute(block, axis, route)


def gather_kernel(n, x_ref, out_ref, send_sem, recv_sem, own_sem):
    me = lax.axis_index("node")
    group = lax.axis_index("sub")
    barrier = pltpu.get_barrier_semaphore()
    for d in range(1, n):
        pl.semaphore_signal(barrier, inc=1, device_id=(group, lax.rem(me + d, n)), device_id_type=MESH)
    pl.semaphore_wait(barrier, n - 1)
    own = pltpu.make_async_copy(x_ref, out_ref.at[me], own_sem)
    own.start()
    copies = []
    for d in range(1, n):
        copy = pltpu.make_async_remote_copy(
            src_ref=x_ref,
            dst_ref=out_ref.at[me],
            send_sem=send_sem.at[d - 1],
            recv_sem=recv_sem.at[d - 1],
            device_id=(group, lax.rem(me + d, n)),
            device_id_type=MESH,
        )
        copy.start()
        copies.append(copy)
    for copy in copies:
        copy.wait_send()
    for d in range(1, n):
        pltpu.make_async_remote_copy(
            src_ref=x_ref,
            dst_ref=out_ref.at[lax.rem(me + n - d, n)],
            send_sem=send_sem.at[d - 1],
            recv_sem=recv_sem.at[d - 1],
            device_id=(group, lax.rem(me + n - d, n)),
            device_id_type=MESH,
        ).wait_recv()
    own.wait()


def node_gather(block, collective_id):
    n = lax.axis_size("node")
    return pl.pallas_call(
        functools.partial(gather_kernel, n),
        out_shape=jax.ShapeDtypeStruct((n,) + block.shape, block.dtype),
        in_specs=[pl.BlockSpec(memory_space=pl.ANY)],
        out_specs=pl.BlockSpec(memory_space=pl.ANY),
        scratch_shapes=[
            pltpu.SemaphoreType.DMA((n - 1,)),
            pltpu.SemaphoreType.DMA((n - 1,)),
            pltpu.SemaphoreType.DMA,
        ],
        compiler_params=pltpu.CompilerParams(collective_id=collective_id, has_side_effects=True),
    )(block)


def node_up(tensor_here, left_env, right_env):
    first = jnp.einsum(
        "xa,abp->xbp", left_env, tensor_here, preferred_element_type=jnp.float32
    ).astype(jnp.bfloat16)
    second = jnp.einsum("yb,xbp->xyp", right_env, first, preferred_element_type=jnp.float32).astype(
        jnp.bfloat16
    )
    return jnp.einsum(
        "xyq,xyp->qp", tensor_here, second, preferred_element_type=jnp.float32
    ).astype(jnp.bfloat16)


def node_down(tensor_here, left_env, right_env, upper_here):
    weighted = jnp.einsum(
        "qp,abp->abq", upper_here, tensor_here, preferred_element_type=jnp.float32
    ).astype(jnp.bfloat16)
    right_part = jnp.einsum(
        "xyq,yb->xbq", tensor_here, right_env, preferred_element_type=jnp.float32
    ).astype(jnp.bfloat16)
    left_part = jnp.einsum(
        "xyq,xa->ayq", tensor_here, left_env, preferred_element_type=jnp.float32
    ).astype(jnp.bfloat16)
    first_child = jnp.einsum(
        "xbq,abq->xa", right_part, weighted, preferred_element_type=jnp.float32
    ).astype(jnp.bfloat16)
    second_child = jnp.einsum(
        "ayq,abq->yb", left_part, weighted, preferred_element_type=jnp.float32
    ).astype(jnp.bfloat16)
    return (first_child, second_child)


def placements(group_roles):
    group_size = group_roles.shape[0]
    spots = jnp.arange(group_size, dtype=jnp.int32)
    return jnp.sum(jnp.where(group_roles[None, :] == spots[:, None], spots[None, :], 0), axis=1)


def local(node_tensor, outer_env, upper_env, role_map, child_slots):
    tensor_here = node_tensor[0, 0]
    outer_envs = outer_env[0, 0]
    upper_envs = upper_env[0, 0]
    group_roles = role_map[0]
    child_links = child_slots[0]
    group_size = lax.axis_size("node")
    top_count = group_size // 4
    mid_count = 2 * top_count
    bond_size = tensor_here.shape[0]
    role_spot = placements(group_roles)
    position = lax.axis_index("node")
    my_role = group_roles[position]
    is_top = my_role < top_count
    is_mid = jnp.logical_and(my_role >= top_count, my_role < top_count + mid_count)
    is_leaf = my_role >= top_count + mid_count
    zero_envs = jnp.zeros((TERMS, bond_size, bond_size), jnp.bfloat16)

    def leaf_work():
        return jnp.stack([node_up(tensor_here, outer_envs[0, 0], outer_envs[1, 0])])

    leaf_up = lax.cond(is_leaf, leaf_work, lambda: zero_envs)
    leaf_spots = role_spot[top_count + mid_count :]
    every_leaf = node_gather(leaf_up, 0)
    leaf_table = jnp.take(every_leaf, leaf_spots, axis=0)
    mid_index = jnp.clip(my_role - top_count, 0, mid_count - 1)

    def mid_work():
        child_envs = []
        for branch in range(2):
            slot_link = child_links[2 * mid_index + branch]
            leaf_pick = leaf_table[jnp.maximum(slot_link, 0)]
            child_envs.append(jnp.where(slot_link >= 0, leaf_pick, outer_envs[branch]))
        return jnp.stack([node_up(tensor_here, child_envs[0][0], child_envs[1][0])])

    mid_up = lax.cond(is_mid, mid_work, lambda: zero_envs)
    mid_spots = role_spot[top_count : top_count + mid_count]
    every_mid = node_gather(mid_up, 1)
    mid_table = jnp.take(every_mid, mid_spots, axis=0)
    top_index = jnp.clip(my_role, 0, top_count - 1)
    next_half = from_behind(mid_table[top_count:], "sub", -1)
    right_envs = next_half[top_index]

    def top_work():
        left_env = mid_table[top_index]
        results = [node_down(tensor_here, left_env[0], right_envs[0], upper_envs[0])]
        return jnp.stack([jnp.stack([r[0] for r in results]), jnp.stack([r[1] for r in results])])

    top_down = lax.cond(
        is_top, top_work, lambda: jnp.zeros((2, TERMS, bond_size, bond_size), jnp.bfloat16)
    )
    top_spots = role_spot[:top_count]
    every_top = node_gather(top_down, 2)
    top_table = jnp.take(every_top, top_spots, axis=0)
    own_field = top_table[jnp.clip(mid_index, 0, top_count - 1), 0]
    from_before = from_behind(top_table[:, 1], "sub", 1)
    other_field = from_before[jnp.clip(mid_index - top_count, 0, top_count - 1)]
    mid_field = jnp.where(mid_index < top_count, own_field, other_field)
    result = jnp.where(is_mid, mid_field, jnp.where(is_leaf, leaf_up, zero_envs))
    return result[None, None]


def solution(mesh):
    return jax.shard_map(
        local,
        mesh=mesh,
        in_specs=(
            P("sub", "node", None, None, None),
            P("sub", "node", None, None, None, None),
            P("sub", "node", None, None, None),
            P("sub", None),
            P("sub", None),
        ),
        out_specs=P("sub", "node", None, None, None),
        check_vma=False,
    )
```

```python
import functools

import jax
import jax.numpy as jnp
from jax import lax
from jax.experimental import pallas as pl
from jax.experimental.pallas import tpu as pltpu
from jax.sharding import PartitionSpec as P

TERMS = 1
MESH = pl.DeviceIdType.MESH


def from_behind(block, axis, distance):
    devices = range(lax.axis_size(axis))
    route = [((i - distance) % len(devices), i) for i in devices]
    return lax.ppermute(block, axis, route)


def gather_kernel(n, x_ref, out_ref, send_sem, recv_sem, own_sem):
    me = lax.axis_index("node")
    group = lax.axis_index("sub")
    right = lax.rem(me + 1, n)
    left = lax.rem(me + n - 1, n)
    barrier = pltpu.get_barrier_semaphore()
    for neighbour in (left, right):
        pl.semaphore_signal(barrier, inc=1, device_id=(group, neighbour), device_id_type=MESH)
    pl.semaphore_wait(barrier, 2)
    own = pltpu.make_async_copy(x_ref, out_ref.at[me], own_sem)
    own.start()
    ways = ((0, 1, right, n // 2), (1, -1, left, n - 1 - n // 2))

    def hop(way, sign, target, step, origin):
        return pltpu.make_async_remote_copy(
            src_ref=x_ref if step == 0 else out_ref.at[origin],
            dst_ref=out_ref.at[origin],
            send_sem=send_sem.at[way, step],
            recv_sem=recv_sem.at[way, step],
            device_id=(group, target),
            device_id_type=MESH,
        )

    sent = []
    for step in range(n // 2):
        for way, sign, target, steps in ways:
            if step >= steps:
                continue
            origin = lax.rem(me - sign * step + 2 * n, n)
            if step > 0:
                hop(way, sign, target, step - 1, origin).wait_recv()
            copy = hop(way, sign, target, step, origin)
            copy.start()
            sent.append(copy)
    for way, sign, target, steps in ways:
        origin = lax.rem(me - sign * steps + 2 * n, n)
        hop(way, sign, target, steps - 1, origin).wait_recv()
    for copy in sent:
        copy.wait_send()
    own.wait()


def node_gather(block, collective_id):
    n = lax.axis_size("node")
    return pl.pallas_call(
        functools.partial(gather_kernel, n),
        out_shape=jax.ShapeDtypeStruct((n,) + block.shape, block.dtype),
        in_specs=[pl.BlockSpec(memory_space=pl.ANY)],
        out_specs=pl.BlockSpec(memory_space=pl.ANY),
        scratch_shapes=[
            pltpu.SemaphoreType.DMA((2, n // 2)),
            pltpu.SemaphoreType.DMA((2, n // 2)),
            pltpu.SemaphoreType.DMA,
        ],
        compiler_params=pltpu.CompilerParams(collective_id=collective_id, has_side_effects=True),
    )(block)


def node_up(tensor_here, left_env, right_env):
    first = jnp.einsum(
        "xa,abp->xbp", left_env, tensor_here, preferred_element_type=jnp.float32
    ).astype(jnp.bfloat16)
    second = jnp.einsum("yb,xbp->xyp", right_env, first, preferred_element_type=jnp.float32).astype(
        jnp.bfloat16
    )
    return jnp.einsum(
        "xyq,xyp->qp", tensor_here, second, preferred_element_type=jnp.float32
    ).astype(jnp.bfloat16)


def node_down(tensor_here, left_env, right_env, upper_here):
    weighted = jnp.einsum(
        "qp,abp->abq", upper_here, tensor_here, preferred_element_type=jnp.float32
    ).astype(jnp.bfloat16)
    right_part = jnp.einsum(
        "xyq,yb->xbq", tensor_here, right_env, preferred_element_type=jnp.float32
    ).astype(jnp.bfloat16)
    left_part = jnp.einsum(
        "xyq,xa->ayq", tensor_here, left_env, preferred_element_type=jnp.float32
    ).astype(jnp.bfloat16)
    first_child = jnp.einsum(
        "xbq,abq->xa", right_part, weighted, preferred_element_type=jnp.float32
    ).astype(jnp.bfloat16)
    second_child = jnp.einsum(
        "ayq,abq->yb", left_part, weighted, preferred_element_type=jnp.float32
    ).astype(jnp.bfloat16)
    return (first_child, second_child)


def placements(group_roles):
    group_size = group_roles.shape[0]
    spots = jnp.arange(group_size, dtype=jnp.int32)
    return jnp.sum(jnp.where(group_roles[None, :] == spots[:, None], spots[None, :], 0), axis=1)


def local(node_tensor, outer_env, upper_env, role_map, child_slots):
    tensor_here = node_tensor[0, 0]
    outer_envs = outer_env[0, 0]
    upper_envs = upper_env[0, 0]
    group_roles = role_map[0]
    child_links = child_slots[0]
    group_size = lax.axis_size("node")
    top_count = group_size // 4
    mid_count = 2 * top_count
    bond_size = tensor_here.shape[0]
    role_spot = placements(group_roles)
    position = lax.axis_index("node")
    my_role = group_roles[position]
    is_top = my_role < top_count
    is_mid = jnp.logical_and(my_role >= top_count, my_role < top_count + mid_count)
    is_leaf = my_role >= top_count + mid_count
    zero_envs = jnp.zeros((TERMS, bond_size, bond_size), jnp.bfloat16)

    def leaf_work():
        return jnp.stack([node_up(tensor_here, outer_envs[0, 0], outer_envs[1, 0])])

    leaf_up = lax.cond(is_leaf, leaf_work, lambda: zero_envs)
    leaf_spots = role_spot[top_count + mid_count :]
    every_leaf = node_gather(leaf_up, 0)
    leaf_table = jnp.take(every_leaf, leaf_spots, axis=0)
    mid_index = jnp.clip(my_role - top_count, 0, mid_count - 1)

    def mid_work():
        child_envs = []
        for branch in range(2):
            slot_link = child_links[2 * mid_index + branch]
            leaf_pick = leaf_table[jnp.maximum(slot_link, 0)]
            child_envs.append(jnp.where(slot_link >= 0, leaf_pick, outer_envs[branch]))
        return jnp.stack([node_up(tensor_here, child_envs[0][0], child_envs[1][0])])

    mid_up = lax.cond(is_mid, mid_work, lambda: zero_envs)
    mid_spots = role_spot[top_count : top_count + mid_count]
    every_mid = node_gather(mid_up, 1)
    mid_table = jnp.take(every_mid, mid_spots, axis=0)
    top_index = jnp.clip(my_role, 0, top_count - 1)
    next_half = from_behind(mid_table[top_count:], "sub", -1)
    right_envs = next_half[top_index]

    def top_work():
        left_env = mid_table[top_index]
        results = [node_down(tensor_here, left_env[0], right_envs[0], upper_envs[0])]
        return jnp.stack([jnp.stack([r[0] for r in results]), jnp.stack([r[1] for r in results])])

    top_down = lax.cond(
        is_top, top_work, lambda: jnp.zeros((2, TERMS, bond_size, bond_size), jnp.bfloat16)
    )
    top_spots = role_spot[:top_count]
    every_top = node_gather(top_down, 2)
    top_table = jnp.take(every_top, top_spots, axis=0)
    own_field = top_table[jnp.clip(mid_index, 0, top_count - 1), 0]
    from_before = from_behind(top_table[:, 1], "sub", 1)
    other_field = from_before[jnp.clip(mid_index - top_count, 0, top_count - 1)]
    mid_field = jnp.where(mid_index < top_count, own_field, other_field)
    result = jnp.where(is_mid, mid_field, jnp.where(is_leaf, leaf_up, zero_envs))
    return result[None, None]


def solution(mesh):
    return jax.shard_map(
        local,
        mesh=mesh,
        in_specs=(
            P("sub", "node", None, None, None),
            P("sub", "node", None, None, None, None),
            P("sub", "node", None, None, None),
            P("sub", None),
            P("sub", None),
        ),
        out_specs=P("sub", "node", None, None, None),
        check_vma=False,
    )
```

```python
import functools

import jax
import jax.numpy as jnp
from jax import lax
from jax.experimental import pallas as pl
from jax.experimental.pallas import tpu as pltpu
from jax.sharding import PartitionSpec as P

TERMS = 1
MESH = pl.DeviceIdType.MESH


def from_behind(block, axis, distance):
    devices = range(lax.axis_size(axis))
    route = [((i - distance) % len(devices), i) for i in devices]
    return lax.ppermute(block, axis, route)


def gather_kernel(n, x_ref, out_ref, send_sem, recv_sem, own_sem):
    me = lax.axis_index("node")
    group = lax.axis_index("sub")
    right = lax.rem(me + 1, n)
    left = lax.rem(me + n - 1, n)
    barrier = pltpu.get_barrier_semaphore()
    for neighbour in (left, right):
        pl.semaphore_signal(barrier, inc=1, device_id=(group, neighbour), device_id_type=MESH)
    pl.semaphore_wait(barrier, 2)
    own = pltpu.make_async_copy(x_ref, out_ref.at[me], own_sem)
    own.start()
    ways = ((0, 1, right, n // 2), (1, -1, left, n - 1 - n // 2))

    def hop(way, sign, target, step, origin):
        return pltpu.make_async_remote_copy(
            src_ref=x_ref if step == 0 else out_ref.at[origin],
            dst_ref=out_ref.at[origin],
            send_sem=send_sem.at[way, step],
            recv_sem=recv_sem.at[way, step],
            device_id=(group, target),
            device_id_type=MESH,
        )

    sent = []
    for step in range(n // 2):
        for way, sign, target, steps in ways:
            if step >= steps:
                continue
            origin = lax.rem(me - sign * step + 2 * n, n)
            if step > 0:
                hop(way, sign, target, step - 1, origin).wait_recv()
            copy = hop(way, sign, target, step, origin)
            copy.start()
            sent.append(copy)
    for way, sign, target, steps in ways:
        origin = lax.rem(me - sign * steps + 2 * n, n)
        hop(way, sign, target, steps - 1, origin).wait_recv()
    for copy in sent:
        copy.wait_send()
    own.wait()


def node_gather(block, collective_id):
    n = lax.axis_size("node")
    return pl.pallas_call(
        functools.partial(gather_kernel, n),
        out_shape=jax.ShapeDtypeStruct((n,) + block.shape, block.dtype),
        in_specs=[pl.BlockSpec(memory_space=pltpu.VMEM)],
        out_specs=pl.BlockSpec(memory_space=pltpu.VMEM),
        scratch_shapes=[
            pltpu.SemaphoreType.DMA((2, n // 2)),
            pltpu.SemaphoreType.DMA((2, n // 2)),
            pltpu.SemaphoreType.DMA,
        ],
        compiler_params=pltpu.CompilerParams(collective_id=collective_id, has_side_effects=True),
    )(block)


def node_up(tensor_here, left_env, right_env):
    first = jnp.einsum(
        "xa,abp->xbp", left_env, tensor_here, preferred_element_type=jnp.float32
    ).astype(jnp.bfloat16)
    second = jnp.einsum("yb,xbp->xyp", right_env, first, preferred_element_type=jnp.float32).astype(
        jnp.bfloat16
    )
    return jnp.einsum(
        "xyq,xyp->qp", tensor_here, second, preferred_element_type=jnp.float32
    ).astype(jnp.bfloat16)


def node_down(tensor_here, left_env, right_env, upper_here):
    weighted = jnp.einsum(
        "qp,abp->abq", upper_here, tensor_here, preferred_element_type=jnp.float32
    ).astype(jnp.bfloat16)
    right_part = jnp.einsum(
        "xyq,yb->xbq", tensor_here, right_env, preferred_element_type=jnp.float32
    ).astype(jnp.bfloat16)
    left_part = jnp.einsum(
        "xyq,xa->ayq", tensor_here, left_env, preferred_element_type=jnp.float32
    ).astype(jnp.bfloat16)
    first_child = jnp.einsum(
        "xbq,abq->xa", right_part, weighted, preferred_element_type=jnp.float32
    ).astype(jnp.bfloat16)
    second_child = jnp.einsum(
        "ayq,abq->yb", left_part, weighted, preferred_element_type=jnp.float32
    ).astype(jnp.bfloat16)
    return (first_child, second_child)


def placements(group_roles):
    group_size = group_roles.shape[0]
    spots = jnp.arange(group_size, dtype=jnp.int32)
    return jnp.sum(jnp.where(group_roles[None, :] == spots[:, None], spots[None, :], 0), axis=1)


def local(node_tensor, outer_env, upper_env, role_map, child_slots):
    tensor_here = node_tensor[0, 0]
    outer_envs = outer_env[0, 0]
    upper_envs = upper_env[0, 0]
    group_roles = role_map[0]
    child_links = child_slots[0]
    group_size = lax.axis_size("node")
    top_count = group_size // 4
    mid_count = 2 * top_count
    bond_size = tensor_here.shape[0]
    role_spot = placements(group_roles)
    position = lax.axis_index("node")
    my_role = group_roles[position]
    is_top = my_role < top_count
    is_mid = jnp.logical_and(my_role >= top_count, my_role < top_count + mid_count)
    is_leaf = my_role >= top_count + mid_count
    zero_envs = jnp.zeros((TERMS, bond_size, bond_size), jnp.bfloat16)

    def leaf_work():
        return jnp.stack([node_up(tensor_here, outer_envs[0, 0], outer_envs[1, 0])])

    leaf_up = lax.cond(is_leaf, leaf_work, lambda: zero_envs)
    leaf_spots = role_spot[top_count + mid_count :]
    every_leaf = node_gather(leaf_up, 0)
    leaf_table = jnp.take(every_leaf, leaf_spots, axis=0)
    mid_index = jnp.clip(my_role - top_count, 0, mid_count - 1)

    def mid_work():
        child_envs = []
        for branch in range(2):
            slot_link = child_links[2 * mid_index + branch]
            leaf_pick = leaf_table[jnp.maximum(slot_link, 0)]
            child_envs.append(jnp.where(slot_link >= 0, leaf_pick, outer_envs[branch]))
        return jnp.stack([node_up(tensor_here, child_envs[0][0], child_envs[1][0])])

    mid_up = lax.cond(is_mid, mid_work, lambda: zero_envs)
    mid_spots = role_spot[top_count : top_count + mid_count]
    every_mid = node_gather(mid_up, 1)
    mid_table = jnp.take(every_mid, mid_spots, axis=0)
    top_index = jnp.clip(my_role, 0, top_count - 1)
    next_half = from_behind(mid_table[top_count:], "sub", -1)
    right_envs = next_half[top_index]

    def top_work():
        left_env = mid_table[top_index]
        results = [node_down(tensor_here, left_env[0], right_envs[0], upper_envs[0])]
        return jnp.stack([jnp.stack([r[0] for r in results]), jnp.stack([r[1] for r in results])])

    top_down = lax.cond(
        is_top, top_work, lambda: jnp.zeros((2, TERMS, bond_size, bond_size), jnp.bfloat16)
    )
    top_spots = role_spot[:top_count]
    every_top = node_gather(top_down, 2)
    top_table = jnp.take(every_top, top_spots, axis=0)
    own_field = top_table[jnp.clip(mid_index, 0, top_count - 1), 0]
    from_before = from_behind(top_table[:, 1], "sub", 1)
    other_field = from_before[jnp.clip(mid_index - top_count, 0, top_count - 1)]
    mid_field = jnp.where(mid_index < top_count, own_field, other_field)
    result = jnp.where(is_mid, mid_field, jnp.where(is_leaf, leaf_up, zero_envs))
    return result[None, None]


def solution(mesh):
    return jax.shard_map(
        local,
        mesh=mesh,
        in_specs=(
            P("sub", "node", None, None, None),
            P("sub", "node", None, None, None, None),
            P("sub", "node", None, None, None),
            P("sub", None),
            P("sub", None),
        ),
        out_specs=P("sub", "node", None, None, None),
        check_vma=False,
    )
```

```python
import functools

import jax
import jax.numpy as jnp
from jax import lax
from jax.experimental import pallas as pl
from jax.experimental.pallas import tpu as pltpu
from jax.sharding import PartitionSpec as P

TERMS = 1
MESH = pl.DeviceIdType.MESH


def from_behind(block, axis, distance):
    devices = range(lax.axis_size(axis))
    route = [((i - distance) % len(devices), i) for i in devices]
    return lax.ppermute(block, axis, route)


def gather_kernel(n, x_ref, out_ref, send_sem, recv_sem, own_sem):
    me = lax.axis_index("node")
    group = lax.axis_index("sub")
    right = lax.rem(me + 1, n)
    left = lax.rem(me + n - 1, n)
    barrier = pltpu.get_barrier_semaphore()
    for neighbour in (left, right):
        pl.semaphore_signal(barrier, inc=1, device_id=(group, neighbour), device_id_type=MESH)
    pl.semaphore_wait(barrier, 2)
    own = pltpu.make_async_copy(x_ref, out_ref.at[me], own_sem)
    own.start()
    ways = ((0, 1, right, n // 2), (1, -1, left, n - 1 - n // 2))

    def hop(way, sign, target, step, origin):
        return pltpu.make_async_remote_copy(
            src_ref=x_ref if step == 0 else out_ref.at[origin],
            dst_ref=out_ref.at[origin],
            send_sem=send_sem.at[way, step],
            recv_sem=recv_sem.at[way, step],
            device_id=(group, target),
            device_id_type=MESH,
        )

    sent = []
    for step in range(n // 2):
        for way, sign, target, steps in ways:
            if step >= steps:
                continue
            origin = lax.rem(me - sign * step + 2 * n, n)
            if step > 0:
                hop(way, sign, target, step - 1, origin).wait_recv()
            copy = hop(way, sign, target, step, origin)
            copy.start()
            sent.append(copy)
    for way, sign, target, steps in ways:
        origin = lax.rem(me - sign * steps + 2 * n, n)
        hop(way, sign, target, steps - 1, origin).wait_recv()
    for copy in sent:
        copy.wait_send()
    own.wait()


def node_gather(block, collective_id):
    n = lax.axis_size("node")
    return pl.pallas_call(
        functools.partial(gather_kernel, n),
        out_shape=jax.ShapeDtypeStruct((n,) + block.shape, block.dtype),
        in_specs=[pl.BlockSpec(memory_space=pltpu.VMEM)],
        out_specs=pl.BlockSpec(memory_space=pltpu.VMEM),
        scratch_shapes=[
            pltpu.SemaphoreType.DMA((2, n // 2)),
            pltpu.SemaphoreType.DMA((2, n // 2)),
            pltpu.SemaphoreType.DMA,
        ],
        compiler_params=pltpu.CompilerParams(collective_id=collective_id, has_side_effects=True),
    )(block)


def node_up(tensor_here, left_env, right_env):
    first = jnp.einsum(
        "xa,abp->xbp", left_env, tensor_here, preferred_element_type=jnp.float32
    ).astype(jnp.bfloat16)
    second = jnp.einsum("yb,xbp->xyp", right_env, first, preferred_element_type=jnp.float32).astype(
        jnp.bfloat16
    )
    return jnp.einsum(
        "xyq,xyp->qp", tensor_here, second, preferred_element_type=jnp.float32
    ).astype(jnp.bfloat16)


def node_down(tensor_here, left_env, right_env, upper_here):
    weighted = jnp.einsum(
        "qp,abp->abq", upper_here, tensor_here, preferred_element_type=jnp.float32
    ).astype(jnp.bfloat16)
    right_part = jnp.einsum(
        "xyq,yb->xbq", tensor_here, right_env, preferred_element_type=jnp.float32
    ).astype(jnp.bfloat16)
    left_part = jnp.einsum(
        "xyq,xa->ayq", tensor_here, left_env, preferred_element_type=jnp.float32
    ).astype(jnp.bfloat16)
    first_child = jnp.einsum(
        "xbq,abq->xa", right_part, weighted, preferred_element_type=jnp.float32
    ).astype(jnp.bfloat16)
    second_child = jnp.einsum(
        "ayq,abq->yb", left_part, weighted, preferred_element_type=jnp.float32
    ).astype(jnp.bfloat16)
    return (first_child, second_child)


def placements(group_roles):
    group_size = group_roles.shape[0]
    spots = jnp.arange(group_size, dtype=jnp.int32)
    return jnp.sum(jnp.where(group_roles[None, :] == spots[:, None], spots[None, :], 0), axis=1)


def local(node_tensor, outer_env, upper_env, role_map, child_slots):
    tensor_here = node_tensor[0, 0]
    outer_envs = outer_env[0, 0]
    upper_envs = upper_env[0, 0]
    group_roles = role_map[0]
    child_links = child_slots[0]
    group_size = lax.axis_size("node")
    top_count = group_size // 4
    mid_count = 2 * top_count
    bond_size = tensor_here.shape[0]
    role_spot = placements(group_roles)
    position = lax.axis_index("node")
    my_role = group_roles[position]
    is_top = my_role < top_count
    is_mid = jnp.logical_and(my_role >= top_count, my_role < top_count + mid_count)
    is_leaf = my_role >= top_count + mid_count
    zero_envs = jnp.zeros((TERMS, bond_size, bond_size), jnp.bfloat16)

    def leaf_work():
        return jnp.stack([node_up(tensor_here, outer_envs[0, 0], outer_envs[1, 0])])

    leaf_up = lax.cond(is_leaf, leaf_work, lambda: zero_envs)
    leaf_spots = role_spot[top_count + mid_count :]
    every_leaf = node_gather(leaf_up, 0)
    leaf_table = jnp.take(every_leaf, leaf_spots, axis=0)
    mid_index = jnp.clip(my_role - top_count, 0, mid_count - 1)

    def mid_work():
        child_envs = []
        for branch in range(2):
            slot_link = child_links[2 * mid_index + branch]
            leaf_pick = leaf_table[jnp.maximum(slot_link, 0)]
            child_envs.append(jnp.where(slot_link >= 0, leaf_pick, outer_envs[branch]))
        return jnp.stack([node_up(tensor_here, child_envs[0][0], child_envs[1][0])])

    mid_up = lax.cond(is_mid, mid_work, lambda: zero_envs)
    next_roles = from_behind(group_roles, "sub", -1)
    prev_roles = from_behind(group_roles, "sub", 1)
    mid_pair = jnp.stack([mid_up, from_behind(mid_up, "sub", -1)])
    every_mid = node_gather(mid_pair, 1)
    top_index = jnp.clip(my_role, 0, top_count - 1)
    left_spot = role_spot[top_count + top_index]
    right_spot = placements(next_roles)[top_count + top_count + top_index]
    left_env = every_mid[left_spot, 0]
    right_env = every_mid[right_spot, 1]

    def top_work():
        results = [node_down(tensor_here, left_env[t], right_env[t], upper_envs[t]) for t in range(TERMS)]
        return jnp.stack([jnp.stack([r[0] for r in results]), jnp.stack([r[1] for r in results])])

    top_down = lax.cond(
        is_top, top_work, lambda: jnp.zeros((2, TERMS, bond_size, bond_size), jnp.bfloat16)
    )
    top_pair = jnp.stack([top_down[0], from_behind(top_down[1], "sub", 1)])
    every_top = node_gather(top_pair, 2)
    own_field = every_top[role_spot[jnp.clip(mid_index, 0, top_count - 1)], 0]
    other_field = every_top[placements(prev_roles)[jnp.clip(mid_index - top_count, 0, top_count - 1)], 1]
    mid_field = jnp.where(mid_index < top_count, own_field, other_field)
    result = jnp.where(is_mid, mid_field, jnp.where(is_leaf, leaf_up, zero_envs))
    return result[None, None]


def solution(mesh):
    return jax.shard_map(
        local,
        mesh=mesh,
        in_specs=(
            P("sub", "node", None, None, None),
            P("sub", "node", None, None, None, None),
            P("sub", "node", None, None, None),
            P("sub", None),
            P("sub", None),
        ),
        out_specs=P("sub", "node", None, None, None),
        check_vma=False,
    )
```

```python
import functools

import jax
import jax.numpy as jnp
from jax import lax
from jax.experimental import pallas as pl
from jax.experimental.pallas import tpu as pltpu
from jax.sharding import PartitionSpec as P

TERMS = 1
MESH = pl.DeviceIdType.MESH


def from_behind(block, axis, distance):
    devices = range(lax.axis_size(axis))
    route = [((i - distance) % len(devices), i) for i in devices]
    return lax.ppermute(block, axis, route)


def gather_kernel(n, groups, shift, x_ref, out_ref, send_sem, recv_sem, own_sem, sub_sem):
    me = lax.axis_index("node")
    group = lax.axis_index("sub")
    right = lax.rem(me + 1, n)
    left = lax.rem(me + n - 1, n)
    barrier = pltpu.get_barrier_semaphore()
    peers = [(group, left), (group, right)]
    if shift:
        peers += [(lax.rem(group + shift + groups, groups), me), (lax.rem(group - shift + groups, groups), me)]
    for peer in peers:
        pl.semaphore_signal(barrier, inc=1, device_id=peer, device_id_type=MESH)
    pl.semaphore_wait(barrier, len(peers))
    if shift:
        own = pltpu.make_async_copy(x_ref.at[0], out_ref.at[me, 0], own_sem)
        own.start()
        across = pltpu.make_async_remote_copy(
            src_ref=x_ref.at[1],
            dst_ref=out_ref.at[me, 1],
            send_sem=sub_sem.at[0],
            recv_sem=sub_sem.at[1],
            device_id=peers[2],
            device_id_type=MESH,
        )
        across.start()
        own.wait()
        across.wait_recv()
        first_src = out_ref.at[me]
    else:
        own = pltpu.make_async_copy(x_ref, out_ref.at[me], own_sem)
        own.start()
        first_src = x_ref
    ways = ((0, 1, right, n // 2), (1, -1, left, n - 1 - n // 2))

    def hop(way, target, step, origin):
        return pltpu.make_async_remote_copy(
            src_ref=first_src if step == 0 else out_ref.at[origin],
            dst_ref=out_ref.at[origin],
            send_sem=send_sem.at[way, step],
            recv_sem=recv_sem.at[way, step],
            device_id=(group, target),
            device_id_type=MESH,
        )

    sent = []
    for step in range(n // 2):
        for way, sign, target, steps in ways:
            if step >= steps:
                continue
            origin = lax.rem(me - sign * step + 2 * n, n)
            if step > 0:
                hop(way, target, step - 1, origin).wait_recv()
            copy = hop(way, target, step, origin)
            copy.start()
            sent.append(copy)
    for way, sign, target, steps in ways:
        origin = lax.rem(me - sign * steps + 2 * n, n)
        hop(way, target, steps - 1, origin).wait_recv()
    for copy in sent:
        copy.wait_send()
    if shift:
        across.wait_send()
    else:
        own.wait()


def node_gather(block, collective_id, shift=0):
    n = lax.axis_size("node")
    groups = lax.axis_size("sub")
    return pl.pallas_call(
        functools.partial(gather_kernel, n, groups, shift),
        out_shape=jax.ShapeDtypeStruct((n,) + block.shape, block.dtype),
        in_specs=[pl.BlockSpec(memory_space=pltpu.VMEM)],
        out_specs=pl.BlockSpec(memory_space=pltpu.VMEM),
        scratch_shapes=[
            pltpu.SemaphoreType.DMA((2, n // 2)),
            pltpu.SemaphoreType.DMA((2, n // 2)),
            pltpu.SemaphoreType.DMA,
            pltpu.SemaphoreType.DMA((2,)),
        ],
        compiler_params=pltpu.CompilerParams(collective_id=collective_id, has_side_effects=True),
    )(block)


def node_up(tensor_here, left_env, right_env):
    first = jnp.einsum(
        "xa,abp->xbp", left_env, tensor_here, preferred_element_type=jnp.float32
    ).astype(jnp.bfloat16)
    second = jnp.einsum("yb,xbp->xyp", right_env, first, preferred_element_type=jnp.float32).astype(
        jnp.bfloat16
    )
    return jnp.einsum(
        "xyq,xyp->qp", tensor_here, second, preferred_element_type=jnp.float32
    ).astype(jnp.bfloat16)


def node_down(tensor_here, left_env, right_env, upper_here):
    weighted = jnp.einsum(
        "qp,abp->abq", upper_here, tensor_here, preferred_element_type=jnp.float32
    ).astype(jnp.bfloat16)
    right_part = jnp.einsum(
        "xyq,yb->xbq", tensor_here, right_env, preferred_element_type=jnp.float32
    ).astype(jnp.bfloat16)
    left_part = jnp.einsum(
        "xyq,xa->ayq", tensor_here, left_env, preferred_element_type=jnp.float32
    ).astype(jnp.bfloat16)
    first_child = jnp.einsum(
        "xbq,abq->xa", right_part, weighted, preferred_element_type=jnp.float32
    ).astype(jnp.bfloat16)
    second_child = jnp.einsum(
        "ayq,abq->yb", left_part, weighted, preferred_element_type=jnp.float32
    ).astype(jnp.bfloat16)
    return (first_child, second_child)


def placements(group_roles):
    group_size = group_roles.shape[0]
    spots = jnp.arange(group_size, dtype=jnp.int32)
    return jnp.sum(jnp.where(group_roles[None, :] == spots[:, None], spots[None, :], 0), axis=1)


def local(node_tensor, outer_env, upper_env, role_map, child_slots):
    tensor_here = node_tensor[0, 0]
    outer_envs = outer_env[0, 0]
    upper_envs = upper_env[0, 0]
    group_roles = role_map[0]
    child_links = child_slots[0]
    group_size = lax.axis_size("node")
    top_count = group_size // 4
    mid_count = 2 * top_count
    bond_size = tensor_here.shape[0]
    role_spot = placements(group_roles)
    position = lax.axis_index("node")
    my_role = group_roles[position]
    is_top = my_role < top_count
    is_mid = jnp.logical_and(my_role >= top_count, my_role < top_count + mid_count)
    is_leaf = my_role >= top_count + mid_count
    zero_envs = jnp.zeros((TERMS, bond_size, bond_size), jnp.bfloat16)

    def leaf_work():
        return jnp.stack([node_up(tensor_here, outer_envs[0, 0], outer_envs[1, 0])])

    leaf_up = lax.cond(is_leaf, leaf_work, lambda: zero_envs)
    leaf_spots = role_spot[top_count + mid_count :]
    every_leaf = node_gather(leaf_up, 0)
    leaf_table = jnp.take(every_leaf, leaf_spots, axis=0)
    mid_index = jnp.clip(my_role - top_count, 0, mid_count - 1)

    def mid_work():
        child_envs = []
        for branch in range(2):
            slot_link = child_links[2 * mid_index + branch]
            leaf_pick = leaf_table[jnp.maximum(slot_link, 0)]
            child_envs.append(jnp.where(slot_link >= 0, leaf_pick, outer_envs[branch]))
        return jnp.stack([node_up(tensor_here, child_envs[0][0], child_envs[1][0])])

    mid_up = lax.cond(is_mid, mid_work, lambda: zero_envs)
    next_roles = from_behind(group_roles, "sub", -1)
    prev_roles = from_behind(group_roles, "sub", 1)
    every_mid = node_gather(jnp.stack([mid_up, mid_up]), 1, -1)
    top_index = jnp.clip(my_role, 0, top_count - 1)
    left_spot = role_spot[top_count + top_index]
    right_spot = placements(next_roles)[top_count + top_count + top_index]
    left_env = every_mid[left_spot, 0]
    right_env = every_mid[right_spot, 1]

    def top_work():
        results = [node_down(tensor_here, left_env[t], right_env[t], upper_envs[t]) for t in range(TERMS)]
        return jnp.stack([jnp.stack([r[0] for r in results]), jnp.stack([r[1] for r in results])])

    top_down = lax.cond(
        is_top, top_work, lambda: jnp.zeros((2, TERMS, bond_size, bond_size), jnp.bfloat16)
    )
    every_top = node_gather(top_down, 2, 1)
    own_field = every_top[role_spot[jnp.clip(mid_index, 0, top_count - 1)], 0]
    other_field = every_top[placements(prev_roles)[jnp.clip(mid_index - top_count, 0, top_count - 1)], 1]
    mid_field = jnp.where(mid_index < top_count, own_field, other_field)
    result = jnp.where(is_mid, mid_field, jnp.where(is_leaf, leaf_up, zero_envs))
    return result[None, None]


def solution(mesh):
    return jax.shard_map(
        local,
        mesh=mesh,
        in_specs=(
            P("sub", "node", None, None, None),
            P("sub", "node", None, None, None, None),
            P("sub", "node", None, None, None),
            P("sub", None),
            P("sub", None),
        ),
        out_specs=P("sub", "node", None, None, None),
        check_vma=False,
    )
```

```python
import functools

import jax
import jax.numpy as jnp
from jax import lax
from jax.experimental import pallas as pl
from jax.experimental.pallas import tpu as pltpu
from jax.sharding import PartitionSpec as P

TERMS = 1
MESH = pl.DeviceIdType.MESH


def from_behind(block, axis, distance):
    devices = range(lax.axis_size(axis))
    route = [((i - distance) % len(devices), i) for i in devices]
    return lax.ppermute(block, axis, route)


def gather_kernel(n, groups, shift, x_ref, out_ref, send_sem, recv_sem, own_sem, sub_sem):
    me = lax.axis_index("node")
    group = lax.axis_index("sub")
    right = lax.rem(me + 1, n)
    left = lax.rem(me + n - 1, n)
    barrier = pltpu.get_barrier_semaphore()
    peers = [(group, left), (group, right)]
    if shift:
        peers += [(lax.rem(group + shift + groups, groups), me), (lax.rem(group - shift + groups, groups), me)]
    for peer in peers:
        pl.semaphore_signal(barrier, inc=1, device_id=peer, device_id_type=MESH)
    pl.semaphore_wait(barrier, len(peers))
    if shift:
        own = pltpu.make_async_copy(x_ref.at[0], out_ref.at[me, 0], own_sem)
        own.start()
        across = pltpu.make_async_remote_copy(
            src_ref=x_ref.at[1],
            dst_ref=out_ref.at[me, 1],
            send_sem=sub_sem.at[0],
            recv_sem=sub_sem.at[1],
            device_id=peers[2],
            device_id_type=MESH,
        )
        across.start()
        own.wait()
        across.wait_recv()
        first_src = out_ref.at[me]
    else:
        own = pltpu.make_async_copy(x_ref, out_ref.at[me], own_sem)
        own.start()
        first_src = x_ref
    ways = ((0, 1, right, n // 2), (1, -1, left, n - 1 - n // 2))

    def hop(way, target, step, origin):
        return pltpu.make_async_remote_copy(
            src_ref=first_src if step == 0 else out_ref.at[origin],
            dst_ref=out_ref.at[origin],
            send_sem=send_sem.at[way, step],
            recv_sem=recv_sem.at[way, step],
            device_id=(group, target),
            device_id_type=MESH,
        )

    sent = []
    for step in range(n // 2):
        for way, sign, target, steps in ways:
            if step >= steps:
                continue
            origin = lax.rem(me - sign * step + 2 * n, n)
            if step > 0:
                hop(way, target, step - 1, origin).wait_recv()
            copy = hop(way, target, step, origin)
            copy.start()
            sent.append(copy)
    for way, sign, target, steps in ways:
        origin = lax.rem(me - sign * steps + 2 * n, n)
        hop(way, target, steps - 1, origin).wait_recv()
    for copy in sent:
        copy.wait_send()
    if shift:
        across.wait_send()
    else:
        own.wait()


def node_gather(block, collective_id, shift=0):
    n = lax.axis_size("node")
    groups = lax.axis_size("sub")
    return pl.pallas_call(
        functools.partial(gather_kernel, n, groups, shift),
        out_shape=jax.ShapeDtypeStruct((n,) + block.shape, block.dtype),
        in_specs=[pl.BlockSpec(memory_space=pltpu.VMEM)],
        out_specs=pl.BlockSpec(memory_space=pltpu.VMEM),
        scratch_shapes=[
            pltpu.SemaphoreType.DMA((2, n // 2)),
            pltpu.SemaphoreType.DMA((2, n // 2)),
            pltpu.SemaphoreType.DMA,
            pltpu.SemaphoreType.DMA((2,)),
        ],
        compiler_params=pltpu.CompilerParams(collective_id=collective_id, has_side_effects=True),
    )(block)


def node_up(tensor_here, left_env, right_env):
    first = jnp.einsum(
        "xa,abp->xbp", left_env, tensor_here, preferred_element_type=jnp.float32
    ).astype(jnp.bfloat16)
    second = jnp.einsum("yb,xbp->xyp", right_env, first, preferred_element_type=jnp.float32).astype(
        jnp.bfloat16
    )
    return jnp.einsum(
        "xyq,xyp->qp", tensor_here, second, preferred_element_type=jnp.float32
    ).astype(jnp.bfloat16)


def node_down(tensor_here, left_env, right_env, upper_here):
    weighted = jnp.einsum(
        "qp,abp->abq", upper_here, tensor_here, preferred_element_type=jnp.float32
    ).astype(jnp.bfloat16)
    right_part = jnp.einsum(
        "xyq,yb->xbq", tensor_here, right_env, preferred_element_type=jnp.float32
    ).astype(jnp.bfloat16)
    left_part = jnp.einsum(
        "xyq,xa->ayq", tensor_here, left_env, preferred_element_type=jnp.float32
    ).astype(jnp.bfloat16)
    first_child = jnp.einsum(
        "xbq,abq->xa", right_part, weighted, preferred_element_type=jnp.float32
    ).astype(jnp.bfloat16)
    second_child = jnp.einsum(
        "ayq,abq->yb", left_part, weighted, preferred_element_type=jnp.float32
    ).astype(jnp.bfloat16)
    return (first_child, second_child)


def placements(group_roles):
    group_size = group_roles.shape[0]
    spots = jnp.arange(group_size, dtype=jnp.int32)
    return jnp.sum(jnp.where(group_roles[None, :] == spots[:, None], spots[None, :], 0), axis=1)


def local(node_tensor, outer_env, upper_env, role_map, child_slots):
    tensor_here = node_tensor[0, 0]
    outer_envs = outer_env[0, 0]
    upper_envs = upper_env[0, 0]
    group_roles = role_map[0]
    child_links = child_slots[0]
    group_size = lax.axis_size("node")
    top_count = group_size // 4
    mid_count = 2 * top_count
    bond_size = tensor_here.shape[0]
    role_spot = placements(group_roles)
    position = lax.axis_index("node")
    my_role = group_roles[position]
    is_top = my_role < top_count
    is_mid = jnp.logical_and(my_role >= top_count, my_role < top_count + mid_count)
    is_leaf = my_role >= top_count + mid_count
    zero_envs = jnp.zeros((TERMS, bond_size, bond_size), jnp.bfloat16)

    def leaf_work():
        return jnp.stack([node_up(tensor_here, outer_envs[0, 0], outer_envs[1, 0])])

    leaf_up = lax.cond(is_leaf, leaf_work, lambda: zero_envs)
    leaf_spots = role_spot[top_count + mid_count :]
    every_leaf = node_gather(leaf_up, 0)
    leaf_table = jnp.take(every_leaf, leaf_spots, axis=0)
    mid_index = jnp.clip(my_role - top_count, 0, mid_count - 1)

    def mid_work():
        child_envs = []
        for branch in range(2):
            slot_link = child_links[2 * mid_index + branch]
            leaf_pick = leaf_table[jnp.maximum(slot_link, 0)]
            child_envs.append(jnp.where(slot_link >= 0, leaf_pick, outer_envs[branch]))
        return jnp.stack([node_up(tensor_here, child_envs[0][0], child_envs[1][0])])

    mid_up = lax.cond(is_mid, mid_work, lambda: zero_envs)
    mid_spots = role_spot[top_count : top_count + mid_count]
    every_mid = node_gather(mid_up, 1)
    mid_table = jnp.take(every_mid, mid_spots, axis=0)
    top_index = jnp.clip(my_role, 0, top_count - 1)
    next_half = from_behind(mid_table[top_count:], "sub", -1)
    right_envs = next_half[top_index]

    def top_work():
        left_env = mid_table[top_index]
        results = [node_down(tensor_here, left_env[0], right_envs[0], upper_envs[0])]
        return jnp.stack([jnp.stack([r[0] for r in results]), jnp.stack([r[1] for r in results])])

    top_down = lax.cond(
        is_top, top_work, lambda: jnp.zeros((2, TERMS, bond_size, bond_size), jnp.bfloat16)
    )
    prev_roles = from_behind(group_roles, "sub", 1)
    every_top = node_gather(top_down, 2, 1)
    own_field = every_top[role_spot[jnp.clip(mid_index, 0, top_count - 1)], 0]
    other_field = every_top[placements(prev_roles)[jnp.clip(mid_index - top_count, 0, top_count - 1)], 1]
    mid_field = jnp.where(mid_index < top_count, own_field, other_field)
    result = jnp.where(is_mid, mid_field, jnp.where(is_leaf, leaf_up, zero_envs))
    return result[None, None]


def solution(mesh):
    return jax.shard_map(
        local,
        mesh=mesh,
        in_specs=(
            P("sub", "node", None, None, None),
            P("sub", "node", None, None, None, None),
            P("sub", "node", None, None, None),
            P("sub", None),
            P("sub", None),
        ),
        out_specs=P("sub", "node", None, None, None),
        check_vma=False,
    )
```

```python
import functools

import jax
import jax.numpy as jnp
from jax import lax
from jax.experimental import pallas as pl
from jax.experimental.pallas import tpu as pltpu
from jax.sharding import PartitionSpec as P

TERMS = 1
MESH = pl.DeviceIdType.MESH


def from_behind(block, axis, distance):
    devices = range(lax.axis_size(axis))
    route = [((i - distance) % len(devices), i) for i in devices]
    return lax.ppermute(block, axis, route)


def gather_kernel(n, groups, shift, pieces, x_ref, out_ref, send_sem, recv_sem, own_sem, sub_sem):
    me = lax.axis_index("node")
    group = lax.axis_index("sub")
    right = lax.rem(me + 1, n)
    left = lax.rem(me + n - 1, n)
    barrier = pltpu.get_barrier_semaphore()
    peers = [(group, left), (group, right)]
    if shift:
        peers += [(lax.rem(group + shift + groups, groups), me), (lax.rem(group - shift + groups, groups), me)]
    for peer in peers:
        pl.semaphore_signal(barrier, inc=1, device_id=peer, device_id_type=MESH)
    pl.semaphore_wait(barrier, len(peers))
    if shift:
        own = pltpu.make_async_copy(x_ref.at[0], out_ref.at[me, 0], own_sem)
        own.start()
        across = pltpu.make_async_remote_copy(
            src_ref=x_ref.at[1],
            dst_ref=out_ref.at[me, 1],
            send_sem=sub_sem.at[0],
            recv_sem=sub_sem.at[1],
            device_id=peers[2],
            device_id_type=MESH,
        )
        across.start()
        own.wait()
        across.wait_recv()
        first_src = out_ref.at[me]
    else:
        own = pltpu.make_async_copy(x_ref, out_ref.at[me], own_sem)
        own.start()
        first_src = x_ref
    ways = ((0, 1, right, n // 2), (1, -1, left, n - 1 - n // 2))
    rows = x_ref.shape[-2] // pieces
    lead = (slice(None),) * (len(x_ref.shape) - 2)

    def hop(way, target, step, origin, piece):
        part = lead + (pl.ds(piece * rows, rows), slice(None))
        return pltpu.make_async_remote_copy(
            src_ref=(first_src if step == 0 else out_ref.at[origin]).at[part],
            dst_ref=out_ref.at[origin].at[part],
            send_sem=send_sem.at[way, step, piece],
            recv_sem=recv_sem.at[way, step, piece],
            device_id=(group, target),
            device_id_type=MESH,
        )

    sent = []
    for step in range(n // 2):
        for way, sign, target, steps in ways:
            if step >= steps:
                continue
            origin = lax.rem(me - sign * step + 2 * n, n)
            for piece in range(pieces):
                if step > 0:
                    hop(way, target, step - 1, origin, piece).wait_recv()
                copy = hop(way, target, step, origin, piece)
                copy.start()
                sent.append(copy)
    for way, sign, target, steps in ways:
        origin = lax.rem(me - sign * steps + 2 * n, n)
        for piece in range(pieces):
            hop(way, target, steps - 1, origin, piece).wait_recv()
    for copy in sent:
        copy.wait_send()
    if shift:
        across.wait_send()
    else:
        own.wait()


def node_gather(block, collective_id, shift=0, pieces=2):
    n = lax.axis_size("node")
    groups = lax.axis_size("sub")
    return pl.pallas_call(
        functools.partial(gather_kernel, n, groups, shift, pieces),
        out_shape=jax.ShapeDtypeStruct((n,) + block.shape, block.dtype),
        in_specs=[pl.BlockSpec(memory_space=pltpu.VMEM)],
        out_specs=pl.BlockSpec(memory_space=pltpu.VMEM),
        scratch_shapes=[
            pltpu.SemaphoreType.DMA((2, n // 2, pieces)),
            pltpu.SemaphoreType.DMA((2, n // 2, pieces)),
            pltpu.SemaphoreType.DMA,
            pltpu.SemaphoreType.DMA((2,)),
        ],
        compiler_params=pltpu.CompilerParams(collective_id=collective_id, has_side_effects=True),
    )(block)


def node_up(tensor_here, left_env, right_env):
    first = jnp.einsum(
        "xa,abp->xbp", left_env, tensor_here, preferred_element_type=jnp.float32
    ).astype(jnp.bfloat16)
    second = jnp.einsum("yb,xbp->xyp", right_env, first, preferred_element_type=jnp.float32).astype(
        jnp.bfloat16
    )
    return jnp.einsum(
        "xyq,xyp->qp", tensor_here, second, preferred_element_type=jnp.float32
    ).astype(jnp.bfloat16)


def node_down(tensor_here, left_env, right_env, upper_here):
    weighted = jnp.einsum(
        "qp,abp->abq", upper_here, tensor_here, preferred_element_type=jnp.float32
    ).astype(jnp.bfloat16)
    right_part = jnp.einsum(
        "xyq,yb->xbq", tensor_here, right_env, preferred_element_type=jnp.float32
    ).astype(jnp.bfloat16)
    left_part = jnp.einsum(
        "xyq,xa->ayq", tensor_here, left_env, preferred_element_type=jnp.float32
    ).astype(jnp.bfloat16)
    first_child = jnp.einsum(
        "xbq,abq->xa", right_part, weighted, preferred_element_type=jnp.float32
    ).astype(jnp.bfloat16)
    second_child = jnp.einsum(
        "ayq,abq->yb", left_part, weighted, preferred_element_type=jnp.float32
    ).astype(jnp.bfloat16)
    return (first_child, second_child)


def placements(group_roles):
    group_size = group_roles.shape[0]
    spots = jnp.arange(group_size, dtype=jnp.int32)
    return jnp.sum(jnp.where(group_roles[None, :] == spots[:, None], spots[None, :], 0), axis=1)


def local(node_tensor, outer_env, upper_env, role_map, child_slots):
    tensor_here = node_tensor[0, 0]
    outer_envs = outer_env[0, 0]
    upper_envs = upper_env[0, 0]
    group_roles = role_map[0]
    child_links = child_slots[0]
    group_size = lax.axis_size("node")
    top_count = group_size // 4
    mid_count = 2 * top_count
    bond_size = tensor_here.shape[0]
    role_spot = placements(group_roles)
    position = lax.axis_index("node")
    my_role = group_roles[position]
    is_top = my_role < top_count
    is_mid = jnp.logical_and(my_role >= top_count, my_role < top_count + mid_count)
    is_leaf = my_role >= top_count + mid_count
    zero_envs = jnp.zeros((TERMS, bond_size, bond_size), jnp.bfloat16)

    def leaf_work():
        return jnp.stack([node_up(tensor_here, outer_envs[0, 0], outer_envs[1, 0])])

    leaf_up = lax.cond(is_leaf, leaf_work, lambda: zero_envs)
    leaf_spots = role_spot[top_count + mid_count :]
    every_leaf = node_gather(leaf_up, 0)
    leaf_table = jnp.take(every_leaf, leaf_spots, axis=0)
    mid_index = jnp.clip(my_role - top_count, 0, mid_count - 1)

    def mid_work():
        child_envs = []
        for branch in range(2):
            slot_link = child_links[2 * mid_index + branch]
            leaf_pick = leaf_table[jnp.maximum(slot_link, 0)]
            child_envs.append(jnp.where(slot_link >= 0, leaf_pick, outer_envs[branch]))
        return jnp.stack([node_up(tensor_here, child_envs[0][0], child_envs[1][0])])

    mid_up = lax.cond(is_mid, mid_work, lambda: zero_envs)
    mid_spots = role_spot[top_count : top_count + mid_count]
    every_mid = node_gather(mid_up, 1)
    mid_table = jnp.take(every_mid, mid_spots, axis=0)
    top_index = jnp.clip(my_role, 0, top_count - 1)
    next_half = from_behind(mid_table[top_count:], "sub", -1)
    right_envs = next_half[top_index]

    def top_work():
        left_env = mid_table[top_index]
        results = [node_down(tensor_here, left_env[0], right_envs[0], upper_envs[0])]
        return jnp.stack([jnp.stack([r[0] for r in results]), jnp.stack([r[1] for r in results])])

    top_down = lax.cond(
        is_top, top_work, lambda: jnp.zeros((2, TERMS, bond_size, bond_size), jnp.bfloat16)
    )
    prev_roles = from_behind(group_roles, "sub", 1)
    every_top = node_gather(top_down, 2, 1)
    own_field = every_top[role_spot[jnp.clip(mid_index, 0, top_count - 1)], 0]
    other_field = every_top[placements(prev_roles)[jnp.clip(mid_index - top_count, 0, top_count - 1)], 1]
    mid_field = jnp.where(mid_index < top_count, own_field, other_field)
    result = jnp.where(is_mid, mid_field, jnp.where(is_leaf, leaf_up, zero_envs))
    return result[None, None]


def solution(mesh):
    return jax.shard_map(
        local,
        mesh=mesh,
        in_specs=(
            P("sub", "node", None, None, None),
            P("sub", "node", None, None, None, None),
            P("sub", "node", None, None, None),
            P("sub", None),
            P("sub", None),
        ),
        out_specs=P("sub", "node", None, None, None),
        check_vma=False,
    )
```

```python
import functools

import jax
import jax.numpy as jnp
from jax import lax
from jax.experimental import pallas as pl
from jax.experimental.pallas import tpu as pltpu
from jax.sharding import PartitionSpec as P

TERMS = 1
MESH = pl.DeviceIdType.MESH


def from_behind(block, axis, distance):
    devices = range(lax.axis_size(axis))
    route = [((i - distance) % len(devices), i) for i in devices]
    return lax.ppermute(block, axis, route)


def gather_kernel(n, groups, shift, pieces, x_ref, out_ref, send_sem, recv_sem, own_sem, sub_sem):
    me = lax.axis_index("node")
    group = lax.axis_index("sub")
    right = lax.rem(me + 1, n)
    left = lax.rem(me + n - 1, n)
    barrier = pltpu.get_barrier_semaphore()
    peers = [(group, left), (group, right)]
    if shift:
        peers += [(lax.rem(group + shift + groups, groups), me), (lax.rem(group - shift + groups, groups), me)]
    for peer in peers:
        pl.semaphore_signal(barrier, inc=1, device_id=peer, device_id_type=MESH)
    pl.semaphore_wait(barrier, len(peers))
    if shift:
        own = pltpu.make_async_copy(x_ref.at[0], out_ref.at[me, 0], own_sem)
        own.start()
        across = pltpu.make_async_remote_copy(
            src_ref=x_ref.at[1],
            dst_ref=out_ref.at[me, 1],
            send_sem=sub_sem.at[0],
            recv_sem=sub_sem.at[1],
            device_id=peers[2],
            device_id_type=MESH,
        )
        across.start()
        own.wait()
        across.wait_recv()
        first_src = out_ref.at[me]
    else:
        own = pltpu.make_async_copy(x_ref, out_ref.at[me], own_sem)
        own.start()
        first_src = x_ref
    ways = ((0, 1, right, n // 2), (1, -1, left, n - 1 - n // 2))
    rows = x_ref.shape[-2] // pieces
    lead = (slice(None),) * (len(x_ref.shape) - 2)

    def hop(way, target, step, origin, piece):
        part = lead + (pl.ds(piece * rows, rows), slice(None))
        return pltpu.make_async_remote_copy(
            src_ref=(first_src if step == 0 else out_ref.at[origin]).at[part],
            dst_ref=out_ref.at[origin].at[part],
            send_sem=send_sem.at[way, step, piece],
            recv_sem=recv_sem.at[way, step, piece],
            device_id=(group, target),
            device_id_type=MESH,
        )

    sent = []
    for step in range(n // 2):
        for way, sign, target, steps in ways:
            if step >= steps:
                continue
            origin = lax.rem(me - sign * step + 2 * n, n)
            for piece in range(pieces):
                if step > 0:
                    hop(way, target, step - 1, origin, piece).wait_recv()
                copy = hop(way, target, step, origin, piece)
                copy.start()
                sent.append(copy)
    for way, sign, target, steps in ways:
        origin = lax.rem(me - sign * steps + 2 * n, n)
        for piece in range(pieces):
            hop(way, target, steps - 1, origin, piece).wait_recv()
    for copy in sent:
        copy.wait_send()
    if shift:
        across.wait_send()
    else:
        own.wait()


def node_gather(block, collective_id, shift=0, pieces=2):
    n = lax.axis_size("node")
    groups = lax.axis_size("sub")
    return pl.pallas_call(
        functools.partial(gather_kernel, n, groups, shift, pieces),
        out_shape=jax.ShapeDtypeStruct((n,) + block.shape, block.dtype),
        in_specs=[pl.BlockSpec(memory_space=pltpu.VMEM)],
        out_specs=pl.BlockSpec(memory_space=pltpu.VMEM),
        scratch_shapes=[
            pltpu.SemaphoreType.DMA((2, n // 2, pieces)),
            pltpu.SemaphoreType.DMA((2, n // 2, pieces)),
            pltpu.SemaphoreType.DMA,
            pltpu.SemaphoreType.DMA((2,)),
        ],
        compiler_params=pltpu.CompilerParams(collective_id=collective_id, has_side_effects=True),
    )(block)


def node_up(tensor_here, left_env, right_env):
    first = jnp.einsum(
        "xa,abp->xbp", left_env, tensor_here, preferred_element_type=jnp.float32
    ).astype(jnp.bfloat16)
    second = jnp.einsum("yb,xbp->xyp", right_env, first, preferred_element_type=jnp.float32).astype(
        jnp.bfloat16
    )
    return jnp.einsum(
        "xyq,xyp->qp", tensor_here, second, preferred_element_type=jnp.float32
    ).astype(jnp.bfloat16)


def node_down(tensor_here, left_env, right_env, upper_here):
    weighted = jnp.einsum(
        "qp,abp->abq", upper_here, tensor_here, preferred_element_type=jnp.float32
    ).astype(jnp.bfloat16)
    right_part = jnp.einsum(
        "xyq,yb->xbq", tensor_here, right_env, preferred_element_type=jnp.float32
    ).astype(jnp.bfloat16)
    left_part = jnp.einsum(
        "xyq,xa->ayq", tensor_here, left_env, preferred_element_type=jnp.float32
    ).astype(jnp.bfloat16)
    first_child = jnp.einsum(
        "xbq,abq->xa", right_part, weighted, preferred_element_type=jnp.float32
    ).astype(jnp.bfloat16)
    second_child = jnp.einsum(
        "ayq,abq->yb", left_part, weighted, preferred_element_type=jnp.float32
    ).astype(jnp.bfloat16)
    return (first_child, second_child)


def placements(group_roles):
    group_size = group_roles.shape[0]
    spots = jnp.arange(group_size, dtype=jnp.int32)
    return jnp.sum(jnp.where(group_roles[None, :] == spots[:, None], spots[None, :], 0), axis=1)


def local(node_tensor, outer_env, upper_env, role_map, child_slots):
    tensor_here = node_tensor[0, 0]
    outer_envs = outer_env[0, 0]
    upper_envs = upper_env[0, 0]
    group_roles = role_map[0]
    child_links = child_slots[0]
    group_size = lax.axis_size("node")
    top_count = group_size // 4
    mid_count = 2 * top_count
    bond_size = tensor_here.shape[0]
    role_spot = placements(group_roles)
    position = lax.axis_index("node")
    my_role = group_roles[position]
    is_top = my_role < top_count
    is_mid = jnp.logical_and(my_role >= top_count, my_role < top_count + mid_count)
    is_leaf = my_role >= top_count + mid_count
    zero_envs = jnp.zeros((TERMS, bond_size, bond_size), jnp.bfloat16)

    def leaf_work():
        return jnp.stack([node_up(tensor_here, outer_envs[0, 0], outer_envs[1, 0])])

    leaf_up = lax.cond(is_leaf, leaf_work, lambda: zero_envs)
    leaf_spots = role_spot[top_count + mid_count :]
    every_leaf = node_gather(leaf_up, 0)
    leaf_table = jnp.take(every_leaf, leaf_spots, axis=0)
    mid_index = jnp.clip(my_role - top_count, 0, mid_count - 1)

    def mid_work():
        child_envs = []
        for branch in range(2):
            slot_link = child_links[2 * mid_index + branch]
            leaf_pick = leaf_table[jnp.maximum(slot_link, 0)]
            child_envs.append(jnp.where(slot_link >= 0, leaf_pick, outer_envs[branch]))
        return jnp.stack([node_up(tensor_here, child_envs[0][0], child_envs[1][0])])

    mid_up = lax.cond(is_mid, mid_work, lambda: zero_envs)
    next_roles = from_behind(group_roles, "sub", -1)
    every_mid = node_gather(jnp.stack([mid_up, mid_up]), 1, -1)
    top_index = jnp.clip(my_role, 0, top_count - 1)
    mid_table = jnp.take(every_mid[:, 0], role_spot[top_count : top_count + mid_count], axis=0)
    next_spots = placements(next_roles)[top_count + top_count : top_count + mid_count]
    right_envs = jnp.take(every_mid[:, 1], next_spots, axis=0)[top_index]

    def top_work():
        left_env = mid_table[top_index]
        results = [node_down(tensor_here, left_env[0], right_envs[0], upper_envs[0])]
        return jnp.stack([jnp.stack([r[0] for r in results]), jnp.stack([r[1] for r in results])])

    top_down = lax.cond(
        is_top, top_work, lambda: jnp.zeros((2, TERMS, bond_size, bond_size), jnp.bfloat16)
    )
    prev_roles = from_behind(group_roles, "sub", 1)
    every_top = node_gather(top_down, 2, 1)
    own_field = every_top[role_spot[jnp.clip(mid_index, 0, top_count - 1)], 0]
    other_field = every_top[placements(prev_roles)[jnp.clip(mid_index - top_count, 0, top_count - 1)], 1]
    mid_field = jnp.where(mid_index < top_count, own_field, other_field)
    result = jnp.where(is_mid, mid_field, jnp.where(is_leaf, leaf_up, zero_envs))
    return result[None, None]


def solution(mesh):
    return jax.shard_map(
        local,
        mesh=mesh,
        in_specs=(
            P("sub", "node", None, None, None),
            P("sub", "node", None, None, None, None),
            P("sub", "node", None, None, None),
            P("sub", None),
            P("sub", None),
        ),
        out_specs=P("sub", "node", None, None, None),
        check_vma=False,
    )
```

```python
import functools

import jax
import jax.numpy as jnp
from jax import lax
from jax.experimental import pallas as pl
from jax.experimental.pallas import tpu as pltpu
from jax.sharding import PartitionSpec as P

TERMS = 1
MESH = pl.DeviceIdType.MESH


def from_behind(block, axis, distance):
    devices = range(lax.axis_size(axis))
    route = [((i - distance) % len(devices), i) for i in devices]
    return lax.ppermute(block, axis, route)


def gather_kernel(n, groups, shift, pieces, *refs):
    if shift:
        x_ref, roles_ref, out_ref, roles_out, send_sem, recv_sem, own_sem, sub_sem = refs
    else:
        x_ref, out_ref, send_sem, recv_sem, own_sem, sub_sem = refs
    me = lax.axis_index("node")
    group = lax.axis_index("sub")
    right = lax.rem(me + 1, n)
    left = lax.rem(me + n - 1, n)
    barrier = pltpu.get_barrier_semaphore()
    peers = [(group, left), (group, right)]
    if shift:
        peers += [(lax.rem(group + shift + groups, groups), me), (lax.rem(group - shift + groups, groups), me)]
    for peer in peers:
        pl.semaphore_signal(barrier, inc=1, device_id=peer, device_id_type=MESH)
    pl.semaphore_wait(barrier, len(peers))
    if shift:
        own = pltpu.make_async_copy(x_ref.at[0], out_ref.at[me, 0], own_sem)
        own.start()
        across = pltpu.make_async_remote_copy(
            src_ref=x_ref.at[1],
            dst_ref=out_ref.at[me, 1],
            send_sem=sub_sem.at[0],
            recv_sem=sub_sem.at[1],
            device_id=peers[2],
            device_id_type=MESH,
        )
        across.start()
        roles_across = pltpu.make_async_remote_copy(
            src_ref=roles_ref,
            dst_ref=roles_out,
            send_sem=sub_sem.at[2],
            recv_sem=sub_sem.at[3],
            device_id=peers[2],
            device_id_type=MESH,
        )
        roles_across.start()
        own.wait()
        across.wait_recv()
        first_src = out_ref.at[me]
    else:
        own = pltpu.make_async_copy(x_ref, out_ref.at[me], own_sem)
        own.start()
        first_src = x_ref
    ways = ((0, 1, right, n // 2), (1, -1, left, n - 1 - n // 2))
    rows = x_ref.shape[-2] // pieces
    lead = (slice(None),) * (len(x_ref.shape) - 2)

    def hop(way, target, step, origin, piece):
        part = lead + (pl.ds(piece * rows, rows), slice(None))
        return pltpu.make_async_remote_copy(
            src_ref=(first_src if step == 0 else out_ref.at[origin]).at[part],
            dst_ref=out_ref.at[origin].at[part],
            send_sem=send_sem.at[way, step, piece],
            recv_sem=recv_sem.at[way, step, piece],
            device_id=(group, target),
            device_id_type=MESH,
        )

    sent = []
    for step in range(n // 2):
        for way, sign, target, steps in ways:
            if step >= steps:
                continue
            origin = lax.rem(me - sign * step + 2 * n, n)
            for piece in range(pieces):
                if step > 0:
                    hop(way, target, step - 1, origin, piece).wait_recv()
                copy = hop(way, target, step, origin, piece)
                copy.start()
                sent.append(copy)
    for way, sign, target, steps in ways:
        origin = lax.rem(me - sign * steps + 2 * n, n)
        for piece in range(pieces):
            hop(way, target, steps - 1, origin, piece).wait_recv()
    for copy in sent:
        copy.wait_send()
    if shift:
        across.wait_send()
        roles_across.wait_send()
        roles_across.wait_recv()
    else:
        own.wait()


def node_gather(block, collective_id, shift=0, roles=None, pieces=2):
    n = lax.axis_size("node")
    groups = lax.axis_size("sub")
    vmem = pl.BlockSpec(memory_space=pltpu.VMEM)
    gathered = jax.ShapeDtypeStruct((n,) + block.shape, block.dtype)
    operands = (block,) if roles is None else (block, roles)
    return pl.pallas_call(
        functools.partial(gather_kernel, n, groups, shift, pieces),
        out_shape=gathered if roles is None else (gathered, jax.ShapeDtypeStruct(roles.shape, roles.dtype)),
        in_specs=[vmem] * len(operands),
        out_specs=vmem if roles is None else (vmem, vmem),
        scratch_shapes=[
            pltpu.SemaphoreType.DMA((2, n // 2, pieces)),
            pltpu.SemaphoreType.DMA((2, n // 2, pieces)),
            pltpu.SemaphoreType.DMA,
            pltpu.SemaphoreType.DMA((4,)),
        ],
        compiler_params=pltpu.CompilerParams(collective_id=collective_id, has_side_effects=True),
    )(*operands)


def node_up(tensor_here, left_env, right_env):
    first = jnp.einsum(
        "xa,abp->xbp", left_env, tensor_here, preferred_element_type=jnp.float32
    ).astype(jnp.bfloat16)
    second = jnp.einsum("yb,xbp->xyp", right_env, first, preferred_element_type=jnp.float32).astype(
        jnp.bfloat16
    )
    return jnp.einsum(
        "xyq,xyp->qp", tensor_here, second, preferred_element_type=jnp.float32
    ).astype(jnp.bfloat16)


def node_down(tensor_here, left_env, right_env, upper_here):
    weighted = jnp.einsum(
        "qp,abp->abq", upper_here, tensor_here, preferred_element_type=jnp.float32
    ).astype(jnp.bfloat16)
    right_part = jnp.einsum(
        "xyq,yb->xbq", tensor_here, right_env, preferred_element_type=jnp.float32
    ).astype(jnp.bfloat16)
    left_part = jnp.einsum(
        "xyq,xa->ayq", tensor_here, left_env, preferred_element_type=jnp.float32
    ).astype(jnp.bfloat16)
    first_child = jnp.einsum(
        "xbq,abq->xa", right_part, weighted, preferred_element_type=jnp.float32
    ).astype(jnp.bfloat16)
    second_child = jnp.einsum(
        "ayq,abq->yb", left_part, weighted, preferred_element_type=jnp.float32
    ).astype(jnp.bfloat16)
    return (first_child, second_child)


def placements(group_roles):
    group_size = group_roles.shape[0]
    spots = jnp.arange(group_size, dtype=jnp.int32)
    return jnp.sum(jnp.where(group_roles[None, :] == spots[:, None], spots[None, :], 0), axis=1)


def local(node_tensor, outer_env, upper_env, role_map, child_slots):
    tensor_here = node_tensor[0, 0]
    outer_envs = outer_env[0, 0]
    upper_envs = upper_env[0, 0]
    group_roles = role_map[0]
    child_links = child_slots[0]
    group_size = lax.axis_size("node")
    top_count = group_size // 4
    mid_count = 2 * top_count
    bond_size = tensor_here.shape[0]
    role_spot = placements(group_roles)
    position = lax.axis_index("node")
    my_role = group_roles[position]
    is_top = my_role < top_count
    is_mid = jnp.logical_and(my_role >= top_count, my_role < top_count + mid_count)
    is_leaf = my_role >= top_count + mid_count
    zero_envs = jnp.zeros((TERMS, bond_size, bond_size), jnp.bfloat16)

    def leaf_work():
        return jnp.stack([node_up(tensor_here, outer_envs[0, 0], outer_envs[1, 0])])

    leaf_up = lax.cond(is_leaf, leaf_work, lambda: zero_envs)
    leaf_spots = role_spot[top_count + mid_count :]
    every_leaf = node_gather(leaf_up, 0)
    leaf_table = jnp.take(every_leaf, leaf_spots, axis=0)
    mid_index = jnp.clip(my_role - top_count, 0, mid_count - 1)

    def mid_work():
        child_envs = []
        for branch in range(2):
            slot_link = child_links[2 * mid_index + branch]
            leaf_pick = leaf_table[jnp.maximum(slot_link, 0)]
            child_envs.append(jnp.where(slot_link >= 0, leaf_pick, outer_envs[branch]))
        return jnp.stack([node_up(tensor_here, child_envs[0][0], child_envs[1][0])])

    mid_up = lax.cond(is_mid, mid_work, lambda: zero_envs)
    every_mid, next_roles = node_gather(jnp.stack([mid_up, mid_up]), 1, -1, role_map)
    top_index = jnp.clip(my_role, 0, top_count - 1)
    mid_table = jnp.take(every_mid[:, 0], role_spot[top_count : top_count + mid_count], axis=0)
    next_spots = placements(next_roles[0])[top_count + top_count : top_count + mid_count]
    right_envs = jnp.take(every_mid[:, 1], next_spots, axis=0)[top_index]

    def top_work():
        left_env = mid_table[top_index]
        results = [node_down(tensor_here, left_env[0], right_envs[0], upper_envs[0])]
        return jnp.stack([jnp.stack([r[0] for r in results]), jnp.stack([r[1] for r in results])])

    top_down = lax.cond(
        is_top, top_work, lambda: jnp.zeros((2, TERMS, bond_size, bond_size), jnp.bfloat16)
    )
    every_top, prev_roles = node_gather(top_down, 2, 1, role_map)
    own_field = every_top[role_spot[jnp.clip(mid_index, 0, top_count - 1)], 0]
    other_field = every_top[placements(prev_roles[0])[jnp.clip(mid_index - top_count, 0, top_count - 1)], 1]
    mid_field = jnp.where(mid_index < top_count, own_field, other_field)
    result = jnp.where(is_mid, mid_field, jnp.where(is_leaf, leaf_up, zero_envs))
    return result[None, None]


def solution(mesh):
    return jax.shard_map(
        local,
        mesh=mesh,
        in_specs=(
            P("sub", "node", None, None, None),
            P("sub", "node", None, None, None, None),
            P("sub", "node", None, None, None),
            P("sub", None),
            P("sub", None),
        ),
        out_specs=P("sub", "node", None, None, None),
        check_vma=False,
    )
```

```python
import functools

import jax
import jax.numpy as jnp
from jax import lax
from jax.experimental import pallas as pl
from jax.experimental.pallas import tpu as pltpu
from jax.sharding import PartitionSpec as P

TERMS = 1
MESH = pl.DeviceIdType.MESH


def from_behind(block, axis, distance):
    devices = range(lax.axis_size(axis))
    route = [((i - distance) % len(devices), i) for i in devices]
    return lax.ppermute(block, axis, route)


def gather_kernel(n, groups, shift, pieces, with_roles, *refs):
    if with_roles:
        x_ref, roles_ref, out_ref, roles_out, send_sem, recv_sem, own_sem, sub_sem = refs
    else:
        x_ref, out_ref, send_sem, recv_sem, own_sem, sub_sem = refs
    me = lax.axis_index("node")
    group = lax.axis_index("sub")
    right = lax.rem(me + 1, n)
    left = lax.rem(me + n - 1, n)
    barrier = pltpu.get_barrier_semaphore()
    peers = [(group, left), (group, right)]
    if shift:
        peers += [(lax.rem(group + shift + groups, groups), me), (lax.rem(group - shift + groups, groups), me)]
    for peer in peers:
        pl.semaphore_signal(barrier, inc=1, device_id=peer, device_id_type=MESH)
    pl.semaphore_wait(barrier, len(peers))
    if shift:
        own = pltpu.make_async_copy(x_ref.at[0], out_ref.at[me, 0], own_sem)
        own.start()
        across = pltpu.make_async_remote_copy(
            src_ref=x_ref.at[1],
            dst_ref=out_ref.at[me, 1],
            send_sem=sub_sem.at[0],
            recv_sem=sub_sem.at[1],
            device_id=peers[2],
            device_id_type=MESH,
        )
        across.start()
        roles_across = [
            pltpu.make_async_remote_copy(
                src_ref=roles_ref,
                dst_ref=roles_out.at[side],
                send_sem=sub_sem.at[2 + 2 * side],
                recv_sem=sub_sem.at[3 + 2 * side],
                device_id=peers[2 + side],
                device_id_type=MESH,
            )
            for side in range(2 if with_roles else 0)
        ]
        for copy in roles_across:
            copy.start()
        own.wait()
        across.wait_recv()
        first_src = out_ref.at[me]
    else:
        own = pltpu.make_async_copy(x_ref, out_ref.at[me], own_sem)
        own.start()
        first_src = x_ref
    ways = ((0, 1, right, n // 2), (1, -1, left, n - 1 - n // 2))
    rows = x_ref.shape[-2] // pieces
    lead = (slice(None),) * (len(x_ref.shape) - 2)

    def hop(way, target, step, origin, piece):
        part = lead + (pl.ds(piece * rows, rows), slice(None))
        return pltpu.make_async_remote_copy(
            src_ref=(first_src if step == 0 else out_ref.at[origin]).at[part],
            dst_ref=out_ref.at[origin].at[part],
            send_sem=send_sem.at[way, step, piece],
            recv_sem=recv_sem.at[way, step, piece],
            device_id=(group, target),
            device_id_type=MESH,
        )

    sent = []
    for step in range(n // 2):
        for way, sign, target, steps in ways:
            if step >= steps:
                continue
            origin = lax.rem(me - sign * step + 2 * n, n)
            for piece in range(pieces):
                if step > 0:
                    hop(way, target, step - 1, origin, piece).wait_recv()
                copy = hop(way, target, step, origin, piece)
                copy.start()
                sent.append(copy)
    for way, sign, target, steps in ways:
        origin = lax.rem(me - sign * steps + 2 * n, n)
        for piece in range(pieces):
            hop(way, target, steps - 1, origin, piece).wait_recv()
    for copy in sent:
        copy.wait_send()
    if shift:
        across.wait_send()
        for copy in roles_across:
            copy.wait_send()
            copy.wait_recv()
    else:
        own.wait()


def node_gather(block, collective_id, shift=0, roles=None, pieces=2):
    n = lax.axis_size("node")
    groups = lax.axis_size("sub")
    vmem = pl.BlockSpec(memory_space=pltpu.VMEM)
    gathered = jax.ShapeDtypeStruct((n,) + block.shape, block.dtype)
    operands = (block,) if roles is None else (block, roles)
    return pl.pallas_call(
        functools.partial(gather_kernel, n, groups, shift, pieces, roles is not None),
        out_shape=gathered if roles is None else (gathered, jax.ShapeDtypeStruct((2,) + roles.shape, roles.dtype)),
        in_specs=[vmem] * len(operands),
        out_specs=vmem if roles is None else (vmem, vmem),
        scratch_shapes=[
            pltpu.SemaphoreType.DMA((2, n // 2, pieces)),
            pltpu.SemaphoreType.DMA((2, n // 2, pieces)),
            pltpu.SemaphoreType.DMA,
            pltpu.SemaphoreType.DMA((6,)),
        ],
        compiler_params=pltpu.CompilerParams(collective_id=collective_id, has_side_effects=True),
    )(*operands)


def node_up(tensor_here, left_env, right_env):
    first = jnp.einsum(
        "xa,abp->xbp", left_env, tensor_here, preferred_element_type=jnp.float32
    ).astype(jnp.bfloat16)
    second = jnp.einsum("yb,xbp->xyp", right_env, first, preferred_element_type=jnp.float32).astype(
        jnp.bfloat16
    )
    return jnp.einsum(
        "xyq,xyp->qp", tensor_here, second, preferred_element_type=jnp.float32
    ).astype(jnp.bfloat16)


def node_down(tensor_here, left_env, right_env, upper_here):
    weighted = jnp.einsum(
        "qp,abp->abq", upper_here, tensor_here, preferred_element_type=jnp.float32
    ).astype(jnp.bfloat16)
    right_part = jnp.einsum(
        "xyq,yb->xbq", tensor_here, right_env, preferred_element_type=jnp.float32
    ).astype(jnp.bfloat16)
    left_part = jnp.einsum(
        "xyq,xa->ayq", tensor_here, left_env, preferred_element_type=jnp.float32
    ).astype(jnp.bfloat16)
    first_child = jnp.einsum(
        "xbq,abq->xa", right_part, weighted, preferred_element_type=jnp.float32
    ).astype(jnp.bfloat16)
    second_child = jnp.einsum(
        "ayq,abq->yb", left_part, weighted, preferred_element_type=jnp.float32
    ).astype(jnp.bfloat16)
    return (first_child, second_child)


def placements(group_roles):
    group_size = group_roles.shape[0]
    spots = jnp.arange(group_size, dtype=jnp.int32)
    return jnp.sum(jnp.where(group_roles[None, :] == spots[:, None], spots[None, :], 0), axis=1)


def local(node_tensor, outer_env, upper_env, role_map, child_slots):
    tensor_here = node_tensor[0, 0]
    outer_envs = outer_env[0, 0]
    upper_envs = upper_env[0, 0]
    group_roles = role_map[0]
    child_links = child_slots[0]
    group_size = lax.axis_size("node")
    top_count = group_size // 4
    mid_count = 2 * top_count
    bond_size = tensor_here.shape[0]
    role_spot = placements(group_roles)
    position = lax.axis_index("node")
    my_role = group_roles[position]
    is_top = my_role < top_count
    is_mid = jnp.logical_and(my_role >= top_count, my_role < top_count + mid_count)
    is_leaf = my_role >= top_count + mid_count
    zero_envs = jnp.zeros((TERMS, bond_size, bond_size), jnp.bfloat16)

    def leaf_work():
        return jnp.stack([node_up(tensor_here, outer_envs[0, 0], outer_envs[1, 0])])

    leaf_up = lax.cond(is_leaf, leaf_work, lambda: zero_envs)
    leaf_spots = role_spot[top_count + mid_count :]
    every_leaf = node_gather(leaf_up, 0)
    leaf_table = jnp.take(every_leaf, leaf_spots, axis=0)
    mid_index = jnp.clip(my_role - top_count, 0, mid_count - 1)

    def mid_work():
        child_envs = []
        for branch in range(2):
            slot_link = child_links[2 * mid_index + branch]
            leaf_pick = leaf_table[jnp.maximum(slot_link, 0)]
            child_envs.append(jnp.where(slot_link >= 0, leaf_pick, outer_envs[branch]))
        return jnp.stack([node_up(tensor_here, child_envs[0][0], child_envs[1][0])])

    mid_up = lax.cond(is_mid, mid_work, lambda: zero_envs)
    every_mid, near_roles = node_gather(jnp.stack([mid_up, mid_up]), 1, -1, role_map)
    next_roles = near_roles[0]
    prev_roles = near_roles[1]
    top_index = jnp.clip(my_role, 0, top_count - 1)
    mid_table = jnp.take(every_mid[:, 0], role_spot[top_count : top_count + mid_count], axis=0)
    next_spots = placements(next_roles[0])[top_count + top_count : top_count + mid_count]
    right_envs = jnp.take(every_mid[:, 1], next_spots, axis=0)[top_index]

    def top_work():
        left_env = mid_table[top_index]
        results = [node_down(tensor_here, left_env[0], right_envs[0], upper_envs[0])]
        return jnp.stack([jnp.stack([r[0] for r in results]), jnp.stack([r[1] for r in results])])

    top_down = lax.cond(
        is_top, top_work, lambda: jnp.zeros((2, TERMS, bond_size, bond_size), jnp.bfloat16)
    )
    every_top = node_gather(top_down, 2, 1)
    own_field = every_top[role_spot[jnp.clip(mid_index, 0, top_count - 1)], 0]
    other_field = every_top[placements(prev_roles[0])[jnp.clip(mid_index - top_count, 0, top_count - 1)], 1]
    mid_field = jnp.where(mid_index < top_count, own_field, other_field)
    result = jnp.where(is_mid, mid_field, jnp.where(is_leaf, leaf_up, zero_envs))
    return result[None, None]


def solution(mesh):
    return jax.shard_map(
        local,
        mesh=mesh,
        in_specs=(
            P("sub", "node", None, None, None),
            P("sub", "node", None, None, None, None),
            P("sub", "node", None, None, None),
            P("sub", None),
            P("sub", None),
        ),
        out_specs=P("sub", "node", None, None, None),
        check_vma=False,
    )
```

```python
import functools

import jax
import jax.numpy as jnp
from jax import lax
from jax.experimental import pallas as pl
from jax.experimental.pallas import tpu as pltpu
from jax.sharding import PartitionSpec as P

TERMS = 1
MESH = pl.DeviceIdType.MESH


def from_behind(block, axis, distance):
    devices = range(lax.axis_size(axis))
    route = [((i - distance) % len(devices), i) for i in devices]
    return lax.ppermute(block, axis, route)


def gather_kernel(n, groups, shift, pieces, with_roles, *refs):
    if with_roles:
        x_ref, roles_ref, out_ref, roles_out, send_sem, recv_sem, own_sem, sub_sem = refs
    else:
        x_ref, out_ref, send_sem, recv_sem, own_sem, sub_sem = refs
    me = lax.axis_index("node")
    group = lax.axis_index("sub")
    right = lax.rem(me + 1, n)
    left = lax.rem(me + n - 1, n)
    barrier = pltpu.get_barrier_semaphore()
    peers = [(group, left), (group, right)]
    if shift:
        peers += [(lax.rem(group + shift + groups, groups), me), (lax.rem(group - shift + groups, groups), me)]
    for peer in peers:
        pl.semaphore_signal(barrier, inc=1, device_id=peer, device_id_type=MESH)
    pl.semaphore_wait(barrier, len(peers))
    if shift:
        own = pltpu.make_async_copy(x_ref.at[0], out_ref.at[me, 0], own_sem)
        own.start()
        across = pltpu.make_async_remote_copy(
            src_ref=x_ref.at[1],
            dst_ref=out_ref.at[me, 1],
            send_sem=sub_sem.at[0],
            recv_sem=sub_sem.at[1],
            device_id=peers[2],
            device_id_type=MESH,
        )
        across.start()
        roles_across = [
            pltpu.make_async_remote_copy(
                src_ref=roles_ref,
                dst_ref=roles_out.at[side],
                send_sem=sub_sem.at[2 + 2 * side],
                recv_sem=sub_sem.at[3 + 2 * side],
                device_id=peers[2 + side],
                device_id_type=MESH,
            )
            for side in range(2 if with_roles else 0)
        ]
        for copy in roles_across:
            copy.start()
        own.wait()
        across.wait_recv()
        first_src = out_ref.at[me]
    else:
        own = pltpu.make_async_copy(x_ref, out_ref.at[me], own_sem)
        own.start()
        first_src = x_ref
    ways = ((0, 1, right, n // 2), (1, -1, left, n - 1 - n // 2))
    rows = x_ref.shape[-2] // pieces
    lead = (slice(None),) * (len(x_ref.shape) - 2)

    def hop(way, target, step, origin, piece):
        part = lead + (pl.ds(piece * rows, rows), slice(None))
        return pltpu.make_async_remote_copy(
            src_ref=(first_src if step == 0 else out_ref.at[origin]).at[part],
            dst_ref=out_ref.at[origin].at[part],
            send_sem=send_sem.at[way, step, piece],
            recv_sem=recv_sem.at[way, step, piece],
            device_id=(group, target),
            device_id_type=MESH,
        )

    sent = []
    for step in range(n // 2):
        for way, sign, target, steps in ways:
            if step >= steps:
                continue
            origin = lax.rem(me - sign * step + 2 * n, n)
            for piece in range(pieces):
                if step > 0:
                    hop(way, target, step - 1, origin, piece).wait_recv()
                copy = hop(way, target, step, origin, piece)
                copy.start()
                sent.append(copy)
    for way, sign, target, steps in ways:
        origin = lax.rem(me - sign * steps + 2 * n, n)
        for piece in range(pieces):
            hop(way, target, steps - 1, origin, piece).wait_recv()
    for copy in sent:
        copy.wait_send()
    if shift:
        across.wait_send()
        for copy in roles_across:
            copy.wait_send()
            copy.wait_recv()
    else:
        own.wait()


def node_gather(block, collective_id, shift=0, roles=None, pieces=2):
    n = lax.axis_size("node")
    groups = lax.axis_size("sub")
    vmem = pl.BlockSpec(memory_space=pltpu.VMEM)
    gathered = jax.ShapeDtypeStruct((n,) + block.shape, block.dtype)
    operands = (block,) if roles is None else (block, roles)
    return pl.pallas_call(
        functools.partial(gather_kernel, n, groups, shift, pieces, roles is not None),
        out_shape=gathered if roles is None else (gathered, jax.ShapeDtypeStruct((2,) + roles.shape, roles.dtype)),
        in_specs=[vmem] * len(operands),
        out_specs=vmem if roles is None else (vmem, vmem),
        scratch_shapes=[
            pltpu.SemaphoreType.DMA((2, n // 2, pieces)),
            pltpu.SemaphoreType.DMA((2, n // 2, pieces)),
            pltpu.SemaphoreType.DMA,
            pltpu.SemaphoreType.DMA((6,)),
        ],
        compiler_params=pltpu.CompilerParams(collective_id=collective_id, has_side_effects=True),
    )(*operands)


def node_up(tensor_here, left_env, right_env):
    first = jnp.einsum(
        "xa,abp->xbp", left_env, tensor_here, preferred_element_type=jnp.float32
    ).astype(jnp.bfloat16)
    second = jnp.einsum("yb,xbp->xyp", right_env, first, preferred_element_type=jnp.float32).astype(
        jnp.bfloat16
    )
    return jnp.einsum(
        "xyq,xyp->qp", tensor_here, second, preferred_element_type=jnp.float32
    ).astype(jnp.bfloat16)


def node_down(tensor_here, left_env, right_env, upper_here):
    weighted = jnp.einsum(
        "qp,abp->abq", upper_here, tensor_here, preferred_element_type=jnp.float32
    ).astype(jnp.bfloat16)
    right_part = jnp.einsum(
        "xyq,yb->xbq", tensor_here, right_env, preferred_element_type=jnp.float32
    ).astype(jnp.bfloat16)
    left_part = jnp.einsum(
        "xyq,xa->ayq", tensor_here, left_env, preferred_element_type=jnp.float32
    ).astype(jnp.bfloat16)
    first_child = jnp.einsum(
        "xbq,abq->xa", right_part, weighted, preferred_element_type=jnp.float32
    ).astype(jnp.bfloat16)
    second_child = jnp.einsum(
        "ayq,abq->yb", left_part, weighted, preferred_element_type=jnp.float32
    ).astype(jnp.bfloat16)
    return (first_child, second_child)


def placements(group_roles):
    group_size = group_roles.shape[0]
    spots = jnp.arange(group_size, dtype=jnp.int32)
    return jnp.sum(jnp.where(group_roles[None, :] == spots[:, None], spots[None, :], 0), axis=1)


def pick(table, hit):
    hit = hit.reshape(hit.shape + (1,) * (table.ndim - 1))
    return jnp.sum(jnp.where(hit, table.astype(jnp.float32), 0.0), axis=0).astype(table.dtype)


def local(node_tensor, outer_env, upper_env, role_map, child_slots):
    tensor_here = node_tensor[0, 0]
    outer_envs = outer_env[0, 0]
    upper_envs = upper_env[0, 0]
    group_roles = role_map[0]
    child_links = child_slots[0]
    group_size = lax.axis_size("node")
    top_count = group_size // 4
    mid_count = 2 * top_count
    bond_size = tensor_here.shape[0]
    role_spot = placements(group_roles)
    position = lax.axis_index("node")
    my_role = group_roles[position]
    is_top = my_role < top_count
    is_mid = jnp.logical_and(my_role >= top_count, my_role < top_count + mid_count)
    is_leaf = my_role >= top_count + mid_count
    zero_envs = jnp.zeros((TERMS, bond_size, bond_size), jnp.bfloat16)

    def leaf_work():
        return jnp.stack([node_up(tensor_here, outer_envs[0, 0], outer_envs[1, 0])])

    leaf_up = lax.cond(is_leaf, leaf_work, lambda: zero_envs)
    leaf_spots = role_spot[top_count + mid_count :]
    every_leaf = node_gather(leaf_up, 0)
    leaf_table = jnp.take(every_leaf, leaf_spots, axis=0)
    mid_index = jnp.clip(my_role - top_count, 0, mid_count - 1)

    def mid_work():
        child_envs = []
        for branch in range(2):
            slot_link = child_links[2 * mid_index + branch]
            leaf_pick = leaf_table[jnp.maximum(slot_link, 0)]
            child_envs.append(jnp.where(slot_link >= 0, leaf_pick, outer_envs[branch]))
        return jnp.stack([node_up(tensor_here, child_envs[0][0], child_envs[1][0])])

    mid_up = lax.cond(is_mid, mid_work, lambda: zero_envs)
    every_mid, near_roles = node_gather(jnp.stack([mid_up, mid_up]), 1, -1, role_map)
    next_roles = near_roles[0]
    prev_roles = near_roles[1]
    top_index = jnp.clip(my_role, 0, top_count - 1)
    left_envs = pick(every_mid[:, 0], group_roles == top_count + top_index)
    right_envs = pick(every_mid[:, 1], next_roles[0] == top_count + top_count + top_index)

    def top_work():
        results = [node_down(tensor_here, left_envs[t], right_envs[t], upper_envs[t]) for t in range(TERMS)]
        return jnp.stack([jnp.stack([r[0] for r in results]), jnp.stack([r[1] for r in results])])

    top_down = lax.cond(
        is_top, top_work, lambda: jnp.zeros((2, TERMS, bond_size, bond_size), jnp.bfloat16)
    )
    every_top = node_gather(top_down, 2, 1)
    own_field = pick(every_top[:, 0], group_roles == jnp.clip(mid_index, 0, top_count - 1))
    other_field = pick(every_top[:, 1], prev_roles[0] == jnp.clip(mid_index - top_count, 0, top_count - 1))
    mid_field = jnp.where(mid_index < top_count, own_field, other_field)
    result = jnp.where(is_mid, mid_field, jnp.where(is_leaf, leaf_up, zero_envs))
    return result[None, None]


def solution(mesh):
    return jax.shard_map(
        local,
        mesh=mesh,
        in_specs=(
            P("sub", "node", None, None, None),
            P("sub", "node", None, None, None, None),
            P("sub", "node", None, None, None),
            P("sub", None),
            P("sub", None),
        ),
        out_specs=P("sub", "node", None, None, None),
        check_vma=False,
    )
```

```python
import functools

import jax
import jax.numpy as jnp
from jax import lax
from jax.experimental import pallas as pl
from jax.experimental.pallas import tpu as pltpu
from jax.sharding import PartitionSpec as P

TERMS = 1
MESH = pl.DeviceIdType.MESH


def from_behind(block, axis, distance):
    devices = range(lax.axis_size(axis))
    route = [((i - distance) % len(devices), i) for i in devices]
    return lax.ppermute(block, axis, route)


def gather_kernel(n, groups, shift, pieces, with_roles, *refs):
    if with_roles:
        x_ref, roles_ref, out_ref, roles_out, send_sem, recv_sem, own_sem, sub_sem = refs
    else:
        x_ref, out_ref, send_sem, recv_sem, own_sem, sub_sem = refs
    me = lax.axis_index("node")
    group = lax.axis_index("sub")
    right = lax.rem(me + 1, n)
    left = lax.rem(me + n - 1, n)
    barrier = pltpu.get_barrier_semaphore()
    peers = [(group, left), (group, right)]
    if shift:
        peers += [(lax.rem(group + shift + groups, groups), me), (lax.rem(group - shift + groups, groups), me)]
    for peer in peers:
        pl.semaphore_signal(barrier, inc=1, device_id=peer, device_id_type=MESH)
    pl.semaphore_wait(barrier, len(peers))
    if shift:
        own = pltpu.make_async_copy(x_ref.at[0], out_ref.at[me, 0], own_sem)
        own.start()
        across = pltpu.make_async_remote_copy(
            src_ref=x_ref.at[1],
            dst_ref=out_ref.at[me, 1],
            send_sem=sub_sem.at[0],
            recv_sem=sub_sem.at[1],
            device_id=peers[2],
            device_id_type=MESH,
        )
        across.start()
        roles_across = [
            pltpu.make_async_remote_copy(
                src_ref=roles_ref,
                dst_ref=roles_out.at[side],
                send_sem=sub_sem.at[2 + 2 * side],
                recv_sem=sub_sem.at[3 + 2 * side],
                device_id=peers[2 + side],
                device_id_type=MESH,
            )
            for side in range(2 if with_roles else 0)
        ]
        for copy in roles_across:
            copy.start()
        own.wait()
        across.wait_recv()
        first_src = out_ref.at[me]
    else:
        own = pltpu.make_async_copy(x_ref, out_ref.at[me], own_sem)
        own.start()
        first_src = x_ref
    ways = ((0, 1, right, n // 2), (1, -1, left, n - 1 - n // 2))
    rows = x_ref.shape[-2] // pieces
    lead = (slice(None),) * (len(x_ref.shape) - 2)

    def hop(way, target, step, origin, piece):
        part = lead + (pl.ds(piece * rows, rows), slice(None))
        return pltpu.make_async_remote_copy(
            src_ref=(first_src if step == 0 else out_ref.at[origin]).at[part],
            dst_ref=out_ref.at[origin].at[part],
            send_sem=send_sem.at[way, step, piece],
            recv_sem=recv_sem.at[way, step, piece],
            device_id=(group, target),
            device_id_type=MESH,
        )

    sent = []
    for step in range(n // 2):
        for way, sign, target, steps in ways:
            if step >= steps:
                continue
            origin = lax.rem(me - sign * step + 2 * n, n)
            for piece in range(pieces):
                if step > 0:
                    hop(way, target, step - 1, origin, piece).wait_recv()
                copy = hop(way, target, step, origin, piece)
                copy.start()
                sent.append(copy)
    for way, sign, target, steps in ways:
        origin = lax.rem(me - sign * steps + 2 * n, n)
        for piece in range(pieces):
            hop(way, target, steps - 1, origin, piece).wait_recv()
    for copy in sent:
        copy.wait_send()
    if shift:
        across.wait_send()
        for copy in roles_across:
            copy.wait_send()
            copy.wait_recv()
    else:
        own.wait()


def node_gather(block, collective_id, shift=0, roles=None, pieces=4):
    n = lax.axis_size("node")
    groups = lax.axis_size("sub")
    vmem = pl.BlockSpec(memory_space=pltpu.VMEM)
    gathered = jax.ShapeDtypeStruct((n,) + block.shape, block.dtype)
    operands = (block,) if roles is None else (block, roles)
    return pl.pallas_call(
        functools.partial(gather_kernel, n, groups, shift, pieces, roles is not None),
        out_shape=gathered if roles is None else (gathered, jax.ShapeDtypeStruct((2,) + roles.shape, roles.dtype)),
        in_specs=[vmem] * len(operands),
        out_specs=vmem if roles is None else (vmem, vmem),
        scratch_shapes=[
            pltpu.SemaphoreType.DMA((2, n // 2, pieces)),
            pltpu.SemaphoreType.DMA((2, n // 2, pieces)),
            pltpu.SemaphoreType.DMA,
            pltpu.SemaphoreType.DMA((6,)),
        ],
        compiler_params=pltpu.CompilerParams(collective_id=collective_id, has_side_effects=True),
    )(*operands)


def node_up(tensor_here, left_env, right_env):
    first = jnp.einsum(
        "xa,abp->xbp", left_env, tensor_here, preferred_element_type=jnp.float32
    ).astype(jnp.bfloat16)
    second = jnp.einsum("yb,xbp->xyp", right_env, first, preferred_element_type=jnp.float32).astype(
        jnp.bfloat16
    )
    return jnp.einsum(
        "xyq,xyp->qp", tensor_here, second, preferred_element_type=jnp.float32
    ).astype(jnp.bfloat16)


def node_down(tensor_here, left_env, right_env, upper_here):
    weighted = jnp.einsum(
        "qp,abp->abq", upper_here, tensor_here, preferred_element_type=jnp.float32
    ).astype(jnp.bfloat16)
    right_part = jnp.einsum(
        "xyq,yb->xbq", tensor_here, right_env, preferred_element_type=jnp.float32
    ).astype(jnp.bfloat16)
    left_part = jnp.einsum(
        "xyq,xa->ayq", tensor_here, left_env, preferred_element_type=jnp.float32
    ).astype(jnp.bfloat16)
    first_child = jnp.einsum(
        "xbq,abq->xa", right_part, weighted, preferred_element_type=jnp.float32
    ).astype(jnp.bfloat16)
    second_child = jnp.einsum(
        "ayq,abq->yb", left_part, weighted, preferred_element_type=jnp.float32
    ).astype(jnp.bfloat16)
    return (first_child, second_child)


def placements(group_roles):
    group_size = group_roles.shape[0]
    spots = jnp.arange(group_size, dtype=jnp.int32)
    return jnp.sum(jnp.where(group_roles[None, :] == spots[:, None], spots[None, :], 0), axis=1)


def pick(table, hit):
    hit = hit.reshape(hit.shape + (1,) * (table.ndim - 1))
    return jnp.sum(jnp.where(hit, table.astype(jnp.float32), 0.0), axis=0).astype(table.dtype)


def local(node_tensor, outer_env, upper_env, role_map, child_slots):
    tensor_here = node_tensor[0, 0]
    outer_envs = outer_env[0, 0]
    upper_envs = upper_env[0, 0]
    group_roles = role_map[0]
    child_links = child_slots[0]
    group_size = lax.axis_size("node")
    top_count = group_size // 4
    mid_count = 2 * top_count
    bond_size = tensor_here.shape[0]
    role_spot = placements(group_roles)
    position = lax.axis_index("node")
    my_role = group_roles[position]
    is_top = my_role < top_count
    is_mid = jnp.logical_and(my_role >= top_count, my_role < top_count + mid_count)
    is_leaf = my_role >= top_count + mid_count
    zero_envs = jnp.zeros((TERMS, bond_size, bond_size), jnp.bfloat16)

    def leaf_work():
        return jnp.stack([node_up(tensor_here, outer_envs[0, 0], outer_envs[1, 0])])

    leaf_up = lax.cond(is_leaf, leaf_work, lambda: zero_envs)
    every_leaf = node_gather(leaf_up, 0)
    mid_index = jnp.clip(my_role - top_count, 0, mid_count - 1)

    def mid_work():
        child_envs = []
        for branch in range(2):
            slot_link = child_links[2 * mid_index + branch]
            leaf_pick = pick(every_leaf, group_roles == top_count + mid_count + jnp.maximum(slot_link, 0))
            child_envs.append(jnp.where(slot_link >= 0, leaf_pick, outer_envs[branch]))
        return jnp.stack([node_up(tensor_here, child_envs[0][0], child_envs[1][0])])

    mid_up = lax.cond(is_mid, mid_work, lambda: zero_envs)
    every_mid, near_roles = node_gather(jnp.stack([mid_up, mid_up]), 1, -1, role_map)
    next_roles = near_roles[0]
    prev_roles = near_roles[1]
    top_index = jnp.clip(my_role, 0, top_count - 1)
    left_envs = pick(every_mid[:, 0], group_roles == top_count + top_index)
    right_envs = pick(every_mid[:, 1], next_roles[0] == top_count + top_count + top_index)

    def top_work():
        results = [node_down(tensor_here, left_envs[t], right_envs[t], upper_envs[t]) for t in range(TERMS)]
        return jnp.stack([jnp.stack([r[0] for r in results]), jnp.stack([r[1] for r in results])])

    top_down = lax.cond(
        is_top, top_work, lambda: jnp.zeros((2, TERMS, bond_size, bond_size), jnp.bfloat16)
    )
    every_top = node_gather(top_down, 2, 1)
    own_field = pick(every_top[:, 0], group_roles == jnp.clip(mid_index, 0, top_count - 1))
    other_field = pick(every_top[:, 1], prev_roles[0] == jnp.clip(mid_index - top_count, 0, top_count - 1))
    mid_field = jnp.where(mid_index < top_count, own_field, other_field)
    result = jnp.where(is_mid, mid_field, jnp.where(is_leaf, leaf_up, zero_envs))
    return result[None, None]


def solution(mesh):
    return jax.shard_map(
        local,
        mesh=mesh,
        in_specs=(
            P("sub", "node", None, None, None),
            P("sub", "node", None, None, None, None),
            P("sub", "node", None, None, None),
            P("sub", None),
            P("sub", None),
        ),
        out_specs=P("sub", "node", None, None, None),
        check_vma=False,
    )
```

```python
import functools

import jax
import jax.numpy as jnp
from jax import lax
from jax.experimental import pallas as pl
from jax.experimental.pallas import tpu as pltpu
from jax.sharding import PartitionSpec as P

TERMS = 1
MESH = pl.DeviceIdType.MESH


def from_behind(block, axis, distance):
    devices = range(lax.axis_size(axis))
    route = [((i - distance) % len(devices), i) for i in devices]
    return lax.ppermute(block, axis, route)


def gather_kernel(n, groups, shift, pieces, with_roles, *refs):
    if with_roles:
        x_ref, roles_ref, out_ref, roles_out, send_sem, recv_sem, own_sem, sub_sem = refs
    else:
        x_ref, out_ref, send_sem, recv_sem, own_sem, sub_sem = refs
    me = lax.axis_index("node")
    group = lax.axis_index("sub")
    right = lax.rem(me + 1, n)
    left = lax.rem(me + n - 1, n)
    barrier = pltpu.get_barrier_semaphore()
    peers = [(group, left), (group, right)]
    if shift:
        peers += [(lax.rem(group + shift + groups, groups), me), (lax.rem(group - shift + groups, groups), me)]
    for peer in peers:
        pl.semaphore_signal(barrier, inc=1, device_id=peer, device_id_type=MESH)
    pl.semaphore_wait(barrier, len(peers))
    if shift:
        own = pltpu.make_async_copy(x_ref.at[0], out_ref.at[me, 0], own_sem)
        own.start()
        across = pltpu.make_async_remote_copy(
            src_ref=x_ref.at[1],
            dst_ref=out_ref.at[me, 1],
            send_sem=sub_sem.at[0],
            recv_sem=sub_sem.at[1],
            device_id=peers[2],
            device_id_type=MESH,
        )
        across.start()
        roles_across = [
            pltpu.make_async_remote_copy(
                src_ref=roles_ref,
                dst_ref=roles_out.at[side],
                send_sem=sub_sem.at[2 + 2 * side],
                recv_sem=sub_sem.at[3 + 2 * side],
                device_id=peers[2 + side],
                device_id_type=MESH,
            )
            for side in range(2 if with_roles else 0)
        ]
        for copy in roles_across:
            copy.start()
        own.wait()
        across.wait_recv()
        first_src = out_ref.at[me]
    else:
        own = pltpu.make_async_copy(x_ref, out_ref.at[me], own_sem)
        own.start()
        first_src = x_ref
    ways = ((0, 1, right, n // 2), (1, -1, left, n - 1 - n // 2))
    rows = x_ref.shape[-2] // pieces
    lead = (slice(None),) * (len(x_ref.shape) - 2)

    def hop(way, target, step, origin, piece):
        part = lead + (pl.ds(piece * rows, rows), slice(None))
        return pltpu.make_async_remote_copy(
            src_ref=(first_src if step == 0 else out_ref.at[origin]).at[part],
            dst_ref=out_ref.at[origin].at[part],
            send_sem=send_sem.at[way, step, piece],
            recv_sem=recv_sem.at[way, step, piece],
            device_id=(group, target),
            device_id_type=MESH,
        )

    sent = []
    for step in range(n // 2):
        for way, sign, target, steps in ways:
            if step >= steps:
                continue
            origin = lax.rem(me - sign * step + 2 * n, n)
            for piece in range(pieces):
                if step > 0:
                    hop(way, target, step - 1, origin, piece).wait_recv()
                copy = hop(way, target, step, origin, piece)
                copy.start()
                sent.append(copy)
    for way, sign, target, steps in ways:
        origin = lax.rem(me - sign * steps + 2 * n, n)
        for piece in range(pieces):
            hop(way, target, steps - 1, origin, piece).wait_recv()
    for copy in sent:
        copy.wait_send()
    if shift:
        across.wait_send()
        for copy in roles_across:
            copy.wait_send()
            copy.wait_recv()
    else:
        own.wait()


def node_gather(block, collective_id, shift=0, roles=None, pieces=8):
    n = lax.axis_size("node")
    groups = lax.axis_size("sub")
    vmem = pl.BlockSpec(memory_space=pltpu.VMEM)
    gathered = jax.ShapeDtypeStruct((n,) + block.shape, block.dtype)
    operands = (block,) if roles is None else (block, roles)
    return pl.pallas_call(
        functools.partial(gather_kernel, n, groups, shift, pieces, roles is not None),
        out_shape=gathered if roles is None else (gathered, jax.ShapeDtypeStruct((2,) + roles.shape, roles.dtype)),
        in_specs=[vmem] * len(operands),
        out_specs=vmem if roles is None else (vmem, vmem),
        scratch_shapes=[
            pltpu.SemaphoreType.DMA((2, n // 2, pieces)),
            pltpu.SemaphoreType.DMA((2, n // 2, pieces)),
            pltpu.SemaphoreType.DMA,
            pltpu.SemaphoreType.DMA((6,)),
        ],
        compiler_params=pltpu.CompilerParams(collective_id=collective_id, has_side_effects=True),
    )(*operands)


def node_up(tensor_here, left_env, right_env):
    first = jnp.einsum(
        "xa,abp->xbp", left_env, tensor_here, preferred_element_type=jnp.float32
    ).astype(jnp.bfloat16)
    second = jnp.einsum("yb,xbp->xyp", right_env, first, preferred_element_type=jnp.float32).astype(
        jnp.bfloat16
    )
    return jnp.einsum(
        "xyq,xyp->qp", tensor_here, second, preferred_element_type=jnp.float32
    ).astype(jnp.bfloat16)


def node_down(tensor_here, left_env, right_env, upper_here):
    weighted = jnp.einsum(
        "qp,abp->abq", upper_here, tensor_here, preferred_element_type=jnp.float32
    ).astype(jnp.bfloat16)
    right_part = jnp.einsum(
        "xyq,yb->xbq", tensor_here, right_env, preferred_element_type=jnp.float32
    ).astype(jnp.bfloat16)
    left_part = jnp.einsum(
        "xyq,xa->ayq", tensor_here, left_env, preferred_element_type=jnp.float32
    ).astype(jnp.bfloat16)
    first_child = jnp.einsum(
        "xbq,abq->xa", right_part, weighted, preferred_element_type=jnp.float32
    ).astype(jnp.bfloat16)
    second_child = jnp.einsum(
        "ayq,abq->yb", left_part, weighted, preferred_element_type=jnp.float32
    ).astype(jnp.bfloat16)
    return (first_child, second_child)


def placements(group_roles):
    group_size = group_roles.shape[0]
    spots = jnp.arange(group_size, dtype=jnp.int32)
    return jnp.sum(jnp.where(group_roles[None, :] == spots[:, None], spots[None, :], 0), axis=1)


def pick(table, hit):
    hit = hit.reshape(hit.shape + (1,) * (table.ndim - 1))
    return jnp.sum(jnp.where(hit, table.astype(jnp.float32), 0.0), axis=0).astype(table.dtype)


def local(node_tensor, outer_env, upper_env, role_map, child_slots):
    tensor_here = node_tensor[0, 0]
    outer_envs = outer_env[0, 0]
    upper_envs = upper_env[0, 0]
    group_roles = role_map[0]
    child_links = child_slots[0]
    group_size = lax.axis_size("node")
    top_count = group_size // 4
    mid_count = 2 * top_count
    bond_size = tensor_here.shape[0]
    role_spot = placements(group_roles)
    position = lax.axis_index("node")
    my_role = group_roles[position]
    is_top = my_role < top_count
    is_mid = jnp.logical_and(my_role >= top_count, my_role < top_count + mid_count)
    is_leaf = my_role >= top_count + mid_count
    zero_envs = jnp.zeros((TERMS, bond_size, bond_size), jnp.bfloat16)

    def leaf_work():
        return jnp.stack([node_up(tensor_here, outer_envs[0, 0], outer_envs[1, 0])])

    leaf_up = lax.cond(is_leaf, leaf_work, lambda: zero_envs)
    every_leaf = node_gather(leaf_up, 0)
    mid_index = jnp.clip(my_role - top_count, 0, mid_count - 1)

    def mid_work():
        child_envs = []
        for branch in range(2):
            slot_link = child_links[2 * mid_index + branch]
            leaf_pick = pick(every_leaf, group_roles == top_count + mid_count + jnp.maximum(slot_link, 0))
            child_envs.append(jnp.where(slot_link >= 0, leaf_pick, outer_envs[branch]))
        return jnp.stack([node_up(tensor_here, child_envs[0][0], child_envs[1][0])])

    mid_up = lax.cond(is_mid, mid_work, lambda: zero_envs)
    every_mid, near_roles = node_gather(jnp.stack([mid_up, mid_up]), 1, -1, role_map)
    next_roles = near_roles[0]
    prev_roles = near_roles[1]
    top_index = jnp.clip(my_role, 0, top_count - 1)
    left_envs = pick(every_mid[:, 0], group_roles == top_count + top_index)
    right_envs = pick(every_mid[:, 1], next_roles[0] == top_count + top_count + top_index)

    def top_work():
        results = [node_down(tensor_here, left_envs[t], right_envs[t], upper_envs[t]) for t in range(TERMS)]
        return jnp.stack([jnp.stack([r[0] for r in results]), jnp.stack([r[1] for r in results])])

    top_down = lax.cond(
        is_top, top_work, lambda: jnp.zeros((2, TERMS, bond_size, bond_size), jnp.bfloat16)
    )
    every_top = node_gather(top_down, 2, 1)
    own_field = pick(every_top[:, 0], group_roles == jnp.clip(mid_index, 0, top_count - 1))
    other_field = pick(every_top[:, 1], prev_roles[0] == jnp.clip(mid_index - top_count, 0, top_count - 1))
    mid_field = jnp.where(mid_index < top_count, own_field, other_field)
    result = jnp.where(is_mid, mid_field, jnp.where(is_leaf, leaf_up, zero_envs))
    return result[None, None]


def solution(mesh):
    return jax.shard_map(
        local,
        mesh=mesh,
        in_specs=(
            P("sub", "node", None, None, None),
            P("sub", "node", None, None, None, None),
            P("sub", "node", None, None, None),
            P("sub", None),
            P("sub", None),
        ),
        out_specs=P("sub", "node", None, None, None),
        check_vma=False,
    )
```

```python
import functools

import jax
import jax.numpy as jnp
from jax import lax
from jax.experimental import pallas as pl
from jax.experimental.pallas import tpu as pltpu
from jax.sharding import PartitionSpec as P

TERMS = 1
MESH = pl.DeviceIdType.MESH


def from_behind(block, axis, distance):
    devices = range(lax.axis_size(axis))
    route = [((i - distance) % len(devices), i) for i in devices]
    return lax.ppermute(block, axis, route)


def gather_kernel(n, groups, shift, pieces, with_roles, *refs):
    if with_roles:
        x_ref, roles_ref, out_ref, roles_out, send_sem, recv_sem, own_sem, sub_sem = refs
    else:
        x_ref, out_ref, send_sem, recv_sem, own_sem, sub_sem = refs
    me = lax.axis_index("node")
    group = lax.axis_index("sub")
    right = lax.rem(me + 1, n)
    left = lax.rem(me + n - 1, n)
    barrier = pltpu.get_barrier_semaphore()
    peers = [(group, left), (group, right)]
    if shift:
        peers += [(lax.rem(group + shift + groups, groups), me), (lax.rem(group - shift + groups, groups), me)]
    for peer in peers:
        pl.semaphore_signal(barrier, inc=1, device_id=peer, device_id_type=MESH)
    pl.semaphore_wait(barrier, len(peers))
    if shift:
        own = pltpu.make_async_copy(x_ref.at[0], out_ref.at[me, 0], own_sem)
        own.start()
        across = pltpu.make_async_remote_copy(
            src_ref=x_ref.at[1],
            dst_ref=out_ref.at[me, 1],
            send_sem=sub_sem.at[0],
            recv_sem=sub_sem.at[1],
            device_id=peers[2],
            device_id_type=MESH,
        )
        across.start()
        roles_across = [
            pltpu.make_async_remote_copy(
                src_ref=roles_ref,
                dst_ref=roles_out.at[side],
                send_sem=sub_sem.at[2 + 2 * side],
                recv_sem=sub_sem.at[3 + 2 * side],
                device_id=peers[2 + side],
                device_id_type=MESH,
            )
            for side in range(2 if with_roles else 0)
        ]
        for copy in roles_across:
            copy.start()
    else:
        own = pltpu.make_async_copy(x_ref, out_ref.at[me], own_sem)
        own.start()
    ways = ((0, 1, right, n // 2), (1, -1, left, n - 1 - n // 2))
    rows = x_ref.shape[-2] // pieces
    slots = (0, 1) if shift else (None,)
    middle = (slice(None),) * (len(x_ref.shape) - 2 - (1 if shift else 0))
    parts = [(slot, chunk) for slot in slots for chunk in range(pieces)]

    def hop(way, target, step, origin, index):
        slot, chunk = parts[index]
        part = ((slot,) if shift else ()) + middle + (pl.ds(chunk * rows, rows), slice(None))
        if step == 0:
            source = out_ref.at[me] if slot == 1 else x_ref
        else:
            source = out_ref.at[origin]
        return pltpu.make_async_remote_copy(
            src_ref=source.at[part],
            dst_ref=out_ref.at[origin].at[part],
            send_sem=send_sem.at[way, step, index],
            recv_sem=recv_sem.at[way, step, index],
            device_id=(group, target),
            device_id_type=MESH,
        )

    sent = []
    for slot in slots:
        if slot == 1:
            across.wait_recv()
        for way, sign, target, steps in ways:
            for index in range(len(parts)):
                if parts[index][0] == slot:
                    copy = hop(way, target, 0, me, index)
                    copy.start()
                    sent.append(copy)
    for step in range(1, n // 2):
        for way, sign, target, steps in ways:
            if step >= steps:
                continue
            origin = lax.rem(me - sign * step + 2 * n, n)
            for index in range(len(parts)):
                hop(way, target, step - 1, origin, index).wait_recv()
                copy = hop(way, target, step, origin, index)
                copy.start()
                sent.append(copy)
    for way, sign, target, steps in ways:
        origin = lax.rem(me - sign * steps + 2 * n, n)
        for index in range(len(parts)):
            hop(way, target, steps - 1, origin, index).wait_recv()
    for copy in sent:
        copy.wait_send()
    own.wait()
    if shift:
        across.wait_send()
        for copy in roles_across:
            copy.wait_send()
            copy.wait_recv()


def node_gather(block, collective_id, shift=0, roles=None, pieces=4):
    n = lax.axis_size("node")
    groups = lax.axis_size("sub")
    vmem = pl.BlockSpec(memory_space=pltpu.VMEM)
    gathered = jax.ShapeDtypeStruct((n,) + block.shape, block.dtype)
    operands = (block,) if roles is None else (block, roles)
    return pl.pallas_call(
        functools.partial(gather_kernel, n, groups, shift, pieces, roles is not None),
        out_shape=gathered if roles is None else (gathered, jax.ShapeDtypeStruct((2,) + roles.shape, roles.dtype)),
        in_specs=[vmem] * len(operands),
        out_specs=vmem if roles is None else (vmem, vmem),
        scratch_shapes=[
            pltpu.SemaphoreType.DMA((2, n // 2, pieces * (2 if shift else 1))),
            pltpu.SemaphoreType.DMA((2, n // 2, pieces * (2 if shift else 1))),
            pltpu.SemaphoreType.DMA,
            pltpu.SemaphoreType.DMA((6,)),
        ],
        compiler_params=pltpu.CompilerParams(collective_id=collective_id, has_side_effects=True),
    )(*operands)


def node_up(tensor_here, left_env, right_env):
    first = jnp.einsum(
        "xa,abp->xbp", left_env, tensor_here, preferred_element_type=jnp.float32
    ).astype(jnp.bfloat16)
    second = jnp.einsum("yb,xbp->xyp", right_env, first, preferred_element_type=jnp.float32).astype(
        jnp.bfloat16
    )
    return jnp.einsum(
        "xyq,xyp->qp", tensor_here, second, preferred_element_type=jnp.float32
    ).astype(jnp.bfloat16)


def node_down(tensor_here, left_env, right_env, upper_here):
    weighted = jnp.einsum(
        "qp,abp->abq", upper_here, tensor_here, preferred_element_type=jnp.float32
    ).astype(jnp.bfloat16)
    right_part = jnp.einsum(
        "xyq,yb->xbq", tensor_here, right_env, preferred_element_type=jnp.float32
    ).astype(jnp.bfloat16)
    left_part = jnp.einsum(
        "xyq,xa->ayq", tensor_here, left_env, preferred_element_type=jnp.float32
    ).astype(jnp.bfloat16)
    first_child = jnp.einsum(
        "xbq,abq->xa", right_part, weighted, preferred_element_type=jnp.float32
    ).astype(jnp.bfloat16)
    second_child = jnp.einsum(
        "ayq,abq->yb", left_part, weighted, preferred_element_type=jnp.float32
    ).astype(jnp.bfloat16)
    return (first_child, second_child)


def placements(group_roles):
    group_size = group_roles.shape[0]
    spots = jnp.arange(group_size, dtype=jnp.int32)
    return jnp.sum(jnp.where(group_roles[None, :] == spots[:, None], spots[None, :], 0), axis=1)


def pick(table, hit):
    hit = hit.reshape(hit.shape + (1,) * (table.ndim - 1))
    return jnp.sum(jnp.where(hit, table.astype(jnp.float32), 0.0), axis=0).astype(table.dtype)


def local(node_tensor, outer_env, upper_env, role_map, child_slots):
    tensor_here = node_tensor[0, 0]
    outer_envs = outer_env[0, 0]
    upper_envs = upper_env[0, 0]
    group_roles = role_map[0]
    child_links = child_slots[0]
    group_size = lax.axis_size("node")
    top_count = group_size // 4
    mid_count = 2 * top_count
    bond_size = tensor_here.shape[0]
    role_spot = placements(group_roles)
    position = lax.axis_index("node")
    my_role = group_roles[position]
    is_top = my_role < top_count
    is_mid = jnp.logical_and(my_role >= top_count, my_role < top_count + mid_count)
    is_leaf = my_role >= top_count + mid_count
    zero_envs = jnp.zeros((TERMS, bond_size, bond_size), jnp.bfloat16)

    def leaf_work():
        return jnp.stack([node_up(tensor_here, outer_envs[0, 0], outer_envs[1, 0])])

    leaf_up = lax.cond(is_leaf, leaf_work, lambda: zero_envs)
    every_leaf = node_gather(leaf_up, 0)
    mid_index = jnp.clip(my_role - top_count, 0, mid_count - 1)

    def mid_work():
        child_envs = []
        for branch in range(2):
            slot_link = child_links[2 * mid_index + branch]
            leaf_pick = pick(every_leaf, group_roles == top_count + mid_count + jnp.maximum(slot_link, 0))
            child_envs.append(jnp.where(slot_link >= 0, leaf_pick, outer_envs[branch]))
        return jnp.stack([node_up(tensor_here, child_envs[0][0], child_envs[1][0])])

    mid_up = lax.cond(is_mid, mid_work, lambda: zero_envs)
    every_mid, near_roles = node_gather(jnp.stack([mid_up, mid_up]), 1, -1, role_map)
    next_roles = near_roles[0]
    prev_roles = near_roles[1]
    top_index = jnp.clip(my_role, 0, top_count - 1)
    left_envs = pick(every_mid[:, 0], group_roles == top_count + top_index)
    right_envs = pick(every_mid[:, 1], next_roles[0] == top_count + top_count + top_index)

    def top_work():
        results = [node_down(tensor_here, left_envs[t], right_envs[t], upper_envs[t]) for t in range(TERMS)]
        return jnp.stack([jnp.stack([r[0] for r in results]), jnp.stack([r[1] for r in results])])

    top_down = lax.cond(
        is_top, top_work, lambda: jnp.zeros((2, TERMS, bond_size, bond_size), jnp.bfloat16)
    )
    every_top = node_gather(top_down, 2, 1)
    own_field = pick(every_top[:, 0], group_roles == jnp.clip(mid_index, 0, top_count - 1))
    other_field = pick(every_top[:, 1], prev_roles[0] == jnp.clip(mid_index - top_count, 0, top_count - 1))
    mid_field = jnp.where(mid_index < top_count, own_field, other_field)
    result = jnp.where(is_mid, mid_field, jnp.where(is_leaf, leaf_up, zero_envs))
    return result[None, None]


def solution(mesh):
    return jax.shard_map(
        local,
        mesh=mesh,
        in_specs=(
            P("sub", "node", None, None, None),
            P("sub", "node", None, None, None, None),
            P("sub", "node", None, None, None),
            P("sub", None),
            P("sub", None),
        ),
        out_specs=P("sub", "node", None, None, None),
        check_vma=False,
    )
```

```python
import functools

import jax
import jax.numpy as jnp
from jax import lax
from jax.experimental import pallas as pl
from jax.experimental.pallas import tpu as pltpu
from jax.sharding import PartitionSpec as P

TERMS = 1
MESH = pl.DeviceIdType.MESH


def from_behind(block, axis, distance):
    devices = range(lax.axis_size(axis))
    route = [((i - distance) % len(devices), i) for i in devices]
    return lax.ppermute(block, axis, route)


def gather_kernel(n, groups, shift, pieces, with_roles, *refs):
    if with_roles:
        x_ref, roles_ref, out_ref, roles_out, send_sem, recv_sem, own_sem, sub_sem = refs
    else:
        x_ref, out_ref, send_sem, recv_sem, own_sem, sub_sem = refs
    me = lax.axis_index("node")
    group = lax.axis_index("sub")
    right = lax.rem(me + 1, n)
    left = lax.rem(me + n - 1, n)
    barrier = pltpu.get_barrier_semaphore()
    peers = [(group, left), (group, right)]
    if shift:
        peers += [(lax.rem(group + shift + groups, groups), me), (lax.rem(group - shift + groups, groups), me)]
    for peer in peers:
        pl.semaphore_signal(barrier, inc=1, device_id=peer, device_id_type=MESH)
    pl.semaphore_wait(barrier, len(peers))
    if shift:
        own = pltpu.make_async_copy(x_ref.at[0], out_ref.at[me, 0], own_sem)
        own.start()
        across = pltpu.make_async_remote_copy(
            src_ref=x_ref.at[1],
            dst_ref=out_ref.at[me, 1],
            send_sem=sub_sem.at[0],
            recv_sem=sub_sem.at[1],
            device_id=peers[2],
            device_id_type=MESH,
        )
        across.start()
        roles_across = [
            pltpu.make_async_remote_copy(
                src_ref=roles_ref,
                dst_ref=roles_out.at[side],
                send_sem=sub_sem.at[2 + 2 * side],
                recv_sem=sub_sem.at[3 + 2 * side],
                device_id=peers[2 + side],
                device_id_type=MESH,
            )
            for side in range(2 if with_roles else 0)
        ]
        for copy in roles_across:
            copy.start()
    else:
        own = pltpu.make_async_copy(x_ref, out_ref.at[me], own_sem)
        own.start()
    ways = ((0, 1, right, n // 2), (1, -1, left, n - 1 - n // 2))
    rows = x_ref.shape[-2] // pieces
    slots = (0, 1) if shift else (None,)
    middle = (slice(None),) * (len(x_ref.shape) - 2 - (1 if shift else 0))
    parts = [(slot, chunk) for slot in slots for chunk in range(pieces)]

    def hop(way, target, step, origin, index):
        slot, chunk = parts[index]
        part = ((slot,) if shift else ()) + middle + (pl.ds(chunk * rows, rows), slice(None))
        if step == 0:
            source = out_ref.at[me] if slot == 1 else x_ref
        else:
            source = out_ref.at[origin]
        return pltpu.make_async_remote_copy(
            src_ref=source.at[part],
            dst_ref=out_ref.at[origin].at[part],
            send_sem=send_sem.at[way, step, index],
            recv_sem=recv_sem.at[way, step, index],
            device_id=(group, target),
            device_id_type=MESH,
        )

    sent = []
    for slot in slots:
        if slot == 1:
            across.wait_recv()
        for way, sign, target, steps in ways:
            for index in range(len(parts)):
                if parts[index][0] == slot:
                    copy = hop(way, target, 0, me, index)
                    copy.start()
                    sent.append(copy)
    for step in range(1, n // 2):
        for way, sign, target, steps in ways:
            if step >= steps:
                continue
            origin = lax.rem(me - sign * step + 2 * n, n)
            for index in range(len(parts)):
                hop(way, target, step - 1, origin, index).wait_recv()
                copy = hop(way, target, step, origin, index)
                copy.start()
                sent.append(copy)
    for way, sign, target, steps in ways:
        origin = lax.rem(me - sign * steps + 2 * n, n)
        for index in range(len(parts)):
            hop(way, target, steps - 1, origin, index).wait_recv()
    for copy in sent:
        copy.wait_send()
    own.wait()
    if shift:
        across.wait_send()
        for copy in roles_across:
            copy.wait_send()
            copy.wait_recv()


def node_gather(block, collective_id, shift=0, roles=None, pieces=4):
    n = lax.axis_size("node")
    groups = lax.axis_size("sub")
    vmem = pl.BlockSpec(memory_space=pltpu.VMEM)
    gathered = jax.ShapeDtypeStruct((n,) + block.shape, block.dtype)
    operands = (block,) if roles is None else (block, roles)
    return pl.pallas_call(
        functools.partial(gather_kernel, n, groups, shift, pieces, roles is not None),
        out_shape=gathered if roles is None else (gathered, jax.ShapeDtypeStruct((2,) + roles.shape, roles.dtype)),
        in_specs=[vmem] * len(operands),
        out_specs=vmem if roles is None else (vmem, vmem),
        scratch_shapes=[
            pltpu.SemaphoreType.DMA((2, n // 2, pieces * (2 if shift else 1))),
            pltpu.SemaphoreType.DMA((2, n // 2, pieces * (2 if shift else 1))),
            pltpu.SemaphoreType.DMA,
            pltpu.SemaphoreType.DMA((6,)),
        ],
        compiler_params=pltpu.CompilerParams(collective_id=collective_id, has_side_effects=True),
    )(*operands)


def node_up(tensor_here, left_env, right_env):
    first = jnp.einsum(
        "xa,abp->xbp", left_env, tensor_here, preferred_element_type=jnp.float32
    ).astype(jnp.bfloat16)
    second = jnp.einsum("yb,xbp->xyp", right_env, first, preferred_element_type=jnp.float32).astype(
        jnp.bfloat16
    )
    return jnp.einsum(
        "xyq,xyp->qp", tensor_here, second, preferred_element_type=jnp.float32
    ).astype(jnp.bfloat16)


def node_down(tensor_here, left_env, right_env, upper_here):
    weighted = jnp.einsum(
        "qp,abp->abq", upper_here, tensor_here, preferred_element_type=jnp.float32
    ).astype(jnp.bfloat16)
    right_part = jnp.einsum(
        "xyq,yb->xbq", tensor_here, right_env, preferred_element_type=jnp.float32
    ).astype(jnp.bfloat16)
    left_part = jnp.einsum(
        "xyq,xa->ayq", tensor_here, left_env, preferred_element_type=jnp.float32
    ).astype(jnp.bfloat16)
    first_child = jnp.einsum(
        "xbq,abq->xa", right_part, weighted, preferred_element_type=jnp.float32
    ).astype(jnp.bfloat16)
    second_child = jnp.einsum(
        "ayq,abq->yb", left_part, weighted, preferred_element_type=jnp.float32
    ).astype(jnp.bfloat16)
    return (first_child, second_child)


def placements(group_roles):
    group_size = group_roles.shape[0]
    spots = jnp.arange(group_size, dtype=jnp.int32)
    return jnp.sum(jnp.where(group_roles[None, :] == spots[:, None], spots[None, :], 0), axis=1)


def pick(table, hit):
    hit = hit.reshape(hit.shape + (1,) * (table.ndim - 1))
    return jnp.sum(jnp.where(hit, table.astype(jnp.float32), 0.0), axis=0).astype(table.dtype)


def local(node_tensor, outer_env, upper_env, role_map, child_slots):
    tensor_here = node_tensor[0, 0]
    outer_envs = outer_env[0, 0]
    upper_envs = upper_env[0, 0]
    group_roles = role_map[0]
    child_links = child_slots[0]
    group_size = lax.axis_size("node")
    top_count = group_size // 4
    mid_count = 2 * top_count
    bond_size = tensor_here.shape[0]
    role_spot = placements(group_roles)
    position = lax.axis_index("node")
    my_role = group_roles[position]
    is_top = my_role < top_count
    is_mid = jnp.logical_and(my_role >= top_count, my_role < top_count + mid_count)
    is_leaf = my_role >= top_count + mid_count
    zero_envs = jnp.zeros((TERMS, bond_size, bond_size), jnp.bfloat16)

    def leaf_work():
        return jnp.stack([node_up(tensor_here, outer_envs[0, 0], outer_envs[1, 0])])

    leaf_up = lax.cond(is_leaf, leaf_work, lambda: zero_envs)
    every_leaf = node_gather(leaf_up, 0)
    mid_index = jnp.clip(my_role - top_count, 0, mid_count - 1)

    def mid_work():
        child_envs = []
        for branch in range(2):
            slot_link = child_links[2 * mid_index + branch]
            leaf_pick = pick(every_leaf, group_roles == top_count + mid_count + jnp.maximum(slot_link, 0))
            child_envs.append(jnp.where(slot_link >= 0, leaf_pick, outer_envs[branch]))
        return jnp.stack([node_up(tensor_here, child_envs[0][0], child_envs[1][0])])

    mid_up = lax.cond(is_mid, mid_work, lambda: zero_envs)
    every_mid, near_roles = node_gather(jnp.stack([mid_up, mid_up]), 1, -1, role_map, pieces=2)
    next_roles = near_roles[0]
    prev_roles = near_roles[1]
    top_index = jnp.clip(my_role, 0, top_count - 1)
    left_envs = pick(every_mid[:, 0], group_roles == top_count + top_index)
    right_envs = pick(every_mid[:, 1], next_roles[0] == top_count + top_count + top_index)

    def top_work():
        results = [node_down(tensor_here, left_envs[t], right_envs[t], upper_envs[t]) for t in range(TERMS)]
        return jnp.stack([jnp.stack([r[0] for r in results]), jnp.stack([r[1] for r in results])])

    top_down = lax.cond(
        is_top, top_work, lambda: jnp.zeros((2, TERMS, bond_size, bond_size), jnp.bfloat16)
    )
    every_top = node_gather(top_down, 2, 1, pieces=2)
    own_field = pick(every_top[:, 0], group_roles == jnp.clip(mid_index, 0, top_count - 1))
    other_field = pick(every_top[:, 1], prev_roles[0] == jnp.clip(mid_index - top_count, 0, top_count - 1))
    mid_field = jnp.where(mid_index < top_count, own_field, other_field)
    result = jnp.where(is_mid, mid_field, jnp.where(is_leaf, leaf_up, zero_envs))
    return result[None, None]


def solution(mesh):
    return jax.shard_map(
        local,
        mesh=mesh,
        in_specs=(
            P("sub", "node", None, None, None),
            P("sub", "node", None, None, None, None),
            P("sub", "node", None, None, None),
            P("sub", None),
            P("sub", None),
        ),
        out_specs=P("sub", "node", None, None, None),
        check_vma=False,
    )
```

```python
import functools

import jax
import jax.numpy as jnp
from jax import lax
from jax.experimental import pallas as pl
from jax.experimental.pallas import tpu as pltpu
from jax.sharding import PartitionSpec as P

TERMS = 1
MESH = pl.DeviceIdType.MESH


def from_behind(block, axis, distance):
    devices = range(lax.axis_size(axis))
    route = [((i - distance) % len(devices), i) for i in devices]
    return lax.ppermute(block, axis, route)


def gather_kernel(n, groups, shift, pieces, with_roles, *refs):
    if with_roles:
        x_ref, roles_ref, out_ref, roles_out, send_sem, recv_sem, own_sem, sub_sem = refs
    else:
        x_ref, out_ref, send_sem, recv_sem, own_sem, sub_sem = refs
    me = lax.axis_index("node")
    group = lax.axis_index("sub")
    right = lax.rem(me + 1, n)
    left = lax.rem(me + n - 1, n)
    barrier = pltpu.get_barrier_semaphore()
    peers = [(group, left), (group, right)]
    if shift:
        peers += [(lax.rem(group + shift + groups, groups), me), (lax.rem(group - shift + groups, groups), me)]
    for peer in peers:
        pl.semaphore_signal(barrier, inc=1, device_id=peer, device_id_type=MESH)
    pl.semaphore_wait(barrier, len(peers))
    if shift:
        own = pltpu.make_async_copy(x_ref.at[0], out_ref.at[me, 0], own_sem)
        own.start()
        across = pltpu.make_async_remote_copy(
            src_ref=x_ref.at[1],
            dst_ref=out_ref.at[me, 1],
            send_sem=sub_sem.at[0],
            recv_sem=sub_sem.at[1],
            device_id=peers[2],
            device_id_type=MESH,
        )
        across.start()
        roles_across = [
            pltpu.make_async_remote_copy(
                src_ref=roles_ref,
                dst_ref=roles_out.at[side],
                send_sem=sub_sem.at[2 + 2 * side],
                recv_sem=sub_sem.at[3 + 2 * side],
                device_id=peers[2 + side],
                device_id_type=MESH,
            )
            for side in range(2 if with_roles else 0)
        ]
        for copy in roles_across:
            copy.start()
    else:
        own = pltpu.make_async_copy(x_ref, out_ref.at[me], own_sem)
        own.start()
    ways = ((0, 1, right, n // 2), (1, -1, left, n - 1 - n // 2))
    rows = x_ref.shape[-2] // pieces
    slots = (0, 1) if shift else (None,)
    middle = (slice(None),) * (len(x_ref.shape) - 2 - (1 if shift else 0))
    parts = [(slot, chunk) for slot in slots for chunk in range(pieces)]

    def hop(way, target, step, origin, index):
        slot, chunk = parts[index]
        part = ((slot,) if shift else ()) + middle + (pl.ds(chunk * rows, rows), slice(None))
        if step == 0:
            source = out_ref.at[me] if slot == 1 else x_ref
        else:
            source = out_ref.at[origin]
        return pltpu.make_async_remote_copy(
            src_ref=source.at[part],
            dst_ref=out_ref.at[origin].at[part],
            send_sem=send_sem.at[way, step, index],
            recv_sem=recv_sem.at[way, step, index],
            device_id=(group, target),
            device_id_type=MESH,
        )

    sent = []
    for slot in slots:
        if slot == 1:
            across.wait_recv()
        for way, sign, target, steps in ways:
            for index in range(len(parts)):
                if parts[index][0] == slot:
                    copy = hop(way, target, 0, me, index)
                    copy.start()
                    sent.append(copy)
    for step in range(1, n // 2):
        for way, sign, target, steps in ways:
            if step >= steps:
                continue
            origin = lax.rem(me - sign * step + 2 * n, n)
            for index in range(len(parts)):
                hop(way, target, step - 1, origin, index).wait_recv()
                copy = hop(way, target, step, origin, index)
                copy.start()
                sent.append(copy)
    for way, sign, target, steps in ways:
        origin = lax.rem(me - sign * steps + 2 * n, n)
        for index in range(len(parts)):
            hop(way, target, steps - 1, origin, index).wait_recv()
    for copy in sent:
        copy.wait_send()
    own.wait()
    if shift:
        across.wait_send()
        for copy in roles_across:
            copy.wait_send()
            copy.wait_recv()


def node_gather(block, collective_id, shift=0, roles=None, pieces=4):
    n = lax.axis_size("node")
    groups = lax.axis_size("sub")
    vmem = pl.BlockSpec(memory_space=pltpu.VMEM)
    gathered = jax.ShapeDtypeStruct((n,) + block.shape, block.dtype)
    operands = (block,) if roles is None else (block, roles)
    return pl.pallas_call(
        functools.partial(gather_kernel, n, groups, shift, pieces, roles is not None),
        out_shape=gathered if roles is None else (gathered, jax.ShapeDtypeStruct((2,) + roles.shape, roles.dtype)),
        in_specs=[vmem] * len(operands),
        out_specs=vmem if roles is None else (vmem, vmem),
        scratch_shapes=[
            pltpu.SemaphoreType.DMA((2, n // 2, pieces * (2 if shift else 1))),
            pltpu.SemaphoreType.DMA((2, n // 2, pieces * (2 if shift else 1))),
            pltpu.SemaphoreType.DMA,
            pltpu.SemaphoreType.DMA((6,)),
        ],
        compiler_params=pltpu.CompilerParams(collective_id=collective_id, has_side_effects=True),
    )(*operands)


def node_up(tensor_here, left_env, right_env):
    first = jnp.einsum(
        "xa,abp->xbp", left_env, tensor_here, preferred_element_type=jnp.float32
    ).astype(jnp.bfloat16)
    second = jnp.einsum("yb,xbp->xyp", right_env, first, preferred_element_type=jnp.float32).astype(
        jnp.bfloat16
    )
    return jnp.einsum(
        "xyq,xyp->qp", tensor_here, second, preferred_element_type=jnp.float32
    ).astype(jnp.bfloat16)


def node_down(tensor_here, left_env, right_env, upper_here):
    weighted = jnp.einsum(
        "qp,abp->abq", upper_here, tensor_here, preferred_element_type=jnp.float32
    ).astype(jnp.bfloat16)
    right_part = jnp.einsum(
        "xyq,yb->xbq", tensor_here, right_env, preferred_element_type=jnp.float32
    ).astype(jnp.bfloat16)
    left_part = jnp.einsum(
        "xyq,xa->ayq", tensor_here, left_env, preferred_element_type=jnp.float32
    ).astype(jnp.bfloat16)
    first_child = jnp.einsum(
        "xbq,abq->xa", right_part, weighted, preferred_element_type=jnp.float32
    ).astype(jnp.bfloat16)
    second_child = jnp.einsum(
        "ayq,abq->yb", left_part, weighted, preferred_element_type=jnp.float32
    ).astype(jnp.bfloat16)
    return (first_child, second_child)


def placements(group_roles):
    group_size = group_roles.shape[0]
    spots = jnp.arange(group_size, dtype=jnp.int32)
    return jnp.sum(jnp.where(group_roles[None, :] == spots[:, None], spots[None, :], 0), axis=1)


def pick(table, hit):
    hit = hit.reshape(hit.shape + (1,) * (table.ndim - 1))
    return jnp.sum(jnp.where(hit, table.astype(jnp.float32), 0.0), axis=0).astype(table.dtype)


def local(node_tensor, outer_env, upper_env, role_map, child_slots):
    tensor_here = node_tensor[0, 0]
    outer_envs = outer_env[0, 0]
    upper_envs = upper_env[0, 0]
    group_roles = role_map[0]
    child_links = child_slots[0]
    group_size = lax.axis_size("node")
    top_count = group_size // 4
    mid_count = 2 * top_count
    bond_size = tensor_here.shape[0]
    role_spot = placements(group_roles)
    position = lax.axis_index("node")
    my_role = group_roles[position]
    is_top = my_role < top_count
    is_mid = jnp.logical_and(my_role >= top_count, my_role < top_count + mid_count)
    is_leaf = my_role >= top_count + mid_count
    zero_envs = jnp.zeros((TERMS, bond_size, bond_size), jnp.bfloat16)

    def leaf_work():
        return jnp.stack([node_up(tensor_here, outer_envs[0, 0], outer_envs[1, 0])])

    leaf_up = lax.cond(is_leaf, leaf_work, lambda: zero_envs)
    every_leaf = node_gather(leaf_up, 0, pieces=2)
    mid_index = jnp.clip(my_role - top_count, 0, mid_count - 1)

    def mid_work():
        child_envs = []
        for branch in range(2):
            slot_link = child_links[2 * mid_index + branch]
            leaf_pick = pick(every_leaf, group_roles == top_count + mid_count + jnp.maximum(slot_link, 0))
            child_envs.append(jnp.where(slot_link >= 0, leaf_pick, outer_envs[branch]))
        return jnp.stack([node_up(tensor_here, child_envs[0][0], child_envs[1][0])])

    mid_up = lax.cond(is_mid, mid_work, lambda: zero_envs)
    every_mid, near_roles = node_gather(jnp.stack([mid_up, mid_up]), 1, -1, role_map, pieces=2)
    next_roles = near_roles[0]
    prev_roles = near_roles[1]
    top_index = jnp.clip(my_role, 0, top_count - 1)
    left_envs = pick(every_mid[:, 0], group_roles == top_count + top_index)
    right_envs = pick(every_mid[:, 1], next_roles[0] == top_count + top_count + top_index)

    def top_work():
        results = [node_down(tensor_here, left_envs[t], right_envs[t], upper_envs[t]) for t in range(TERMS)]
        return jnp.stack([jnp.stack([r[0] for r in results]), jnp.stack([r[1] for r in results])])

    top_down = lax.cond(
        is_top, top_work, lambda: jnp.zeros((2, TERMS, bond_size, bond_size), jnp.bfloat16)
    )
    every_top = node_gather(top_down, 2, 1, pieces=2)
    own_field = pick(every_top[:, 0], group_roles == jnp.clip(mid_index, 0, top_count - 1))
    other_field = pick(every_top[:, 1], prev_roles[0] == jnp.clip(mid_index - top_count, 0, top_count - 1))
    mid_field = jnp.where(mid_index < top_count, own_field, other_field)
    result = jnp.where(is_mid, mid_field, jnp.where(is_leaf, leaf_up, zero_envs))
    return result[None, None]


def solution(mesh):
    return jax.shard_map(
        local,
        mesh=mesh,
        in_specs=(
            P("sub", "node", None, None, None),
            P("sub", "node", None, None, None, None),
            P("sub", "node", None, None, None),
            P("sub", None),
            P("sub", None),
        ),
        out_specs=P("sub", "node", None, None, None),
        check_vma=False,
    )
```

```python
import functools

import jax
import jax.numpy as jnp
from jax import lax
from jax.experimental import pallas as pl
from jax.experimental.pallas import tpu as pltpu
from jax.sharding import PartitionSpec as P

TERMS = 1
MESH = pl.DeviceIdType.MESH


def from_behind(block, axis, distance):
    devices = range(lax.axis_size(axis))
    route = [((i - distance) % len(devices), i) for i in devices]
    return lax.ppermute(block, axis, route)


def gather_kernel(n, groups, shift, pieces, with_roles, *refs):
    if with_roles:
        x_ref, roles_ref, out_ref, roles_out, send_sem, recv_sem, own_sem, sub_sem = refs
    else:
        x_ref, out_ref, send_sem, recv_sem, own_sem, sub_sem = refs
    me = lax.axis_index("node")
    group = lax.axis_index("sub")
    right = lax.rem(me + 1, n)
    left = lax.rem(me + n - 1, n)
    barrier = pltpu.get_barrier_semaphore()
    peers = [(group, left), (group, right)]
    if shift:
        peers += [(lax.rem(group + shift + groups, groups), me), (lax.rem(group - shift + groups, groups), me)]
    for peer in peers:
        pl.semaphore_signal(barrier, inc=1, device_id=peer, device_id_type=MESH)
    pl.semaphore_wait(barrier, len(peers))
    if shift:
        own = pltpu.make_async_copy(x_ref.at[0], out_ref.at[me, 0], own_sem)
        own.start()
        across = pltpu.make_async_remote_copy(
            src_ref=x_ref.at[1],
            dst_ref=out_ref.at[me, 1],
            send_sem=sub_sem.at[0],
            recv_sem=sub_sem.at[1],
            device_id=peers[2],
            device_id_type=MESH,
        )
        across.start()
        roles_across = [
            pltpu.make_async_remote_copy(
                src_ref=roles_ref,
                dst_ref=roles_out.at[side],
                send_sem=sub_sem.at[2 + 2 * side],
                recv_sem=sub_sem.at[3 + 2 * side],
                device_id=peers[2 + side],
                device_id_type=MESH,
            )
            for side in range(2 if with_roles else 0)
        ]
        for copy in roles_across:
            copy.start()
    else:
        own = pltpu.make_async_copy(x_ref, out_ref.at[me], own_sem)
        own.start()
    ways = ((0, 1, right, n // 2), (1, -1, left, n - 1 - n // 2))
    rows = x_ref.shape[-2] // pieces
    slots = (0, 1) if shift else (None,)
    middle = (slice(None),) * (len(x_ref.shape) - 2 - (1 if shift else 0))
    parts = [(slot, chunk) for slot in slots for chunk in range(pieces)]

    def hop(way, target, step, origin, index):
        slot, chunk = parts[index]
        part = ((slot,) if shift else ()) + middle + (pl.ds(chunk * rows, rows), slice(None))
        if step == 0:
            source = out_ref.at[me] if slot == 1 else x_ref
        else:
            source = out_ref.at[origin]
        return pltpu.make_async_remote_copy(
            src_ref=source.at[part],
            dst_ref=out_ref.at[origin].at[part],
            send_sem=send_sem.at[way, step, index],
            recv_sem=recv_sem.at[way, step, index],
            device_id=(group, target),
            device_id_type=MESH,
        )

    sent = []
    for slot in slots:
        if slot == 1:
            across.wait_recv()
        for way, sign, target, steps in ways:
            for index in range(len(parts)):
                if parts[index][0] == slot:
                    copy = hop(way, target, 0, me, index)
                    copy.start()
                    sent.append(copy)
    for step in range(1, n // 2):
        for way, sign, target, steps in ways:
            if step >= steps:
                continue
            origin = lax.rem(me - sign * step + 2 * n, n)
            for index in range(len(parts)):
                hop(way, target, step - 1, origin, index).wait_recv()
                copy = hop(way, target, step, origin, index)
                copy.start()
                sent.append(copy)
    for way, sign, target, steps in ways:
        origin = lax.rem(me - sign * steps + 2 * n, n)
        for index in range(len(parts)):
            hop(way, target, steps - 1, origin, index).wait_recv()
    for copy in sent:
        copy.wait_send()
    own.wait()
    if shift:
        across.wait_send()
        for copy in roles_across:
            copy.wait_send()
            copy.wait_recv()


def node_gather(block, collective_id, shift=0, roles=None, pieces=4):
    n = lax.axis_size("node")
    groups = lax.axis_size("sub")
    vmem = pl.BlockSpec(memory_space=pltpu.VMEM)
    gathered = jax.ShapeDtypeStruct((n,) + block.shape, block.dtype)
    operands = (block,) if roles is None else (block, roles)
    return pl.pallas_call(
        functools.partial(gather_kernel, n, groups, shift, pieces, roles is not None),
        out_shape=gathered if roles is None else (gathered, jax.ShapeDtypeStruct((2,) + roles.shape, roles.dtype)),
        in_specs=[vmem] * len(operands),
        out_specs=vmem if roles is None else (vmem, vmem),
        scratch_shapes=[
            pltpu.SemaphoreType.DMA((2, n // 2, pieces * (2 if shift else 1))),
            pltpu.SemaphoreType.DMA((2, n // 2, pieces * (2 if shift else 1))),
            pltpu.SemaphoreType.DMA,
            pltpu.SemaphoreType.DMA((6,)),
        ],
        compiler_params=pltpu.CompilerParams(collective_id=collective_id, has_side_effects=True),
    )(*operands)


def node_up(tensor_here, left_env, right_env):
    first = jnp.einsum(
        "abp,yb->ayp", tensor_here, right_env, preferred_element_type=jnp.float32
    ).astype(jnp.bfloat16)
    second = jnp.einsum("xa,ayp->xyp", left_env, first, preferred_element_type=jnp.float32).astype(
        jnp.bfloat16
    )
    return jnp.einsum(
        "xyq,xyp->qp", tensor_here, second, preferred_element_type=jnp.float32
    ).astype(jnp.bfloat16)


def node_down(tensor_here, left_env, right_env, upper_here):
    weighted = jnp.einsum(
        "qp,abp->abq", upper_here, tensor_here, preferred_element_type=jnp.float32
    ).astype(jnp.bfloat16)
    right_part = jnp.einsum(
        "xyq,yb->xbq", tensor_here, right_env, preferred_element_type=jnp.float32
    ).astype(jnp.bfloat16)
    left_part = jnp.einsum(
        "xyq,xa->ayq", tensor_here, left_env, preferred_element_type=jnp.float32
    ).astype(jnp.bfloat16)
    first_child = jnp.einsum(
        "xbq,abq->xa", right_part, weighted, preferred_element_type=jnp.float32
    ).astype(jnp.bfloat16)
    second_child = jnp.einsum(
        "ayq,abq->yb", left_part, weighted, preferred_element_type=jnp.float32
    ).astype(jnp.bfloat16)
    return (first_child, second_child)


def placements(group_roles):
    group_size = group_roles.shape[0]
    spots = jnp.arange(group_size, dtype=jnp.int32)
    return jnp.sum(jnp.where(group_roles[None, :] == spots[:, None], spots[None, :], 0), axis=1)


def pick(table, hit):
    hit = hit.reshape(hit.shape + (1,) * (table.ndim - 1))
    return jnp.sum(jnp.where(hit, table.astype(jnp.float32), 0.0), axis=0).astype(table.dtype)


def local(node_tensor, outer_env, upper_env, role_map, child_slots):
    tensor_here = node_tensor[0, 0]
    outer_envs = outer_env[0, 0]
    upper_envs = upper_env[0, 0]
    group_roles = role_map[0]
    child_links = child_slots[0]
    group_size = lax.axis_size("node")
    top_count = group_size // 4
    mid_count = 2 * top_count
    bond_size = tensor_here.shape[0]
    role_spot = placements(group_roles)
    position = lax.axis_index("node")
    my_role = group_roles[position]
    is_top = my_role < top_count
    is_mid = jnp.logical_and(my_role >= top_count, my_role < top_count + mid_count)
    is_leaf = my_role >= top_count + mid_count
    zero_envs = jnp.zeros((TERMS, bond_size, bond_size), jnp.bfloat16)

    def leaf_work():
        return jnp.stack([node_up(tensor_here, outer_envs[0, 0], outer_envs[1, 0])])

    leaf_up = lax.cond(is_leaf, leaf_work, lambda: zero_envs)
    every_leaf = node_gather(leaf_up, 0, pieces=2)
    mid_index = jnp.clip(my_role - top_count, 0, mid_count - 1)

    def mid_work():
        child_envs = []
        for branch in range(2):
            slot_link = child_links[2 * mid_index + branch]
            leaf_pick = pick(every_leaf, group_roles == top_count + mid_count + jnp.maximum(slot_link, 0))
            child_envs.append(jnp.where(slot_link >= 0, leaf_pick, outer_envs[branch]))
        return jnp.stack([node_up(tensor_here, child_envs[0][0], child_envs[1][0])])

    mid_up = lax.cond(is_mid, mid_work, lambda: zero_envs)
    every_mid, near_roles = node_gather(jnp.stack([mid_up, mid_up]), 1, -1, role_map, pieces=2)
    next_roles = near_roles[0]
    prev_roles = near_roles[1]
    top_index = jnp.clip(my_role, 0, top_count - 1)
    left_envs = pick(every_mid[:, 0], group_roles == top_count + top_index)
    right_envs = pick(every_mid[:, 1], next_roles[0] == top_count + top_count + top_index)

    def top_work():
        results = [node_down(tensor_here, left_envs[t], right_envs[t], upper_envs[t]) for t in range(TERMS)]
        return jnp.stack([jnp.stack([r[0] for r in results]), jnp.stack([r[1] for r in results])])

    top_down = lax.cond(
        is_top, top_work, lambda: jnp.zeros((2, TERMS, bond_size, bond_size), jnp.bfloat16)
    )
    every_top = node_gather(top_down, 2, 1, pieces=2)
    own_field = pick(every_top[:, 0], group_roles == jnp.clip(mid_index, 0, top_count - 1))
    other_field = pick(every_top[:, 1], prev_roles[0] == jnp.clip(mid_index - top_count, 0, top_count - 1))
    mid_field = jnp.where(mid_index < top_count, own_field, other_field)
    result = jnp.where(is_mid, mid_field, jnp.where(is_leaf, leaf_up, zero_envs))
    return result[None, None]


def solution(mesh):
    return jax.shard_map(
        local,
        mesh=mesh,
        in_specs=(
            P("sub", "node", None, None, None),
            P("sub", "node", None, None, None, None),
            P("sub", "node", None, None, None),
            P("sub", None),
            P("sub", None),
        ),
        out_specs=P("sub", "node", None, None, None),
        check_vma=False,
    )
```

```python
import functools

import jax
import jax.numpy as jnp
from jax import lax
from jax.experimental import pallas as pl
from jax.experimental.pallas import tpu as pltpu
from jax.sharding import PartitionSpec as P

TERMS = 1
MESH = pl.DeviceIdType.MESH


def from_behind(block, axis, distance):
    devices = range(lax.axis_size(axis))
    route = [((i - distance) % len(devices), i) for i in devices]
    return lax.ppermute(block, axis, route)


def gather_kernel(n, groups, shift, pieces, with_roles, *refs):
    if with_roles:
        x_ref, roles_ref, out_ref, roles_out, send_sem, recv_sem, own_sem, sub_sem = refs
    else:
        x_ref, out_ref, send_sem, recv_sem, own_sem, sub_sem = refs
    me = lax.axis_index("node")
    group = lax.axis_index("sub")
    right = lax.rem(me + 1, n)
    left = lax.rem(me + n - 1, n)
    barrier = pltpu.get_barrier_semaphore()
    peers = [(group, left), (group, right)]
    if shift:
        peers += [(lax.rem(group + shift + groups, groups), me), (lax.rem(group - shift + groups, groups), me)]
    for peer in peers:
        pl.semaphore_signal(barrier, inc=1, device_id=peer, device_id_type=MESH)
    pl.semaphore_wait(barrier, len(peers))
    if shift:
        own = pltpu.make_async_copy(x_ref.at[0], out_ref.at[me, 0], own_sem)
        own.start()
        across = pltpu.make_async_remote_copy(
            src_ref=x_ref.at[1],
            dst_ref=out_ref.at[me, 1],
            send_sem=sub_sem.at[0],
            recv_sem=sub_sem.at[1],
            device_id=peers[2],
            device_id_type=MESH,
        )
        across.start()
        roles_across = [
            pltpu.make_async_remote_copy(
                src_ref=roles_ref,
                dst_ref=roles_out.at[side],
                send_sem=sub_sem.at[2 + 2 * side],
                recv_sem=sub_sem.at[3 + 2 * side],
                device_id=peers[2 + side],
                device_id_type=MESH,
            )
            for side in range(2 if with_roles else 0)
        ]
        for copy in roles_across:
            copy.start()
    else:
        own = pltpu.make_async_copy(x_ref, out_ref.at[me], own_sem)
        own.start()
    ways = ((0, 1, right, n // 2), (1, -1, left, n - 1 - n // 2))
    rows = x_ref.shape[-2] // pieces
    slots = (0, 1) if shift else (None,)
    middle = (slice(None),) * (len(x_ref.shape) - 2 - (1 if shift else 0))
    parts = [(slot, chunk) for slot in slots for chunk in range(pieces)]

    def hop(way, target, step, origin, index):
        slot, chunk = parts[index]
        part = ((slot,) if shift else ()) + middle + (pl.ds(chunk * rows, rows), slice(None))
        if step == 0:
            source = out_ref.at[me] if slot == 1 else x_ref
        else:
            source = out_ref.at[origin]
        return pltpu.make_async_remote_copy(
            src_ref=source.at[part],
            dst_ref=out_ref.at[origin].at[part],
            send_sem=send_sem.at[way, step, index],
            recv_sem=recv_sem.at[way, step, index],
            device_id=(group, target),
            device_id_type=MESH,
        )

    sent = []
    for slot in slots:
        if slot == 1:
            across.wait_recv()
        for way, sign, target, steps in ways:
            for index in range(len(parts)):
                if parts[index][0] == slot:
                    copy = hop(way, target, 0, me, index)
                    copy.start()
                    sent.append(copy)
    for step in range(1, n // 2):
        for way, sign, target, steps in ways:
            if step >= steps:
                continue
            origin = lax.rem(me - sign * step + 2 * n, n)
            for index in range(len(parts)):
                hop(way, target, step - 1, origin, index).wait_recv()
                copy = hop(way, target, step, origin, index)
                copy.start()
                sent.append(copy)
    for way, sign, target, steps in ways:
        origin = lax.rem(me - sign * steps + 2 * n, n)
        for index in range(len(parts)):
            hop(way, target, steps - 1, origin, index).wait_recv()
    for copy in sent:
        copy.wait_send()
    own.wait()
    if shift:
        across.wait_send()
        for copy in roles_across:
            copy.wait_send()
            copy.wait_recv()


def node_gather(block, collective_id, shift=0, roles=None, pieces=4):
    n = lax.axis_size("node")
    groups = lax.axis_size("sub")
    vmem = pl.BlockSpec(memory_space=pltpu.VMEM)
    gathered = jax.ShapeDtypeStruct((n,) + block.shape, block.dtype)
    operands = (block,) if roles is None else (block, roles)
    return pl.pallas_call(
        functools.partial(gather_kernel, n, groups, shift, pieces, roles is not None),
        out_shape=gathered if roles is None else (gathered, jax.ShapeDtypeStruct((2,) + roles.shape, roles.dtype)),
        in_specs=[vmem] * len(operands),
        out_specs=vmem if roles is None else (vmem, vmem),
        scratch_shapes=[
            pltpu.SemaphoreType.DMA((2, n // 2, pieces * (2 if shift else 1))),
            pltpu.SemaphoreType.DMA((2, n // 2, pieces * (2 if shift else 1))),
            pltpu.SemaphoreType.DMA,
            pltpu.SemaphoreType.DMA((6,)),
        ],
        compiler_params=pltpu.CompilerParams(collective_id=collective_id, has_side_effects=True),
    )(*operands)


def node_up(tensor_here, left_env, right_env):
    first = jnp.einsum(
        "xa,abp->xbp", left_env, tensor_here, preferred_element_type=jnp.float32
    ).astype(jnp.bfloat16)
    second = jnp.einsum("yb,xbp->xyp", right_env, first, preferred_element_type=jnp.float32).astype(
        jnp.bfloat16
    )
    return jnp.einsum(
        "xyq,xyp->qp", tensor_here, second, preferred_element_type=jnp.float32
    ).astype(jnp.bfloat16)


def node_down(tensor_here, left_env, right_env, upper_here):
    weighted = jnp.einsum(
        "qp,abp->abq", upper_here, tensor_here, preferred_element_type=jnp.float32
    ).astype(jnp.bfloat16)
    right_part = jnp.einsum(
        "xyq,yb->xbq", tensor_here, right_env, preferred_element_type=jnp.float32
    ).astype(jnp.bfloat16)
    left_part = jnp.einsum(
        "xyq,xa->ayq", tensor_here, left_env, preferred_element_type=jnp.float32
    ).astype(jnp.bfloat16)
    first_child = jnp.einsum(
        "xbq,abq->xa", right_part, weighted, preferred_element_type=jnp.float32
    ).astype(jnp.bfloat16)
    second_child = jnp.einsum(
        "ayq,abq->yb", left_part, weighted, preferred_element_type=jnp.float32
    ).astype(jnp.bfloat16)
    return (first_child, second_child)


def placements(group_roles):
    group_size = group_roles.shape[0]
    spots = jnp.arange(group_size, dtype=jnp.int32)
    return jnp.sum(jnp.where(group_roles[None, :] == spots[:, None], spots[None, :], 0), axis=1)


def pick(table, hit):
    hit = hit.reshape(hit.shape + (1,) * (table.ndim - 1))
    return jnp.sum(jnp.where(hit, table.astype(jnp.float32), 0.0), axis=0).astype(table.dtype)


def local(node_tensor, outer_env, upper_env, role_map, child_slots):
    tensor_here = node_tensor[0, 0]
    outer_envs = outer_env[0, 0]
    upper_envs = upper_env[0, 0]
    group_roles = role_map[0]
    child_links = child_slots[0]
    group_size = lax.axis_size("node")
    top_count = group_size // 4
    mid_count = 2 * top_count
    bond_size = tensor_here.shape[0]
    role_spot = placements(group_roles)
    position = lax.axis_index("node")
    my_role = group_roles[position]
    is_top = my_role < top_count
    is_mid = jnp.logical_and(my_role >= top_count, my_role < top_count + mid_count)
    is_leaf = my_role >= top_count + mid_count
    zero_envs = jnp.zeros((TERMS, bond_size, bond_size), jnp.bfloat16)

    def leaf_work():
        return jnp.stack([node_up(tensor_here, outer_envs[0, 0], outer_envs[1, 0])])

    leaf_up = lax.cond(is_leaf, leaf_work, lambda: zero_envs)
    every_leaf = node_gather(leaf_up, 0, pieces=2)
    mid_index = jnp.clip(my_role - top_count, 0, mid_count - 1)

    def mid_work():
        child_envs = []
        for branch in range(2):
            slot_link = child_links[2 * mid_index + branch]
            leaf_pick = pick(every_leaf, group_roles == top_count + mid_count + jnp.maximum(slot_link, 0))
            child_envs.append(jnp.where(slot_link >= 0, leaf_pick, outer_envs[branch]))
        return jnp.stack([node_up(tensor_here, child_envs[0][0], child_envs[1][0])])

    mid_up = lax.cond(is_mid, mid_work, lambda: zero_envs)
    every_mid, near_roles = node_gather(jnp.stack([mid_up, mid_up]), 1, -1, role_map, pieces=2)
    next_roles = near_roles[0]
    prev_roles = near_roles[1]
    top_index = jnp.clip(my_role, 0, top_count - 1)
    left_envs = pick(every_mid[:, 0], group_roles == top_count + top_index)
    right_envs = pick(every_mid[:, 1], next_roles[0] == top_count + top_count + top_index)

    def top_work():
        results = [node_down(tensor_here, left_envs[t], right_envs[t], upper_envs[t]) for t in range(TERMS)]
        return jnp.stack([jnp.stack([r[0] for r in results]), jnp.stack([r[1] for r in results])])

    top_down = lax.cond(
        is_top, top_work, lambda: jnp.zeros((2, TERMS, bond_size, bond_size), jnp.bfloat16)
    )
    every_top = node_gather(top_down, 2, 1, pieces=2)
    own_hit = jnp.logical_and(mid_index < top_count, group_roles == mid_index)
    other_hit = jnp.logical_and(mid_index >= top_count, prev_roles[0] == mid_index - top_count)
    hits = jnp.logical_and(is_mid, jnp.stack([own_hit, other_hit], axis=1))
    mid_field = pick(every_top.reshape((-1,) + every_top.shape[2:]), hits.reshape(-1))
    result = jnp.where(is_leaf, leaf_up, mid_field)
    return result[None, None]


def solution(mesh):
    return jax.shard_map(
        local,
        mesh=mesh,
        in_specs=(
            P("sub", "node", None, None, None),
            P("sub", "node", None, None, None, None),
            P("sub", "node", None, None, None),
            P("sub", None),
            P("sub", None),
        ),
        out_specs=P("sub", "node", None, None, None),
        check_vma=False,
    )
```

```python
import functools

import jax
import jax.numpy as jnp
from jax import lax
from jax.experimental import pallas as pl
from jax.experimental.pallas import tpu as pltpu
from jax.sharding import PartitionSpec as P

TERMS = 1
MESH = pl.DeviceIdType.MESH


def from_behind(block, axis, distance):
    devices = range(lax.axis_size(axis))
    route = [((i - distance) % len(devices), i) for i in devices]
    return lax.ppermute(block, axis, route)


def gather_kernel(n, groups, shift, pieces, with_roles, *refs):
    if with_roles:
        x_ref, roles_ref, out_ref, roles_out, send_sem, recv_sem, own_sem, sub_sem = refs
    else:
        x_ref, out_ref, send_sem, recv_sem, own_sem, sub_sem = refs
    me = lax.axis_index("node")
    group = lax.axis_index("sub")
    right = lax.rem(me + 1, n)
    left = lax.rem(me + n - 1, n)
    barrier = pltpu.get_barrier_semaphore()
    peers = [(group, left), (group, right)]
    if shift:
        peers += [(lax.rem(group + shift + groups, groups), me), (lax.rem(group - shift + groups, groups), me)]
    for peer in peers:
        pl.semaphore_signal(barrier, inc=1, device_id=peer, device_id_type=MESH)
    pl.semaphore_wait(barrier, len(peers))
    if shift:
        own = pltpu.make_async_copy(x_ref.at[0], out_ref.at[me, 0], own_sem)
        own.start()
        across = pltpu.make_async_remote_copy(
            src_ref=x_ref.at[1],
            dst_ref=out_ref.at[me, 1],
            send_sem=sub_sem.at[0],
            recv_sem=sub_sem.at[1],
            device_id=peers[2],
            device_id_type=MESH,
        )
        across.start()
        roles_across = [
            pltpu.make_async_remote_copy(
                src_ref=roles_ref,
                dst_ref=roles_out.at[side],
                send_sem=sub_sem.at[2 + 2 * side],
                recv_sem=sub_sem.at[3 + 2 * side],
                device_id=peers[2 + side],
                device_id_type=MESH,
            )
            for side in range(2 if with_roles else 0)
        ]
        for copy in roles_across:
            copy.start()
    else:
        own = pltpu.make_async_copy(x_ref, out_ref.at[me], own_sem)
        own.start()
    ways = ((0, 1, right, n // 2), (1, -1, left, n - 1 - n // 2))
    rows = x_ref.shape[-2] // pieces
    slots = (0, 1) if shift else (None,)
    middle = (slice(None),) * (len(x_ref.shape) - 2 - (1 if shift else 0))
    parts = [(slot, chunk) for slot in slots for chunk in range(pieces)]

    def hop(way, target, step, origin, index):
        slot, chunk = parts[index]
        part = ((slot,) if shift else ()) + middle + (pl.ds(chunk * rows, rows), slice(None))
        if step == 0:
            source = out_ref.at[me] if slot == 1 else x_ref
        else:
            source = out_ref.at[origin]
        return pltpu.make_async_remote_copy(
            src_ref=source.at[part],
            dst_ref=out_ref.at[origin].at[part],
            send_sem=send_sem.at[way, step, index],
            recv_sem=recv_sem.at[way, step, index],
            device_id=(group, target),
            device_id_type=MESH,
        )

    sent = []
    for slot in slots:
        if slot == 1:
            across.wait_recv()
        for way, sign, target, steps in ways:
            for index in range(len(parts)):
                if parts[index][0] == slot:
                    copy = hop(way, target, 0, me, index)
                    copy.start()
                    sent.append(copy)
    for step in range(1, n // 2):
        for way, sign, target, steps in ways:
            if step >= steps:
                continue
            origin = lax.rem(me - sign * step + 2 * n, n)
            for index in range(len(parts)):
                hop(way, target, step - 1, origin, index).wait_recv()
                copy = hop(way, target, step, origin, index)
                copy.start()
                sent.append(copy)
    for way, sign, target, steps in ways:
        origin = lax.rem(me - sign * steps + 2 * n, n)
        for index in range(len(parts)):
            hop(way, target, steps - 1, origin, index).wait_recv()
    for copy in sent:
        copy.wait_send()
    own.wait()
    if shift:
        across.wait_send()
        for copy in roles_across:
            copy.wait_send()
            copy.wait_recv()


def node_gather(block, collective_id, shift=0, roles=None, pieces=4):
    n = lax.axis_size("node")
    groups = lax.axis_size("sub")
    vmem = pl.BlockSpec(memory_space=pltpu.VMEM)
    gathered = jax.ShapeDtypeStruct((n,) + block.shape, block.dtype)
    operands = (block,) if roles is None else (block, roles)
    return pl.pallas_call(
        functools.partial(gather_kernel, n, groups, shift, pieces, roles is not None),
        out_shape=gathered if roles is None else (gathered, jax.ShapeDtypeStruct((2,) + roles.shape, roles.dtype)),
        in_specs=[vmem] * len(operands),
        out_specs=vmem if roles is None else (vmem, vmem),
        scratch_shapes=[
            pltpu.SemaphoreType.DMA((2, n // 2, pieces * (2 if shift else 1))),
            pltpu.SemaphoreType.DMA((2, n // 2, pieces * (2 if shift else 1))),
            pltpu.SemaphoreType.DMA,
            pltpu.SemaphoreType.DMA((6,)),
        ],
        compiler_params=pltpu.CompilerParams(collective_id=collective_id, has_side_effects=True),
    )(*operands)


def node_up(tensor_here, left_env, right_env):
    first = jnp.einsum(
        "xa,abp->xbp", left_env, tensor_here, preferred_element_type=jnp.float32
    ).astype(jnp.bfloat16)
    second = jnp.einsum("yb,xbp->xyp", right_env, first, preferred_element_type=jnp.float32).astype(
        jnp.bfloat16
    )
    return jnp.einsum(
        "xyq,xyp->qp", tensor_here, second, preferred_element_type=jnp.float32
    ).astype(jnp.bfloat16)


def node_down(tensor_here, left_env, right_env, upper_here):
    weighted = jnp.einsum(
        "qp,abp->abq", upper_here, tensor_here, preferred_element_type=jnp.float32
    ).astype(jnp.bfloat16)
    right_part = jnp.einsum(
        "xyq,yb->xbq", tensor_here, right_env, preferred_element_type=jnp.float32
    ).astype(jnp.bfloat16)
    left_part = jnp.einsum(
        "xyq,xa->ayq", tensor_here, left_env, preferred_element_type=jnp.float32
    ).astype(jnp.bfloat16)
    first_child = jnp.einsum(
        "xbq,abq->xa", right_part, weighted, preferred_element_type=jnp.float32
    ).astype(jnp.bfloat16)
    second_child = jnp.einsum(
        "ayq,abq->yb", left_part, weighted, preferred_element_type=jnp.float32
    ).astype(jnp.bfloat16)
    return (first_child, second_child)


def placements(group_roles):
    group_size = group_roles.shape[0]
    spots = jnp.arange(group_size, dtype=jnp.int32)
    return jnp.sum(jnp.where(group_roles[None, :] == spots[:, None], spots[None, :], 0), axis=1)


def pick(table, hit):
    hit = hit.reshape(hit.shape + (1,) * (table.ndim - 1))
    return jnp.sum(jnp.where(hit, table.astype(jnp.float32), 0.0), axis=0).astype(table.dtype)


def local(node_tensor, outer_env, upper_env, role_map, child_slots):
    tensor_here = node_tensor[0, 0]
    outer_envs = outer_env[0, 0]
    upper_envs = upper_env[0, 0]
    group_roles = role_map[0]
    child_links = child_slots[0]
    group_size = lax.axis_size("node")
    top_count = group_size // 4
    mid_count = 2 * top_count
    bond_size = tensor_here.shape[0]
    role_spot = placements(group_roles)
    position = lax.axis_index("node")
    my_role = group_roles[position]
    is_top = my_role < top_count
    is_mid = jnp.logical_and(my_role >= top_count, my_role < top_count + mid_count)
    is_leaf = my_role >= top_count + mid_count
    zero_envs = jnp.zeros((TERMS, bond_size, bond_size), jnp.bfloat16)

    def leaf_work():
        return jnp.stack([node_up(tensor_here, outer_envs[0, 0], outer_envs[1, 0])])

    leaf_up = lax.cond(is_leaf, leaf_work, lambda: zero_envs)
    every_leaf = node_gather(leaf_up, 0, pieces=2)
    mid_index = jnp.clip(my_role - top_count, 0, mid_count - 1)

    def mid_work():
        child_envs = []
        for branch in range(2):
            slot_link = child_links[2 * mid_index + branch]
            leaf_pick = pick(every_leaf, group_roles == top_count + mid_count + jnp.maximum(slot_link, 0))
            child_envs.append(jnp.where(slot_link >= 0, leaf_pick, outer_envs[branch]))
        return jnp.stack([node_up(tensor_here, child_envs[0][0], child_envs[1][0])])

    mid_up = lax.cond(is_mid, mid_work, lambda: zero_envs)
    every_mid, near_roles = node_gather(jnp.stack([mid_up, mid_up]), 1, -1, role_map, pieces=1)
    next_roles = near_roles[0]
    prev_roles = near_roles[1]
    top_index = jnp.clip(my_role, 0, top_count - 1)
    left_envs = pick(every_mid[:, 0], group_roles == top_count + top_index)
    right_envs = pick(every_mid[:, 1], next_roles[0] == top_count + top_count + top_index)

    def top_work():
        results = [node_down(tensor_here, left_envs[t], right_envs[t], upper_envs[t]) for t in range(TERMS)]
        return jnp.stack([jnp.stack([r[0] for r in results]), jnp.stack([r[1] for r in results])])

    top_down = lax.cond(
        is_top, top_work, lambda: jnp.zeros((2, TERMS, bond_size, bond_size), jnp.bfloat16)
    )
    every_top = node_gather(top_down, 2, 1, pieces=1)
    own_field = pick(every_top[:, 0], group_roles == jnp.clip(mid_index, 0, top_count - 1))
    other_field = pick(every_top[:, 1], prev_roles[0] == jnp.clip(mid_index - top_count, 0, top_count - 1))
    mid_field = jnp.where(mid_index < top_count, own_field, other_field)
    result = jnp.where(is_mid, mid_field, jnp.where(is_leaf, leaf_up, zero_envs))
    return result[None, None]


def solution(mesh):
    return jax.shard_map(
        local,
        mesh=mesh,
        in_specs=(
            P("sub", "node", None, None, None),
            P("sub", "node", None, None, None, None),
            P("sub", "node", None, None, None),
            P("sub", None),
            P("sub", None),
        ),
        out_specs=P("sub", "node", None, None, None),
        check_vma=False,
    )
```

```python
import functools

import jax
import jax.numpy as jnp
from jax import lax
from jax.experimental import pallas as pl
from jax.experimental.pallas import tpu as pltpu
from jax.sharding import PartitionSpec as P

TERMS = 1
MESH = pl.DeviceIdType.MESH


def from_behind(block, axis, distance):
    devices = range(lax.axis_size(axis))
    route = [((i - distance) % len(devices), i) for i in devices]
    return lax.ppermute(block, axis, route)


def gather_kernel(n, groups, shift, pieces, with_roles, *refs):
    if with_roles:
        x_ref, roles_ref, out_ref, roles_out, send_sem, recv_sem, own_sem, sub_sem = refs
    else:
        x_ref, out_ref, send_sem, recv_sem, own_sem, sub_sem = refs
    me = lax.axis_index("node")
    group = lax.axis_index("sub")
    right = lax.rem(me + 1, n)
    left = lax.rem(me + n - 1, n)
    barrier = pltpu.get_barrier_semaphore()
    peers = [(group, left), (group, right)]
    if shift:
        peers += [(lax.rem(group + shift + groups, groups), me), (lax.rem(group - shift + groups, groups), me)]
    for peer in peers:
        pl.semaphore_signal(barrier, inc=1, device_id=peer, device_id_type=MESH)
    pl.semaphore_wait(barrier, len(peers))
    if shift:
        own = pltpu.make_async_copy(x_ref.at[0], out_ref.at[me, 0], own_sem)
        own.start()
        across = pltpu.make_async_remote_copy(
            src_ref=x_ref.at[1],
            dst_ref=out_ref.at[me, 1],
            send_sem=sub_sem.at[0],
            recv_sem=sub_sem.at[1],
            device_id=peers[2],
            device_id_type=MESH,
        )
        across.start()
        roles_across = [
            pltpu.make_async_remote_copy(
                src_ref=roles_ref,
                dst_ref=roles_out.at[side],
                send_sem=sub_sem.at[2 + 2 * side],
                recv_sem=sub_sem.at[3 + 2 * side],
                device_id=peers[2 + side],
                device_id_type=MESH,
            )
            for side in range(2 if with_roles else 0)
        ]
        for copy in roles_across:
            copy.start()
    else:
        own = pltpu.make_async_copy(x_ref, out_ref.at[me], own_sem)
        own.start()
    ways = ((0, 1, right, n // 2), (1, -1, left, n - 1 - n // 2))
    rows = x_ref.shape[-2] // pieces
    slots = (0, 1) if shift else (None,)
    middle = (slice(None),) * (len(x_ref.shape) - 2 - (1 if shift else 0))
    parts = [(slot, chunk) for slot in slots for chunk in range(pieces)]

    def hop(way, target, step, origin, index):
        slot, chunk = parts[index]
        part = ((slot,) if shift else ()) + middle + (pl.ds(chunk * rows, rows), slice(None))
        if step == 0:
            source = out_ref.at[me] if slot == 1 else x_ref
        else:
            source = out_ref.at[origin]
        return pltpu.make_async_remote_copy(
            src_ref=source.at[part],
            dst_ref=out_ref.at[origin].at[part],
            send_sem=send_sem.at[way, step, index],
            recv_sem=recv_sem.at[way, step, index],
            device_id=(group, target),
            device_id_type=MESH,
        )

    sent = []
    for slot in slots:
        if slot == 1:
            across.wait_recv()
        for way, sign, target, steps in ways:
            for index in range(len(parts)):
                if parts[index][0] == slot:
                    copy = hop(way, target, 0, me, index)
                    copy.start()
                    sent.append(copy)
    for step in range(1, n // 2):
        for way, sign, target, steps in ways:
            if step >= steps:
                continue
            origin = lax.rem(me - sign * step + 2 * n, n)
            for index in range(len(parts)):
                hop(way, target, step - 1, origin, index).wait_recv()
                copy = hop(way, target, step, origin, index)
                copy.start()
                sent.append(copy)
    for way, sign, target, steps in ways:
        origin = lax.rem(me - sign * steps + 2 * n, n)
        for index in range(len(parts)):
            hop(way, target, steps - 1, origin, index).wait_recv()
    for copy in sent:
        copy.wait_send()
    own.wait()
    if shift:
        across.wait_send()
        for copy in roles_across:
            copy.wait_send()
            copy.wait_recv()


def node_gather(block, collective_id, shift=0, roles=None, pieces=4):
    n = lax.axis_size("node")
    groups = lax.axis_size("sub")
    vmem = pl.BlockSpec(memory_space=pltpu.VMEM)
    gathered = jax.ShapeDtypeStruct((n,) + block.shape, block.dtype)
    operands = (block,) if roles is None else (block, roles)
    return pl.pallas_call(
        functools.partial(gather_kernel, n, groups, shift, pieces, roles is not None),
        out_shape=gathered if roles is None else (gathered, jax.ShapeDtypeStruct((2,) + roles.shape, roles.dtype)),
        in_specs=[vmem] * len(operands),
        out_specs=vmem if roles is None else (vmem, vmem),
        scratch_shapes=[
            pltpu.SemaphoreType.DMA((2, n // 2, pieces * (2 if shift else 1))),
            pltpu.SemaphoreType.DMA((2, n // 2, pieces * (2 if shift else 1))),
            pltpu.SemaphoreType.DMA,
            pltpu.SemaphoreType.DMA((6,)),
        ],
        compiler_params=pltpu.CompilerParams(collective_id=collective_id, has_side_effects=True),
    )(*operands)


def node_up(tensor_here, left_env, right_env):
    first = jnp.einsum(
        "xa,abp->xbp", left_env, tensor_here, preferred_element_type=jnp.float32
    ).astype(jnp.bfloat16)
    second = jnp.einsum("yb,xbp->xyp", right_env, first, preferred_element_type=jnp.float32).astype(
        jnp.bfloat16
    )
    return jnp.einsum(
        "xyq,xyp->qp", tensor_here, second, preferred_element_type=jnp.float32
    ).astype(jnp.bfloat16)


def node_down(tensor_here, left_env, right_env, upper_here):
    weighted = jnp.einsum(
        "qp,abp->abq", upper_here, tensor_here, preferred_element_type=jnp.float32
    ).astype(jnp.bfloat16)
    right_part = jnp.einsum(
        "xyq,yb->xbq", tensor_here, right_env, preferred_element_type=jnp.float32
    ).astype(jnp.bfloat16)
    left_part = jnp.einsum(
        "xyq,xa->ayq", tensor_here, left_env, preferred_element_type=jnp.float32
    ).astype(jnp.bfloat16)
    first_child = jnp.einsum(
        "xbq,abq->xa", right_part, weighted, preferred_element_type=jnp.float32
    ).astype(jnp.bfloat16)
    second_child = jnp.einsum(
        "ayq,abq->yb", left_part, weighted, preferred_element_type=jnp.float32
    ).astype(jnp.bfloat16)
    return (first_child, second_child)


def placements(group_roles):
    group_size = group_roles.shape[0]
    spots = jnp.arange(group_size, dtype=jnp.int32)
    return jnp.sum(jnp.where(group_roles[None, :] == spots[:, None], spots[None, :], 0), axis=1)


def pick(table, hit):
    hit = hit.reshape(hit.shape + (1,) * (table.ndim - 1))
    return jnp.sum(jnp.where(hit, table.astype(jnp.float32), 0.0), axis=0).astype(table.dtype)


def local(node_tensor, outer_env, upper_env, role_map, child_slots):
    tensor_here = node_tensor[0, 0]
    outer_envs = outer_env[0, 0]
    upper_envs = upper_env[0, 0]
    group_roles = role_map[0]
    child_links = child_slots[0]
    group_size = lax.axis_size("node")
    top_count = group_size // 4
    mid_count = 2 * top_count
    bond_size = tensor_here.shape[0]
    role_spot = placements(group_roles)
    position = lax.axis_index("node")
    my_role = group_roles[position]
    is_top = my_role < top_count
    is_mid = jnp.logical_and(my_role >= top_count, my_role < top_count + mid_count)
    is_leaf = my_role >= top_count + mid_count
    zero_envs = jnp.zeros((TERMS, bond_size, bond_size), jnp.bfloat16)

    def leaf_work():
        return jnp.stack([node_up(tensor_here, outer_envs[0, 0], outer_envs[1, 0])])

    leaf_up = lax.cond(is_leaf, leaf_work, lambda: zero_envs)
    every_leaf = node_gather(leaf_up, 0, pieces=1)
    mid_index = jnp.clip(my_role - top_count, 0, mid_count - 1)

    def mid_work():
        child_envs = []
        for branch in range(2):
            slot_link = child_links[2 * mid_index + branch]
            leaf_pick = pick(every_leaf, group_roles == top_count + mid_count + jnp.maximum(slot_link, 0))
            child_envs.append(jnp.where(slot_link >= 0, leaf_pick, outer_envs[branch]))
        return jnp.stack([node_up(tensor_here, child_envs[0][0], child_envs[1][0])])

    mid_up = lax.cond(is_mid, mid_work, lambda: zero_envs)
    every_mid, near_roles = node_gather(jnp.stack([mid_up, mid_up]), 1, -1, role_map, pieces=2)
    next_roles = near_roles[0]
    prev_roles = near_roles[1]
    top_index = jnp.clip(my_role, 0, top_count - 1)
    left_envs = pick(every_mid[:, 0], group_roles == top_count + top_index)
    right_envs = pick(every_mid[:, 1], next_roles[0] == top_count + top_count + top_index)

    def top_work():
        results = [node_down(tensor_here, left_envs[t], right_envs[t], upper_envs[t]) for t in range(TERMS)]
        return jnp.stack([jnp.stack([r[0] for r in results]), jnp.stack([r[1] for r in results])])

    top_down = lax.cond(
        is_top, top_work, lambda: jnp.zeros((2, TERMS, bond_size, bond_size), jnp.bfloat16)
    )
    every_top = node_gather(top_down, 2, 1, pieces=2)
    own_field = pick(every_top[:, 0], group_roles == jnp.clip(mid_index, 0, top_count - 1))
    other_field = pick(every_top[:, 1], prev_roles[0] == jnp.clip(mid_index - top_count, 0, top_count - 1))
    mid_field = jnp.where(mid_index < top_count, own_field, other_field)
    result = jnp.where(is_mid, mid_field, jnp.where(is_leaf, leaf_up, zero_envs))
    return result[None, None]


def solution(mesh):
    return jax.shard_map(
        local,
        mesh=mesh,
        in_specs=(
            P("sub", "node", None, None, None),
            P("sub", "node", None, None, None, None),
            P("sub", "node", None, None, None),
            P("sub", None),
            P("sub", None),
        ),
        out_specs=P("sub", "node", None, None, None),
        check_vma=False,
    )
```

```python
import functools

import jax
import jax.numpy as jnp
from jax import lax
from jax.experimental import pallas as pl
from jax.experimental.pallas import tpu as pltpu
from jax.sharding import PartitionSpec as P

TERMS = 1
MESH = pl.DeviceIdType.MESH


def from_behind(block, axis, distance):
    devices = range(lax.axis_size(axis))
    route = [((i - distance) % len(devices), i) for i in devices]
    return lax.ppermute(block, axis, route)


def gather_kernel(n, groups, shift, pieces, with_roles, *refs):
    if with_roles:
        x_ref, roles_ref, out_ref, roles_out, send_sem, recv_sem, own_sem, sub_sem = refs
    else:
        x_ref, out_ref, send_sem, recv_sem, own_sem, sub_sem = refs
    me = lax.axis_index("node")
    group = lax.axis_index("sub")
    right = lax.rem(me + 1, n)
    left = lax.rem(me + n - 1, n)
    barrier = pltpu.get_barrier_semaphore()
    peers = [(group, left), (group, right)]
    if shift:
        peers += [(lax.rem(group + shift + groups, groups), me), (lax.rem(group - shift + groups, groups), me)]
    for peer in peers:
        pl.semaphore_signal(barrier, inc=1, device_id=peer, device_id_type=MESH)
    pl.semaphore_wait(barrier, len(peers))
    if shift:
        own = pltpu.make_async_copy(x_ref.at[0], out_ref.at[me, 0], own_sem)
        own.start()
        across = pltpu.make_async_remote_copy(
            src_ref=x_ref.at[1],
            dst_ref=out_ref.at[me, 1],
            send_sem=sub_sem.at[0],
            recv_sem=sub_sem.at[1],
            device_id=peers[2],
            device_id_type=MESH,
        )
        across.start()
        roles_across = [
            pltpu.make_async_remote_copy(
                src_ref=roles_ref,
                dst_ref=roles_out.at[side],
                send_sem=sub_sem.at[2 + 2 * side],
                recv_sem=sub_sem.at[3 + 2 * side],
                device_id=peers[2 + side],
                device_id_type=MESH,
            )
            for side in range(2 if with_roles else 0)
        ]
        for copy in roles_across:
            copy.start()
    else:
        own = pltpu.make_async_copy(x_ref, out_ref.at[me], own_sem)
        own.start()
    ways = ((0, 1, right, n // 2), (1, -1, left, n - 1 - n // 2))
    rows = x_ref.shape[-2] // pieces
    slots = (0, 1) if shift else (None,)
    middle = (slice(None),) * (len(x_ref.shape) - 2 - (1 if shift else 0))
    parts = [(slot, chunk) for slot in slots for chunk in range(pieces)]

    def hop(way, target, step, origin, index):
        slot, chunk = parts[index]
        part = ((slot,) if shift else ()) + middle + (pl.ds(chunk * rows, rows), slice(None))
        if step == 0:
            source = out_ref.at[me] if slot == 1 else x_ref
        else:
            source = out_ref.at[origin]
        return pltpu.make_async_remote_copy(
            src_ref=source.at[part],
            dst_ref=out_ref.at[origin].at[part],
            send_sem=send_sem.at[way, step, index],
            recv_sem=recv_sem.at[way, step, index],
            device_id=(group, target),
            device_id_type=MESH,
        )

    sent = []
    for slot in slots:
        if slot == 1:
            across.wait_recv()
        for way, sign, target, steps in ways:
            for index in range(len(parts)):
                if parts[index][0] == slot:
                    copy = hop(way, target, 0, me, index)
                    copy.start()
                    sent.append(copy)
    for step in range(1, n // 2):
        for way, sign, target, steps in ways:
            if step >= steps:
                continue
            origin = lax.rem(me - sign * step + 2 * n, n)
            for index in range(len(parts)):
                hop(way, target, step - 1, origin, index).wait_recv()
                copy = hop(way, target, step, origin, index)
                copy.start()
                sent.append(copy)
    for way, sign, target, steps in ways:
        origin = lax.rem(me - sign * steps + 2 * n, n)
        for index in range(len(parts)):
            hop(way, target, steps - 1, origin, index).wait_recv()
    for copy in sent:
        copy.wait_send()
    own.wait()
    if shift:
        across.wait_send()
        for copy in roles_across:
            copy.wait_send()
            copy.wait_recv()


def node_gather(block, collective_id, shift=0, roles=None, pieces=4):
    n = lax.axis_size("node")
    groups = lax.axis_size("sub")
    vmem = pl.BlockSpec(memory_space=pltpu.VMEM)
    gathered = jax.ShapeDtypeStruct((n,) + block.shape, block.dtype)
    operands = (block,) if roles is None else (block, roles)
    return pl.pallas_call(
        functools.partial(gather_kernel, n, groups, shift, pieces, roles is not None),
        out_shape=gathered if roles is None else (gathered, jax.ShapeDtypeStruct((2,) + roles.shape, roles.dtype)),
        in_specs=[vmem] * len(operands),
        out_specs=vmem if roles is None else (vmem, vmem),
        scratch_shapes=[
            pltpu.SemaphoreType.DMA((2, n // 2, pieces * (2 if shift else 1))),
            pltpu.SemaphoreType.DMA((2, n // 2, pieces * (2 if shift else 1))),
            pltpu.SemaphoreType.DMA,
            pltpu.SemaphoreType.DMA((6,)),
        ],
        compiler_params=pltpu.CompilerParams(collective_id=collective_id),
    )(*operands)


def node_up(tensor_here, left_env, right_env):
    first = jnp.einsum(
        "xa,abp->xbp", left_env, tensor_here, preferred_element_type=jnp.float32
    ).astype(jnp.bfloat16)
    second = jnp.einsum("yb,xbp->xyp", right_env, first, preferred_element_type=jnp.float32).astype(
        jnp.bfloat16
    )
    return jnp.einsum(
        "xyq,xyp->qp", tensor_here, second, preferred_element_type=jnp.float32
    ).astype(jnp.bfloat16)


def node_down(tensor_here, left_env, right_env, upper_here):
    weighted = jnp.einsum(
        "qp,abp->abq", upper_here, tensor_here, preferred_element_type=jnp.float32
    ).astype(jnp.bfloat16)
    right_part = jnp.einsum(
        "xyq,yb->xbq", tensor_here, right_env, preferred_element_type=jnp.float32
    ).astype(jnp.bfloat16)
    left_part = jnp.einsum(
        "xyq,xa->ayq", tensor_here, left_env, preferred_element_type=jnp.float32
    ).astype(jnp.bfloat16)
    first_child = jnp.einsum(
        "xbq,abq->xa", right_part, weighted, preferred_element_type=jnp.float32
    ).astype(jnp.bfloat16)
    second_child = jnp.einsum(
        "ayq,abq->yb", left_part, weighted, preferred_element_type=jnp.float32
    ).astype(jnp.bfloat16)
    return (first_child, second_child)


def placements(group_roles):
    group_size = group_roles.shape[0]
    spots = jnp.arange(group_size, dtype=jnp.int32)
    return jnp.sum(jnp.where(group_roles[None, :] == spots[:, None], spots[None, :], 0), axis=1)


def pick(table, hit):
    hit = hit.reshape(hit.shape + (1,) * (table.ndim - 1))
    return jnp.sum(jnp.where(hit, table.astype(jnp.float32), 0.0), axis=0).astype(table.dtype)


def local(node_tensor, outer_env, upper_env, role_map, child_slots):
    tensor_here = node_tensor[0, 0]
    outer_envs = outer_env[0, 0]
    upper_envs = upper_env[0, 0]
    group_roles = role_map[0]
    child_links = child_slots[0]
    group_size = lax.axis_size("node")
    top_count = group_size // 4
    mid_count = 2 * top_count
    bond_size = tensor_here.shape[0]
    role_spot = placements(group_roles)
    position = lax.axis_index("node")
    my_role = group_roles[position]
    is_top = my_role < top_count
    is_mid = jnp.logical_and(my_role >= top_count, my_role < top_count + mid_count)
    is_leaf = my_role >= top_count + mid_count
    zero_envs = jnp.zeros((TERMS, bond_size, bond_size), jnp.bfloat16)

    def leaf_work():
        return jnp.stack([node_up(tensor_here, outer_envs[0, 0], outer_envs[1, 0])])

    leaf_up = lax.cond(is_leaf, leaf_work, lambda: zero_envs)
    every_leaf = node_gather(leaf_up, 0, pieces=2)
    mid_index = jnp.clip(my_role - top_count, 0, mid_count - 1)

    def mid_work():
        child_envs = []
        for branch in range(2):
            slot_link = child_links[2 * mid_index + branch]
            leaf_pick = pick(every_leaf, group_roles == top_count + mid_count + jnp.maximum(slot_link, 0))
            child_envs.append(jnp.where(slot_link >= 0, leaf_pick, outer_envs[branch]))
        return jnp.stack([node_up(tensor_here, child_envs[0][0], child_envs[1][0])])

    mid_up = lax.cond(is_mid, mid_work, lambda: zero_envs)
    every_mid, near_roles = node_gather(jnp.stack([mid_up, mid_up]), 1, -1, role_map, pieces=2)
    next_roles = near_roles[0]
    prev_roles = near_roles[1]
    top_index = jnp.clip(my_role, 0, top_count - 1)
    left_envs = pick(every_mid[:, 0], group_roles == top_count + top_index)
    right_envs = pick(every_mid[:, 1], next_roles[0] == top_count + top_count + top_index)

    def top_work():
        results = [node_down(tensor_here, left_envs[t], right_envs[t], upper_envs[t]) for t in range(TERMS)]
        return jnp.stack([jnp.stack([r[0] for r in results]), jnp.stack([r[1] for r in results])])

    top_down = lax.cond(
        is_top, top_work, lambda: jnp.zeros((2, TERMS, bond_size, bond_size), jnp.bfloat16)
    )
    every_top = node_gather(top_down, 2, 1, pieces=2)
    own_field = pick(every_top[:, 0], group_roles == jnp.clip(mid_index, 0, top_count - 1))
    other_field = pick(every_top[:, 1], prev_roles[0] == jnp.clip(mid_index - top_count, 0, top_count - 1))
    mid_field = jnp.where(mid_index < top_count, own_field, other_field)
    result = jnp.where(is_mid, mid_field, jnp.where(is_leaf, leaf_up, zero_envs))
    return result[None, None]


def solution(mesh):
    return jax.shard_map(
        local,
        mesh=mesh,
        in_specs=(
            P("sub", "node", None, None, None),
            P("sub", "node", None, None, None, None),
            P("sub", "node", None, None, None),
            P("sub", None),
            P("sub", None),
        ),
        out_specs=P("sub", "node", None, None, None),
        check_vma=False,
    )
```
